32 devices in a mesh: bucket: 2 (over x), dp: 4 (over z), seq: 4 (over y, core).
Axes of the slice: x: 2, y: 2, z: 4, core: 2. Of those that a mesh axis runs over, the one named last changes fastest.
Arguments:
- patches: bfloat16 [8192, 768], P(('bucket', 'dp', 'seq')), may hold values from -6 to 6
- conditioning: bfloat16 [32, 768], P(('bucket', 'dp')), may hold values from -6 to 6
- image_slot: int32 [8192], P(('bucket', 'dp')), may hold values from 0 to 3, as said below
- routes: int32 [8192, 2], P(('bucket', 'dp', 'seq')), may hold values from 0 to 7, all different within a row; in each aligned block of 256 rows (0 to 255, 256 to 511, ...) at most 96 rows name the same one
- ada_weight: bfloat16 [768, 4608], P('dp'), may hold values from -0.21875 to 0.21875
- ada_bias: bfloat16 [4608], P('dp'), may hold values from -3 to 3
- qkv_weight: bfloat16 [768, 2304], P('dp'), may hold values from -0.21875 to 0.21875
- out_weight: bfloat16 [768, 768], P('dp'), may hold values from -0.875 to 0.875
- router_weight: bfloat16 [768, 8], P('dp'), may hold values from -0.15625 to 0.15625
- shared_in: bfloat16 [768, 3072], P('dp'), may hold values from -0.21875 to 0.21875
- shared_out: bfloat16 [3072, 768], P('dp'), may hold values from -0.109375 to 0.109375
- expert_in: bfloat16 [8, 768, 3072], P('seq'), may hold values from -0.21875 to 0.21875
- expert_out: bfloat16 [8, 3072, 768], P('seq'), may hold values from -0.109375 to 0.109375
- out_grad: bfloat16 [8192, 768], P(('bucket', 'dp', 'seq')), may hold values from -6 to 6
Outputs:
- block_out: bfloat16 [8192, 768], P(('bucket', 'dp', 'seq'))
- patch_grad: float32 [8192, 768], P(('bucket', 'dp', 'seq'))
- cond_grad: float32 [32, 768], P(('bucket', 'dp'), 'seq')
- ada_weight_grad: float32 [768, 4608], P(('bucket', 'dp', 'seq'))
- ada_bias_grad: float32 [4608], P(('bucket', 'dp', 'seq'))
- qkv_grad: float32 [768, 2304], P(('bucket', 'dp', 'seq'))
- out_weight_grad: float32 [768, 768], P(('bucket', 'dp', 'seq'))
- router_grad: float32 [768, 8], P(('bucket', 'dp', 'seq'))
- shared_in_grad: float32 [768, 3072], P(('bucket', 'dp', 'seq'))
- shared_out_grad: float32 [3072, 768], P(('bucket', 'dp', 'seq'))
- expert_in_grad: float32 [8, 768, 3072], P('seq', ('bucket', 'dp'))
- expert_out_grad: float32 [8, 3072, 768], P('seq', ('bucket', 'dp'))
The draws below stay inside these ranges and needn't reach their ends.
Inputs may be any that keep to these rules, and one draw needn't show every extreme that they name: `image_slot`: in each group of 1024 patches, each aligned block of 1024 patches holds either one long image, whose patches all carry slot 4 * (block index), or four short images of 256 patches carrying their own unit index (position // 256); both kinds occur. `routes`: the two experts of a patch differ; among the patches of one device no expert is named more than 96 times.
All inputs are finite; a program needn't handle non-finite values.
Results may differ from the reference program's by a relative error of at most 0.019.
The reference program's roundings to bfloat16 on the way count: a program that leaves them out, or rounds other values in their place, can miss the bound.
Values may be sent and summed in bfloat16 or wider, within the bound.
A program may use at most 320 MiB of HBM per device.

```python
import math
import jax
import jax.numpy as jnp
import numpy as np
from jax import lax

D = 768
FF = 3072
HEADS = 12
HEAD_DIM = 64
EXPERTS = 8
TOK_DEV = 256
SHORT = 256
LONG = 1024
GROUP = 1024
IMGS = 4
IMAGES = 32
TOKENS = 8192
CAP = 96


def draw_image_slot(key, part):
    group_count = TOKENS // GROUP
    block_count = GROUP // LONG
    flags = jax.random.randint(key, (group_count, block_count), 0, 2)
    group_ids = jnp.arange(group_count)[:, None]
    block_ids = jnp.arange(block_count)[None, :]
    flags = jnp.where((group_ids == 0) & (block_ids == 0), 1, flags)
    flags = jnp.where((group_ids == 1) & (block_ids == block_count - 1), 0, flags)
    position = jnp.arange(GROUP)
    block_of = position // LONG
    unit_of = position // SHORT
    long_slot = block_of * (LONG // SHORT)
    slots = jnp.where(flags[:, block_of] == 1, long_slot[None, :], unit_of[None, :])
    return slots.reshape(TOKENS).astype(jnp.int32)


def levels(rng, dims, shards, least, high):
    loudness, own = 1.0, jax.random.fold_in(rng, 6)
    for dim, blocks in shards:
        draws = jnp.exp(jax.random.uniform(jax.random.fold_in(own, dim), (blocks,), jnp.float32, least / len(shards), high / len(shards)))
        loudness = loudness * jnp.repeat(draws, dims[dim] // blocks).reshape([-1 if axis == dim else 1 for axis in range(len(dims))])
    return loudness


def routed_block(stream_key, own, number, rows, number_of, top, limit, skew):
    sequence = jax.random.permutation(stream_key, number_of)
    crowded, common = shares(number_of, rows * top, limit, skew, True), shares(number_of, rows * top, limit, skew, False)
    places = jnp.arange(number_of)

    def named(tallies, rotation):
        used = int((tallies > 0).sum())
        fixed = max(1, used // 4)
        passed = fixed + (places - fixed + rotation * (used - fixed)) % max(1, number_of - fixed)
        return jnp.zeros((number_of,), jnp.int32).at[sequence[jnp.where(places < fixed, places, passed)]].set(jnp.asarray(tallies, jnp.int32))

    tallies = jnp.where(number % 4 == 0, named(crowded, number // 4), named(common, number - number // 4 - 1))
    mixed = jax.random.permutation(jax.random.fold_in(own, 3), number_of)
    donor, sink = mixed[0:number_of // 2 * 2:2], mixed[1:number_of // 2 * 2:2]
    margin = jnp.minimum(tallies[donor] - 1, limit - tallies[sink]) // 2
    margin = jnp.where((donor == sequence[0]) | (sink == sequence[0]) | (tallies[sink] == 0), 0, jnp.maximum(margin, 0))
    passed = jax.random.randint(jax.random.fold_in(own, 4), (number_of // 2,), 0, 1 << 20) % (margin + 1)
    tallies = tallies.at[donor].add(-passed).at[sink].add(passed)
    items = jnp.searchsorted(jnp.cumsum(tallies), jnp.arange(rows * top), side="right").astype(jnp.int32)
    table = items.reshape(top, rows).T
    table = table[jax.random.permutation(jax.random.fold_in(own, 1), rows)]
    rotation = jax.random.randint(jax.random.fold_in(own, 2), (rows, 1), 0, top)
    return jnp.take_along_axis(table, (jnp.arange(top)[None, :] + rotation) % top, axis=1)


def shares(number_of, total, limit, lean, full):
    weights = [(1 << 20) // math.isqrt(standing ** lean) + 1 for standing in range(1, number_of + 1)]
    largest = limit if full else min(limit, max(-(-total // number_of), total * weights[0] // sum(weights)))
    least = 1 if total - largest >= number_of - 1 else 0
    given, spare = [largest] + [least] * (number_of - 1), total - largest - least * (number_of - 1)
    while spare > 0:
        movable = [i for i in range(1, number_of) if given[i] < largest] or [i for i in range(1, number_of) if given[i] < limit]
        mass, remaining = sum([weights[i] for i in movable]), spare
        for i in movable:
            more = min(limit - given[i], max(1, remaining * weights[i] // mass), spare)
            given[i] = given[i] + more
            spare = spare - more
    return np.array(given)


def noise(stream_key, dims, scale, bound, cuts=(), held_as=jnp.bfloat16):
    values = scale * jax.random.normal(stream_key, dims, jnp.float32)
    if cuts:
        values = values * levels(stream_key, dims, cuts, -0.22, 0.18)
    return jnp.clip(values, -bound, bound).astype(held_as)


def setup_inputs(seed: int = 0) -> dict:
    arg_keys = jax.random.split(jax.random.key(seed), 15)
    patches = noise(arg_keys[0], (TOKENS, D), 1.0, 6.0, ((0, 32),))
    conditioning = noise(arg_keys[1], (IMAGES, D), 1.0, 6.0, ((0, 8),))
    image_slot = draw_image_slot(jax.random.fold_in(arg_keys[14], 71), 0)
    routes_keys = jax.random.split(jax.random.fold_in(arg_keys[3], 1), TOKENS // TOK_DEV)
    routes_turns = jax.random.permutation(jax.random.fold_in(arg_keys[3], 3), TOKENS // TOK_DEV)
    routes = jax.vmap(lambda own, number: routed_block(jax.random.fold_in(arg_keys[3], 2), own, number, TOK_DEV, EXPERTS, 2, CAP, 2))(routes_keys, routes_turns).reshape((TOKENS, 2))
    ada_weight = noise(arg_keys[4], (D, 6 * D), D ** -0.5, 0.21875, ((0, 4),))
    ada_bias = noise(arg_keys[5], (6 * D,), 0.5, 3.0, ((0, 4),))
    qkv_weight = noise(arg_keys[6], (D, 3 * D), D ** -0.5, 0.21875, ((0, 4),))
    out_weight = noise(arg_keys[7], (D, D), (D // 16) ** -0.5, 0.875, ((0, 4),))
    router_weight = noise(arg_keys[8], (D, EXPERTS), (2 * D) ** -0.5, 0.15625, ((0, 4),))
    shared_in = noise(arg_keys[9], (D, FF), D ** -0.5, 0.21875, ((0, 4),))
    shared_out = noise(arg_keys[10], (FF, D), FF ** -0.5, 0.109375, ((0, 4),))
    expert_in = noise(arg_keys[11], (EXPERTS, D, FF), D ** -0.5, 0.21875, ((0, 4),))
    expert_out = noise(arg_keys[12], (EXPERTS, FF, D), FF ** -0.5, 0.109375, ((0, 4),))
    out_grad = noise(arg_keys[13], (TOKENS, D), 1.0, 6.0, ((0, 32),))
    return dict(patches=patches, conditioning=conditioning, image_slot=image_slot, routes=routes, ada_weight=ada_weight, ada_bias=ada_bias, qkv_weight=qkv_weight, out_weight=out_weight, router_weight=router_weight, shared_in=shared_in, shared_out=shared_out, expert_in=expert_in, expert_out=expert_out, out_grad=out_grad)


highest = lax.Precision.HIGHEST
norm_eps = 1e-06
gelu_coef = 0.7978845608
cube_coef = 0.044715

@jax.custom_vjp
def low(v):
    return lax.optimization_barrier(v.astype(jnp.bfloat16)).astype(jnp.float32)

@jax.custom_vjp
def low_back(v):
    return v

def low_keep(v):
    return (low(v), None)

def low_pass(kept, grad):
    return (grad,)

def back_keep(v):
    return (v, None)

def back_low(kept, grad):
    return (low(grad),)
low.defvjp(low_keep, low_pass)
low_back.defvjp(back_keep, back_low)

def matmul(left, right):
    return jnp.dot(left, right, precision=highest)

def silu_curve(inputs):
    return inputs / (1.0 + jnp.exp(-inputs))

def gelu_curve(inputs):
    return 0.5 * inputs * (1.0 + jnp.tanh(gelu_coef * (inputs + cube_coef * inputs * inputs * inputs)))

def modulate(rows_in, scale_in, shift_in):
    centred = rows_in - lax.optimization_barrier(jnp.mean(rows_in, axis=-1, keepdims=True))
    normed = centred * lax.rsqrt(lax.optimization_barrier(jnp.mean(centred * centred, axis=-1, keepdims=True)) + norm_eps)
    return normed * (1.0 + scale_in) + shift_in

def slot_table(routes):
    blocks = routes.reshape(TOKENS // TOK_DEV, TOK_DEV * 2)
    expert_ids = jnp.arange(EXPERTS, dtype=jnp.int32)
    hits = (blocks[:, :, None] == expert_ids[None, None, :]).astype(jnp.int32)
    running = jnp.cumsum(hits, axis=1)
    place = lax.optimization_barrier(jnp.sum(running * hits, axis=2)) - 1
    base = (jnp.arange(TOKENS // TOK_DEV, dtype=jnp.int32) * CAP)[:, None]
    return (place + base).reshape(TOKENS, 2).astype(jnp.int32)

def attend_group(qkv_mat, proj_mat, rows_in, slots_in, modul_in):
    image_ids = jnp.arange(IMGS, dtype=jnp.int32)
    onehot = (slots_in[:, None] == image_ids[None, :]).astype(jnp.float32)
    per_row = matmul(onehot, modul_in)
    shift_one, scale_one, gate_one, shift_two, scale_two, gate_two = jnp.split(per_row, 6, axis=1)
    hidden_one = low(modulate(rows_in, scale_one, shift_one))
    project = low(low_back(matmul(hidden_one, qkv_mat)))
    queries = project[:, :D].reshape(GROUP, HEADS, HEAD_DIM)
    keys_all = project[:, D:2 * D].reshape(GROUP, HEADS, HEAD_DIM)
    values_all = project[:, 2 * D:].reshape(GROUP, HEADS, HEAD_DIM)
    scores = low_back(jnp.einsum('qhd,khd->hqk', queries, keys_all, precision=highest) * (1.0 / math.sqrt(HEAD_DIM)))
    same = slots_in[:, None] == slots_in[None, :]
    scores = jnp.where(same[None, :, :], scores, -1e+30)
    row_max = lax.optimization_barrier(jnp.max(scores, axis=-1, keepdims=True))
    exp_scores = jnp.exp(scores - row_max)
    probs = exp_scores / lax.optimization_barrier(jnp.sum(exp_scores, axis=-1, keepdims=True))
    mixed = jnp.einsum('hqk,khd->qhd', low(probs), values_all, precision=highest).reshape(GROUP, D)
    mixed = low_back(low(mixed))
    branch = low_back(matmul(mixed, proj_mat))
    after = rows_in + gate_one * branch
    hidden_two = low(modulate(after, scale_two, shift_two))
    return (after, hidden_two)

def expert_block(padded, weight_in, weight_out, indices):
    taken = low_back(padded[indices])
    inner = low_back(matmul(taken, weight_in))
    active = low(gelu_curve(inner))
    return low_back(low(matmul(active, weight_out)))

def finish_group(router_mat, inner_mat, outer_mat, after, hidden_two, slots_in, modul_in, chosen, picked):
    image_ids = jnp.arange(IMGS, dtype=jnp.int32)
    onehot = (slots_in[:, None] == image_ids[None, :]).astype(jnp.float32)
    gate_two = matmul(onehot, modul_in)[:, 5 * D:]
    inner = low_back(matmul(hidden_two, inner_mat))
    shared = low_back(matmul(low(gelu_curve(inner)), outer_mat))
    logits = low_back(matmul(hidden_two, router_mat))
    pair = jnp.take_along_axis(logits, chosen, axis=1)
    pair_max = lax.optimization_barrier(jnp.max(pair, axis=1, keepdims=True))
    pair_exp = jnp.exp(pair - pair_max)
    gates = pair_exp / lax.optimization_barrier(jnp.sum(pair_exp, axis=1, keepdims=True))
    mixture = shared + gates[:, 0:1] * picked[:, 0] + gates[:, 1:2] * picked[:, 1]
    return after + gate_two * mixture

def reference(patches, conditioning, image_slot, routes, ada_weight, ada_bias, qkv_weight, out_weight, router_weight, shared_in, shared_out, expert_in, expert_out, out_grad):
    groups = TOKENS // GROUP
    slot_groups = image_slot.reshape(groups, GROUP)
    route_groups = routes.reshape(groups, GROUP, 2)
    place = slot_table(routes)
    flat_experts = routes.reshape(-1)
    flat_place = place.reshape(-1)
    owners = jnp.repeat(jnp.arange(TOKENS, dtype=jnp.int32), 2)
    indices = jnp.full((EXPERTS, TOKENS // TOK_DEV * CAP), TOKENS, dtype=jnp.int32)
    indices = indices.at[flat_experts, flat_place].set(owners)
    weights = tuple((item.astype(jnp.float32) for item in (ada_weight, ada_bias, qkv_weight, out_weight, router_weight, shared_in, shared_out, expert_in, expert_out)))

    def forward(weights, rows, cond):
        ada_mat, ada_vec, qkv_mat, proj_mat, router_mat, inner_mat, outer_mat, exp_in_mat, exp_out_mat = weights
        modul = matmul(low(silu_curve(cond)), ada_mat) + ada_vec
        modul_groups = modul.reshape(groups, IMGS, 6 * D)
        row_groups = rows.reshape(groups, GROUP, D)
        attend_ckpt = jax.checkpoint(attend_group)

        def attend_step(carry, items):
            return (carry, attend_ckpt(qkv_mat, proj_mat, items[0], items[1], items[2]))
        carry_zero = jnp.zeros((), jnp.float32)
        carry_one, outputs = lax.scan(attend_step, carry_zero, (row_groups, slot_groups, modul_groups))
        after, hidden_two = outputs
        padded = jnp.concatenate([hidden_two.reshape(TOKENS, D), jnp.zeros((1, D), jnp.float32)], axis=0)

        def expert_step(items):
            return expert_block(padded, items[0], items[1], items[2])
        expert_vals = lax.map(jax.checkpoint(expert_step), (exp_in_mat, exp_out_mat, indices))
        picked = expert_vals[flat_experts, flat_place].reshape(groups, GROUP, 2, D)
        finish_ckpt = jax.checkpoint(finish_group)

        def finish_step(carry, items):
            return (carry, finish_ckpt(router_mat, inner_mat, outer_mat, items[0], items[1], items[2], items[3], items[4], items[5]))
        carry_two, block = lax.scan(finish_step, carry_zero, (after, hidden_two, slot_groups, modul_groups, route_groups, picked))
        return block.reshape(TOKENS, D)
    block, pullback = jax.vjp(forward, weights, patches.astype(jnp.float32), conditioning.astype(jnp.float32))
    weight_grads, patch_grad, cond_grad = pullback(out_grad.astype(jnp.float32))
    return (block.astype(jnp.bfloat16), patch_grad, cond_grad, weight_grads[0], weight_grads[1], weight_grads[2], weight_grads[3], weight_grads[4], weight_grads[5], weight_grads[6], weight_grads[7], weight_grads[8])
```

```python
import functools
import math

import jax
import jax.numpy as jnp
from jax import lax
from jax.experimental import pallas as pl
from jax.experimental.pallas import tpu as pltpu
from jax.sharding import PartitionSpec as P

HEADS = 12


highest = lax.Precision.HIGHEST
norm_eps = 1e-06
gelu_coef = 0.7978845608
cube_coef = 0.044715


def sigmoid_curve(inputs):
    return 1.0 / (1.0 + jnp.exp(-inputs))


def silu_curve(inputs):
    return inputs / (1.0 + jnp.exp(-inputs))


def silu_slope(inputs):
    sigma = sigmoid_curve(inputs)
    return sigma * (1.0 + inputs * (1.0 - sigma))


def gelu_curve(inputs):
    return (
        0.5 * inputs * (1.0 + jnp.tanh(gelu_coef * (inputs + cube_coef * inputs * inputs * inputs)))
    )


def gelu_slope(inputs):
    bent = jnp.tanh(gelu_coef * (inputs + cube_coef * inputs * inputs * inputs))
    return 0.5 * (1.0 + bent) + 0.5 * inputs * (1.0 - bent * bent) * gelu_coef * (
        1.0 + 3.0 * cube_coef * inputs * inputs
    )


def modulate(rows_in, scale_in, shift_in):
    centred = rows_in - jnp.mean(rows_in, axis=-1, keepdims=True)
    normed = centred * lax.rsqrt(jnp.mean(centred * centred, axis=-1, keepdims=True) + norm_eps)
    return normed * (1.0 + scale_in) + shift_in


def matmul_low(left, right):
    return jnp.dot(left, right, preferred_element_type=jnp.float32)


def matmul_left_t(left, right):
    return lax.dot_general(
        left, right, (((0,), (0,)), ((), ())), preferred_element_type=jnp.float32
    )


def matmul_right_t(left, right):
    return lax.dot_general(
        left, right, (((1,), (1,)), ((), ())), preferred_element_type=jnp.float32
    )


def order_rows(term, outer_count, inner_count):
    rows = term.shape[0]
    rest = term.shape[1:]
    blocks = term.reshape((outer_count, inner_count, rows // (outer_count * inner_count)) + rest)
    return jnp.swapaxes(blocks, 0, 1).reshape((rows,) + rest)

MESH = pl.DeviceIdType.MESH


def hand_over(src, dst, sems, index, where):
    return pltpu.make_async_remote_copy(
        src_ref=src,
        dst_ref=dst,
        send_sem=sems[0].at[index],
        recv_sem=sems[1].at[index],
        device_id=where,
        device_id_type=MESH,
    )


def greet(partners):
    barrier = pltpu.get_barrier_semaphore()
    for where in partners:
        pl.semaphore_signal(barrier, inc=1, device_id=where, device_id_type=MESH)
    pl.semaphore_wait(barrier, len(partners))


def own_place():
    bucket, dp, seq = (lax.axis_index(name) for name in ("bucket", "dp", "seq"))
    far = lax.rem(seq + 2, 4)
    twin = seq + 1 - 2 * lax.rem(seq, 2)
    return bucket, dp, seq, far, twin


class Spread:
    def __init__(self, ins, outs, whole, sems, own_sem):
        self.ins, self.outs, self.whole = ins, outs, whole
        self.sems, self.own_sem = sems, own_sem
        self.bucket, self.dp, self.seq, self.far, twin = own_place()
        self.to_bucket, self.to_far, self.to_twin = (
            {"bucket": 1 - self.bucket},
            {"seq": self.far},
            {"seq": twin},
        )
        self.to_dp = [None] + [{"dp": lax.rem(self.dp + k, 4)} for k in (1, 2, 3)]
        self.partners = [self.to_bucket, self.to_far, self.to_twin] + self.to_dp[1:]
        self.arrays = range(len(ins))

    def place(self, a, j, own_bucket, own_far, half=None):
        rows = self.ins[a].shape[0] // (8 if self.whole[a] else 1)
        slot = (
            lax.rem(self.dp + 4 - j, 4) * 8
            + (self.bucket if own_bucket else 1 - self.bucket) * 4
            + (self.seq if own_far else self.far)
        )
        cut = self.outs[a].at[pl.ds(pl.multiple_of(slot * rows, 8), rows)]
        if half is None:
            return cut
        columns = self.outs[a].shape[1]
        mid = columns // 256 * 128
        return cut.at[:, pl.ds(0, mid)] if half == 0 else cut.at[:, pl.ds(mid, columns - mid)]

    def own(self, a):
        if not self.whole[a]:
            return self.ins[a]
        rows = self.ins[a].shape[0] // 8
        at = pl.multiple_of((self.bucket * 4 + self.seq) * rows, 8)
        return self.ins[a].at[pl.ds(at, rows)]

    def copy(self, a, kind, j):
        if kind == "dp":
            return hand_over(
                self.own(a), self.place(a, 0, True, True), self.sems, (a, j - 1), self.to_dp[j]
            )
        first, where, view = {
            "bucket": (3, self.to_bucket, (True, True)),
            "far": (7, self.to_far, (True, True)),
            "twin": (11, self.to_twin, (True, True)),
            "corner_far": (15, self.to_far, (False, True, 0)),
            "corner_bucket": (19, self.to_bucket, (True, False, 1)),
            "twin_bucket": (23, self.to_twin, (False, True)),
            "twin_far": (27, self.to_twin, (True, False)),
            "twin_corner0": (31, self.to_twin, (False, False, 0)),
            "twin_corner1": (35, self.to_twin, (False, False, 1)),
        }[kind]
        dst = self.place(a, j, *view)
        src = self.own(a) if first <= 11 and j == 0 else dst
        return hand_over(src, dst, self.sems, (a, first + j), where)

    def keep(self, a):
        return pltpu.make_async_copy(
            self.own(a), self.place(a, 0, True, True), self.own_sem.at[a]
        )

    def start(self):
        for a in self.arrays:
            for kind in ("bucket", "far"):
                self.copy(a, kind, 0).start()
            for j in (1, 3, 2):
                self.copy(a, "dp", j).start()
            self.copy(a, "twin", 0).start()
            self.keep(a).start()

    def relay(self, step):
        if step < 4:
            for a in self.arrays:
                self.copy(a, "dp", step).wait_recv()
                for kind in ("bucket", "far", "twin"):
                    self.copy(a, kind, step).start()
        j = {1: 0, 3: 1, 2: 3, 4: 2}[step]
        for a in self.arrays:
            self.copy(a, "bucket", j).wait_recv()
            self.copy(a, "corner_far", j).start()
            self.copy(a, "twin_bucket", j).start()
            self.copy(a, "far", j).wait_recv()
            self.copy(a, "corner_bucket", j).start()
            self.copy(a, "twin_far", j).start()

    def finish(self):
        for j in (0, 1, 3, 2):
            for a in self.arrays:
                self.copy(a, "corner_far", j).wait_recv()
                self.copy(a, "twin_corner0", j).start()
                self.copy(a, "corner_bucket", j).wait_recv()
                self.copy(a, "twin_corner1", j).start()
        last = ("twin", "twin_bucket", "twin_far", "twin_corner0", "twin_corner1")
        for a in self.arrays:
            self.keep(a).wait()
            for j in range(4):
                for kind in last:
                    self.copy(a, kind, j).wait_recv()
            for j in range(4):
                if j:
                    self.copy(a, "dp", j).wait_send()
                for kind in ("bucket", "far", "corner_far", "corner_bucket") + last:
                    self.copy(a, kind, j).wait_send()


class Group:
    def __init__(self, x_ref, out_ref, parts, sems, own_sem):
        bucket, dp, seq, far, twin = own_place()
        to_far, to_twin = {"seq": far}, {"seq": twin}
        rows = x_ref.shape[0] // parts

        def cut(ref, p):
            return ref.at[pl.ds(p * rows, rows)]

        self.keep = pltpu.make_async_copy(x_ref, out_ref.at[seq], own_sem)
        self.fars = [
            hand_over(cut(x_ref, p), cut(out_ref.at[seq], p), sems, p, to_far)
            for p in range(parts)
        ]
        self.twins = hand_over(x_ref, out_ref.at[seq], sems, parts, to_twin)
        self.relays = [
            hand_over(cut(out_ref.at[far], p), cut(out_ref.at[far], p), sems, parts + 1 + p, to_twin)
            for p in range(parts)
        ]

    def start(self):
        for copy in self.fars:
            copy.start()
        self.twins.start()
        self.keep.start()

    def finish(self):
        for far, relay in zip(self.fars, self.relays):
            far.wait_recv()
            relay.start()
        self.keep.wait()
        self.twins.wait()
        for far, relay in zip(self.fars, self.relays):
            far.wait_send()
            relay.wait()


def gather_all_kernel(x_ref, out_ref, send_sem, recv_sem, own_sem):
    spread = Spread((x_ref,), (out_ref,), (False,), (send_sem, recv_sem), own_sem)
    greet(spread.partners)
    spread.start()
    for step in (1, 3, 2, 4):
        spread.relay(step)
    spread.finish()


def gather_all(block, number):
    return pl.pallas_call(
        gather_all_kernel,
        out_shape=jax.ShapeDtypeStruct((32 * block.shape[0], block.shape[1]), block.dtype),
        in_specs=[pl.BlockSpec(memory_space=pl.ANY)],
        out_specs=pl.BlockSpec(memory_space=pl.ANY),
        scratch_shapes=[
            pltpu.SemaphoreType.DMA((1, 39)),
            pltpu.SemaphoreType.DMA((1, 39)),
            pltpu.SemaphoreType.DMA((1,)),
        ],
        compiler_params=pltpu.CompilerParams(collective_id=number, has_side_effects=True),
    )(block)


def group_kernel(parts, x_ref, out_ref, send_sem, recv_sem, own_sem):
    group = Group(x_ref, out_ref, parts, (send_sem, recv_sem), own_sem)
    bucket, dp, seq, far, twin = own_place()
    greet([{"seq": far}, {"seq": twin}])
    group.start()
    group.finish()


def gather_group(block, number, parts=2):
    return pl.pallas_call(
        functools.partial(group_kernel, parts),
        out_shape=jax.ShapeDtypeStruct((4,) + block.shape, block.dtype),
        in_specs=[pl.BlockSpec(memory_space=pl.ANY)],
        out_specs=pl.BlockSpec(memory_space=pl.ANY),
        scratch_shapes=[
            pltpu.SemaphoreType.DMA((2 * parts + 1,)),
            pltpu.SemaphoreType.DMA((2 * parts + 1,)),
            pltpu.SemaphoreType.DMA,
        ],
        compiler_params=pltpu.CompilerParams(collective_id=number, has_side_effects=True),
    )(block)


def opening_kernel(
    cond_ref,
    ada_ref,
    bias_ref,
    patches_ref,
    grad_ref,
    qkv_ref,
    small_ref,
    modul_ref,
    patches_out,
    grad_out,
    qkv_out,
    small_out,
    cond_in,
    part,
    part_in,
    send_sem,
    recv_sem,
    own_sem,
    side_send,
    side_recv,
    side_own,
    mod_send,
    mod_recv,
):
    bucket, dp, seq, far, twin = own_place()
    spread = Spread(
        (qkv_ref, small_ref), (qkv_out, small_out), (True, True), (send_sem, recv_sem), own_sem
    )
    sides = [
        Group(ref, out, 2, (side_send.at[i], side_recv.at[i]), side_own.at[i])
        for i, (ref, out) in enumerate(((patches_ref, patches_out), (grad_ref, grad_out)))
    ]
    greet(spread.partners)
    mods = (mod_send, mod_recv)
    conds = [
        hand_over(cond_ref.at[lax.rem(dp + k, 4)], cond_in.at[k - 1], mods, (0, k - 1), spread.to_dp[k])
        for k in (1, 2, 3)
    ]
    for copy in conds:
        copy.start()
    sides[0].start()
    spread.start()
    sides[1].start()
    for copy in conds:
        copy.wait_recv()
    images = cond_ref.shape[1]
    width = ada_ref.shape[1]
    chunk = width // 4
    for k in range(4):
        rows = cond_ref[dp] if k == 0 else cond_in[k - 1]
        for c in range(4):
            here = pl.ds(c * chunk, chunk)
            share = jnp.dot(
                rows.astype(jnp.bfloat16), ada_ref[:, here], preferred_element_type=jnp.float32
            )
            part[k, :, here] = share
        at = pl.ds(pl.multiple_of(dp * chunk, 128), chunk)
        part[k, :, at] = part[k, :, at] + bias_ref[...]
    shares = [
        hand_over(part.at[k], part_in.at[k - 1], mods, (1, k - 1), spread.to_dp[4 - k])
        for k in (1, 2, 3)
    ]
    for copy in shares:
        copy.start()
    spread.relay(1)
    spread.relay(3)
    for copy in shares:
        copy.wait_recv()
    modul_ref[...] = part[0] + part_in[0] + part_in[1] + part_in[2]
    spread.relay(2)
    spread.relay(4)
    sides[0].finish()
    spread.finish()
    sides[1].finish()
    for copy in conds + shares:
        copy.wait_send()


def opening(cond_cols, ada_weight, bias, patches, out_grad, qkv_weight, small, number):
    _, images, columns = cond_cols.shape
    width = ada_weight.shape[1]
    anywhere = pl.BlockSpec(memory_space=pl.ANY)
    inside = pl.BlockSpec(memory_space=pltpu.VMEM)
    dma = pltpu.SemaphoreType.DMA
    return pl.pallas_call(
        opening_kernel,
        out_shape=(
            jax.ShapeDtypeStruct((images, width), jnp.float32),
            jax.ShapeDtypeStruct((4,) + patches.shape, patches.dtype),
            jax.ShapeDtypeStruct((4,) + out_grad.shape, out_grad.dtype),
            jax.ShapeDtypeStruct((4 * qkv_weight.shape[0], qkv_weight.shape[1]), qkv_weight.dtype),
            jax.ShapeDtypeStruct((4 * small.shape[0], small.shape[1]), small.dtype),
        ),
        in_specs=[inside] * 3 + [anywhere] * 4,
        out_specs=(inside,) + (anywhere,) * 4,
        scratch_shapes=[
            pltpu.VMEM((3, images, columns), jnp.float32),
            pltpu.VMEM((4, images, width), jnp.float32),
            pltpu.VMEM((3, images, width), jnp.float32),
            dma((2, 39)),
            dma((2, 39)),
            dma((2,)),
            dma((2, 5)),
            dma((2, 5)),
            dma((2,)),
            dma((2, 3)),
            dma((2, 3)),
        ],
        compiler_params=pltpu.CompilerParams(
            collective_id=number, has_side_effects=True, vmem_limit_bytes=16 * 2**20
        ),
    )(cond_cols, ada_weight, bias, patches, out_grad, qkv_weight, small)


def settle_kernel(parts, x_ref, out_ref, from_twin, outgo, from_far, send_sem, recv_sem):
    sems = (send_sem, recv_sem)
    bucket, dp, seq, far, twin = own_place()
    twin_far = lax.rem(twin + 2, 4)
    to_far, to_twin = {"seq": far}, {"seq": twin}
    greet([to_far, to_twin])
    rows = x_ref.shape[1] // parts

    def cut(ref, p):
        return ref.at[pl.ds(p * rows, rows)]

    first = [
        hand_over(cut(x_ref.at[twin_far], p), cut(from_twin.at[0], p), sems, p, to_twin)
        for p in range(parts)
    ]
    second = hand_over(x_ref.at[twin], from_twin.at[1], sems, parts, to_twin)
    third = [
        hand_over(cut(outgo, p), cut(from_far, p), sems, parts + 1 + p, to_far)
        for p in range(parts)
    ]
    for copy in first:
        copy.start()
    second.start()
    for p in range(parts):
        first[p].wait_recv()
        here = pl.ds(p * rows, rows)
        outgo[here] = (
            x_ref[far, here].astype(jnp.float32) + from_twin[0, here].astype(jnp.float32)
        ).astype(outgo.dtype)
        third[p].start()
    second.wait_recv()
    for p in range(parts):
        here = pl.ds(p * rows, rows)
        third[p].wait_recv()
        out_ref[here] = (
            x_ref[seq, here].astype(jnp.float32)
            + from_twin[1, here].astype(jnp.float32)
            + from_far[here].astype(jnp.float32)
        ).astype(out_ref.dtype)
    second.wait_send()
    for p in range(parts):
        first[p].wait_send()
        third[p].wait_send()


def settle_group(shares, number, parts=4):
    _, rows, columns = shares.shape
    return pl.pallas_call(
        functools.partial(settle_kernel, parts),
        out_shape=jax.ShapeDtypeStruct((rows, columns), shares.dtype),
        in_specs=[pl.BlockSpec(memory_space=pltpu.VMEM)],
        out_specs=pl.BlockSpec(memory_space=pltpu.VMEM),
        scratch_shapes=[
            pltpu.VMEM((2, rows, columns), shares.dtype),
            pltpu.VMEM((rows, columns), shares.dtype),
            pltpu.VMEM((rows, columns), shares.dtype),
            pltpu.SemaphoreType.DMA((2 * parts + 1,)),
            pltpu.SemaphoreType.DMA((2 * parts + 1,)),
        ],
        compiler_params=pltpu.CompilerParams(
            collective_id=number, has_side_effects=True, vmem_limit_bytes=24 * 2**20
        ),
    )(shares)


def body_general(
    patches,
    conditioning,
    image_slot,
    routes,
    ada_weight,
    ada_bias,
    qkv_weight,
    out_weight,
    router_weight,
    shared_in,
    shared_out,
    expert_in,
    expert_out,
    out_grad,
):
    seq_count = lax.axis_size("seq")
    seq_place = lax.axis_index("seq")
    outer_count = lax.axis_size(("bucket", "dp"))
    tok_rows = patches.shape[0]
    width = patches.shape[1]
    images = conditioning.shape[0]
    local_experts = expert_in.shape[0]
    all_experts = local_experts * seq_count
    capacity = 3 * tok_rows // all_experts
    head_dim = width // HEADS
    score_scale = 1.0 / math.sqrt(head_dim)
    dense = (
        lax.all_gather(ada_weight, "dp", axis=0, tiled=True),
        lax.all_gather(ada_bias, "dp", axis=0, tiled=True),
        lax.all_gather(qkv_weight, "dp", axis=0, tiled=True),
        lax.all_gather(out_weight, "dp", axis=0, tiled=True),
        lax.all_gather(router_weight, "dp", axis=0, tiled=True),
        lax.all_gather(shared_in, "dp", axis=0, tiled=True),
        lax.all_gather(shared_out, "dp", axis=0, tiled=True),
    )
    ada_full, bias_full, qkv_full, proj_full, router_full, inner_full, outer_full = dense
    cond_float = conditioning.astype(jnp.float32)
    cond_act = silu_curve(cond_float).astype(jnp.bfloat16)
    modul = matmul_low(cond_act, ada_full) + bias_full.astype(jnp.float32)
    own_slots = lax.dynamic_slice_in_dim(image_slot, seq_place * tok_rows, tok_rows)
    image_ids = jnp.arange(images, dtype=jnp.int32)
    onehot = (own_slots[:, None] == image_ids[None, :]).astype(jnp.float32)
    per_row = jnp.dot(onehot, modul, precision=highest)
    shift_one, scale_one, gate_one, shift_two, scale_two, gate_two = jnp.split(per_row, 6, axis=1)
    rows_float = patches.astype(jnp.float32)
    hidden_one_f, norm_one_pull = jax.vjp(modulate, rows_float, scale_one, shift_one)
    hidden_one = hidden_one_f.astype(jnp.bfloat16)
    project = matmul_low(hidden_one, qkv_full).astype(jnp.bfloat16)
    queries_heads = project[:, :width].reshape(tok_rows, HEADS, head_dim)
    key_value = project[:, width:]
    kv_all = lax.all_gather(key_value, "seq", axis=0, tiled=True)
    group_rows = kv_all.shape[0]
    keys_all = kv_all[:, :width].reshape(group_rows, HEADS, head_dim)
    values_all = kv_all[:, width:].reshape(group_rows, HEADS, head_dim)
    scores = (
        jnp.einsum("qhd,khd->hqk", queries_heads, keys_all, preferred_element_type=jnp.float32)
        * score_scale
    )
    same_image = own_slots[:, None] == image_slot[None, :]
    scores = jnp.where(same_image[None, :, :], scores, -1e30)
    row_max = jnp.max(scores, axis=-1, keepdims=True)
    exp_scores = jnp.exp(scores - row_max)
    probs = exp_scores / jnp.sum(exp_scores, axis=-1, keepdims=True)
    probs_low = probs.astype(jnp.bfloat16)
    mixed = (
        jnp.einsum("hqk,khd->qhd", probs_low, values_all, preferred_element_type=jnp.float32)
        .reshape(tok_rows, width)
        .astype(jnp.bfloat16)
    )
    branch = matmul_low(mixed, proj_full)
    after = rows_float + gate_one * branch
    hidden_two_f, norm_two_pull = jax.vjp(modulate, after, scale_two, shift_two)
    hidden_two = hidden_two_f.astype(jnp.bfloat16)
    shared_inner = matmul_low(hidden_two, inner_full)
    shared_act = gelu_curve(shared_inner).astype(jnp.bfloat16)
    shared_val = matmul_low(shared_act, outer_full)
    logits = matmul_low(hidden_two, router_full)
    expert_ids = jnp.arange(all_experts, dtype=jnp.int32)
    pick_zero = (routes[:, 0:1] == expert_ids[None, :]).astype(jnp.float32)
    pick_one = (routes[:, 1:2] == expert_ids[None, :]).astype(jnp.float32)
    pair = jnp.stack(
        [jnp.sum(logits * pick_zero, axis=1), jnp.sum(logits * pick_one, axis=1)], axis=1
    )
    pair_max = jnp.max(pair, axis=1, keepdims=True)
    pair_exp = jnp.exp(pair - pair_max)
    gates = pair_exp / jnp.sum(pair_exp, axis=1, keepdims=True)
    flat_routes = routes.reshape(-1)
    pair_hits = (flat_routes[:, None] == expert_ids[None, :]).astype(jnp.int32)
    running = jnp.cumsum(pair_hits, axis=0)
    place = jnp.sum(running * pair_hits, axis=1) - 1
    slot_of = flat_routes * capacity + place
    slot_ids = jnp.arange(all_experts * capacity, dtype=jnp.int32)
    spread = (slot_ids[:, None] == slot_of[None, :]).astype(jnp.bfloat16)
    spread_pairs = spread.reshape(all_experts * capacity, tok_rows, 2)
    dispatch_mat = spread_pairs[:, :, 0] + spread_pairs[:, :, 1]
    send = (
        matmul_low(dispatch_mat, hidden_two)
        .astype(jnp.bfloat16)
        .reshape(seq_count, local_experts, capacity, width)
    )
    inner = jnp.einsum(
        "secd,edf->secf",
        lax.all_to_all(send, "seq", split_axis=0, concat_axis=0, tiled=True),
        expert_in,
        preferred_element_type=jnp.float32,
    )
    active = gelu_curve(inner).astype(jnp.bfloat16)
    result = jnp.einsum(
        "secf,efd->secd", active, expert_out, preferred_element_type=jnp.float32
    ).astype(jnp.bfloat16)
    returned = lax.all_to_all(result, "seq", split_axis=0, concat_axis=0, tiled=True)
    slot_values = returned.reshape(all_experts * capacity, width)
    picked_zero = matmul_left_t(spread_pairs[:, :, 0], slot_values)
    picked_one = matmul_left_t(spread_pairs[:, :, 1], slot_values)
    mixture = shared_val + gates[:, 0:1] * picked_zero + gates[:, 1:2] * picked_one
    block_out = (after + gate_two * mixture).astype(jnp.bfloat16)
    grad_block = out_grad.astype(jnp.float32)
    grad_gate_two = grad_block * mixture
    grad_mix = grad_block * gate_two
    back_dense = (
        lax.all_gather(ada_weight, "dp", axis=0, tiled=True),
        lax.all_gather(qkv_weight, "dp", axis=0, tiled=True),
        lax.all_gather(out_weight, "dp", axis=0, tiled=True),
        lax.all_gather(router_weight, "dp", axis=0, tiled=True),
        lax.all_gather(shared_in, "dp", axis=0, tiled=True),
        lax.all_gather(shared_out, "dp", axis=0, tiled=True),
    )
    ada_back, qkv_back, proj_back, router_back, inner_back, outer_back = back_dense
    grad_shared = grad_mix.astype(jnp.bfloat16)
    grad_shared_act = matmul_right_t(grad_shared, outer_back)
    grad_shared_inner = (grad_shared_act * gelu_slope(shared_inner)).astype(jnp.bfloat16)
    grad_outer_w = matmul_left_t(shared_act, grad_shared)
    grad_inner_w = matmul_left_t(hidden_two, grad_shared_inner)
    grad_hidden = matmul_right_t(grad_shared_inner, inner_back)
    grad_gates = jnp.stack(
        [jnp.sum(grad_mix * picked_zero, axis=1), jnp.sum(grad_mix * picked_one, axis=1)], axis=1
    )
    grad_pair = gates * (grad_gates - jnp.sum(gates * grad_gates, axis=1, keepdims=True))
    grad_logits = (grad_pair[:, 0:1] * pick_zero + grad_pair[:, 1:2] * pick_one).astype(
        jnp.bfloat16
    )
    grad_router_w = matmul_left_t(hidden_two, grad_logits)
    grad_hidden = grad_hidden + matmul_right_t(grad_logits, router_back)
    grad_pairs = (
        jnp.stack([gates[:, 0:1] * grad_mix, gates[:, 1:2] * grad_mix], axis=1)
        .reshape(2 * tok_rows, width)
        .astype(jnp.bfloat16)
    )
    grad_send = (
        matmul_low(spread, grad_pairs)
        .astype(jnp.bfloat16)
        .reshape(seq_count, local_experts, capacity, width)
    )
    inputs_in = lax.all_to_all(send, "seq", split_axis=0, concat_axis=0, tiled=True)
    grads_in = lax.all_to_all(grad_send, "seq", split_axis=0, concat_axis=0, tiled=True)
    inner = jnp.einsum("secd,edf->secf", inputs_in, expert_in, preferred_element_type=jnp.float32)
    active = gelu_curve(inner).astype(jnp.bfloat16)
    grad_act = jnp.einsum(
        "secd,efd->secf", grads_in, expert_out, preferred_element_type=jnp.float32
    )
    grad_inner = (grad_act * gelu_slope(inner)).astype(jnp.bfloat16)
    grad_rows = jnp.einsum(
        "secf,edf->secd", grad_inner, expert_in, preferred_element_type=jnp.float32
    ).astype(jnp.bfloat16)
    sent_back = lax.all_to_all(grad_rows, "seq", split_axis=0, concat_axis=0, tiled=True)
    grad_expert_in = jnp.einsum(
        "secd,secf->edf", inputs_in, grad_inner, preferred_element_type=jnp.float32
    )
    grad_expert_out = jnp.einsum(
        "secf,secd->efd", active, grads_in, preferred_element_type=jnp.float32
    )
    grad_hidden = grad_hidden + matmul_left_t(
        dispatch_mat, sent_back.reshape(all_experts * capacity, width)
    )
    grad_after_norm, grad_scale_two, grad_shift_two = norm_two_pull(grad_hidden)
    grad_after = grad_block + grad_after_norm
    grad_gate_one = grad_after * branch
    grad_branch = (grad_after * gate_one).astype(jnp.bfloat16)
    grad_proj_w = matmul_left_t(mixed, grad_branch)
    grad_mixed = matmul_right_t(grad_branch, proj_back).astype(jnp.bfloat16)
    grad_mixed_heads = grad_mixed.reshape(tok_rows, HEADS, head_dim)
    grad_probs = jnp.einsum(
        "qhd,khd->hqk", grad_mixed_heads, values_all, preferred_element_type=jnp.float32
    )
    row_dot = jnp.sum(probs * grad_probs, axis=-1, keepdims=True)
    grad_scores = (probs * (grad_probs - row_dot)).astype(jnp.bfloat16)
    grad_queries = (
        jnp.einsum("hqk,khd->qhd", grad_scores, keys_all, preferred_element_type=jnp.float32)
        * score_scale
    )
    grad_keys = (
        jnp.einsum("hqk,qhd->khd", grad_scores, queries_heads, preferred_element_type=jnp.float32)
        * score_scale
    )
    grad_values = jnp.einsum(
        "hqk,qhd->khd", probs_low, grad_mixed_heads, preferred_element_type=jnp.float32
    )
    grad_kv = lax.psum_scatter(
        jnp.concatenate(
            [
                grad_keys.reshape(lax.axis_size("seq") * tok_rows, width),
                grad_values.reshape(lax.axis_size("seq") * tok_rows, width),
            ],
            axis=1,
        ).astype(jnp.bfloat16),
        "seq",
        scatter_dimension=0,
        tiled=True,
    ).astype(jnp.float32)
    grad_project = jnp.concatenate([grad_queries.reshape(tok_rows, width), grad_kv], axis=1).astype(
        jnp.bfloat16
    )
    grad_qkv_w = matmul_left_t(hidden_one, grad_project)
    grad_hidden_one = matmul_right_t(grad_project, qkv_back)
    grad_rows, grad_scale_one, grad_shift_one = norm_one_pull(grad_hidden_one)
    patch_grad = grad_after + grad_rows
    grad_per_row = jnp.concatenate(
        [
            grad_shift_one,
            grad_scale_one,
            grad_gate_one,
            grad_shift_two,
            grad_scale_two,
            grad_gate_two,
        ],
        axis=1,
    )
    grad_modul = lax.dot_general(onehot, grad_per_row, (((0,), (0,)), ((), ())), precision=highest)
    grad_ada_w = lax.dot_general(
        cond_act.astype(jnp.float32), grad_modul, (((0,), (0,)), ((), ())), precision=highest
    )
    grad_ada_b = jnp.sum(grad_modul, axis=0)
    grad_cond_part = lax.dot_general(
        grad_modul,
        ada_back,
        (((1,), (1,)), ((), ())),
        precision=highest,
        preferred_element_type=jnp.float32,
    ) * silu_slope(cond_float)
    dense_terms = (
        grad_ada_w,
        grad_ada_b,
        grad_qkv_w,
        grad_proj_w,
        grad_router_w,
        grad_inner_w,
        grad_outer_w,
    )
    ordered = tuple((order_rows(term, outer_count, seq_count) for term in dense_terms))
    first_sums = (
        lax.psum_scatter(
            grad_cond_part.astype(jnp.bfloat16), "seq", scatter_dimension=1, tiled=True
        ).astype(jnp.float32),
        lax.psum_scatter(
            ordered[0].astype(jnp.bfloat16), "seq", scatter_dimension=0, tiled=True
        ).astype(jnp.float32),
        lax.psum_scatter(
            ordered[1].astype(jnp.bfloat16), "seq", scatter_dimension=0, tiled=True
        ).astype(jnp.float32),
        lax.psum_scatter(
            ordered[2].astype(jnp.bfloat16), "seq", scatter_dimension=0, tiled=True
        ).astype(jnp.float32),
        lax.psum_scatter(
            ordered[3].astype(jnp.bfloat16), "seq", scatter_dimension=0, tiled=True
        ).astype(jnp.float32),
        lax.psum_scatter(
            ordered[4].astype(jnp.bfloat16), "seq", scatter_dimension=0, tiled=True
        ).astype(jnp.float32),
        lax.psum_scatter(
            ordered[5].astype(jnp.bfloat16), "seq", scatter_dimension=0, tiled=True
        ).astype(jnp.float32),
        lax.psum_scatter(
            ordered[6].astype(jnp.bfloat16), "seq", scatter_dimension=0, tiled=True
        ).astype(jnp.float32),
    )
    cond_grad = first_sums[0]
    second_sums = (
        lax.psum_scatter(first_sums[1], ("bucket", "dp"), scatter_dimension=0, tiled=True),
        lax.psum_scatter(first_sums[2], ("bucket", "dp"), scatter_dimension=0, tiled=True),
        lax.psum_scatter(first_sums[3], ("bucket", "dp"), scatter_dimension=0, tiled=True),
        lax.psum_scatter(first_sums[4], ("bucket", "dp"), scatter_dimension=0, tiled=True),
        lax.psum_scatter(first_sums[5], ("bucket", "dp"), scatter_dimension=0, tiled=True),
        lax.psum_scatter(first_sums[6], ("bucket", "dp"), scatter_dimension=0, tiled=True),
        lax.psum_scatter(first_sums[7], ("bucket", "dp"), scatter_dimension=0, tiled=True),
        lax.psum_scatter(grad_expert_in, ("bucket", "dp"), scatter_dimension=1, tiled=True),
        lax.psum_scatter(grad_expert_out, ("bucket", "dp"), scatter_dimension=1, tiled=True),
    )
    dense_out = second_sums[:7]
    expert_sums = second_sums[7:]
    return (
        block_out,
        patch_grad,
        cond_grad,
        dense_out[0],
        dense_out[1],
        dense_out[2],
        dense_out[3],
        dense_out[4],
        dense_out[5],
        dense_out[6],
        expert_sums[0],
        expert_sums[1],
    )


def norm_parts(rows_in):
    centred = rows_in - jnp.mean(rows_in, axis=-1, keepdims=True)
    scale = lax.rsqrt(jnp.mean(centred * centred, axis=-1, keepdims=True) + norm_eps)
    return centred * scale, scale


def norm_back(grad_normed, normed, scale):
    mean_grad = jnp.mean(grad_normed, axis=-1, keepdims=True)
    mean_prod = jnp.mean(grad_normed * normed, axis=-1, keepdims=True)
    return scale * (grad_normed - mean_grad - normed * mean_prod)


def two_parts(value):
    high = value.astype(jnp.bfloat16)
    return high, (value - high.astype(jnp.float32)).astype(jnp.bfloat16)


def body_tokens(
    patches,
    conditioning,
    image_slot,
    routes,
    ada_weight,
    ada_bias,
    qkv_weight,
    out_weight,
    router_weight,
    shared_in,
    shared_out,
    expert_in,
    expert_out,
    out_grad,
):
    bf16, f32 = jnp.bfloat16, jnp.float32
    every = ("bucket", "dp", "seq")
    outer = ("bucket", "dp")
    spare = ("bucket", "seq")
    seq_count = lax.axis_size("seq")
    dp_count = lax.axis_size("dp")
    outer_count = lax.axis_size(outer)
    spare_count = lax.axis_size(spare)
    devices = outer_count * seq_count
    seq_place = lax.axis_index("seq")
    dp_place = lax.axis_index("dp")
    outer_place = lax.axis_index(outer)
    place_all = lax.axis_index(every)
    spare_place = lax.axis_index(spare)
    tok_rows, width = patches.shape
    images = conditioning.shape[0]
    hidden = shared_in.shape[1]
    quarters = hidden // width
    local_experts = expert_in.shape[0]
    all_experts = local_experts * seq_count
    capacity = 3 * tok_rows // all_experts
    head_dim = width // HEADS
    score_scale = 1.0 / math.sqrt(head_dim)

    def piece(weight):
        rows = weight.shape[0] // spare_count
        return lax.dynamic_slice_in_dim(weight, spare_place * rows, rows)

    turned = ("dp", "bucket", "seq")
    pieces = piece(shared_in).reshape(-1, quarters, width)
    rows_in = pieces.shape[0]
    load = jnp.concatenate(
        [out_grad, jnp.swapaxes(pieces, 0, 1).reshape(-1, width), piece(shared_out)], axis=0
    )
    loads = lax.all_gather(load, turned, axis=0, tiled=True).reshape(devices, -1, width)
    inner_full = jnp.swapaxes(
        loads[:, tok_rows : tok_rows + quarters * rows_in].reshape(devices, quarters, rows_in, width),
        0,
        1,
    ).reshape(quarters, width, width)
    outer_full = loads[:, tok_rows + quarters * rows_in :].reshape(quarters, width, width)

    cond_float = conditioning.astype(f32)
    cond_act = silu_curve(cond_float).astype(bf16)
    cond_all = lax.all_gather(cond_act, outer, axis=0, tiled=True)
    cond_cols = jnp.swapaxes(cond_act.astype(f32).reshape(images, dp_count, -1), 0, 1)
    small = jnp.concatenate(
        [out_weight, jnp.pad(router_weight, ((0, 0), (0, 128 - all_experts)))], axis=1
    )
    modul, patches_group, grads_group, qkv_full, small_full = opening(
        cond_cols,
        ada_weight,
        ada_bias.astype(f32)[None, :],
        patches,
        out_grad,
        qkv_weight,
        small,
        1,
    )
    proj_full = small_full[:, :width]
    router_full = small_full[:, width : width + all_experts]
    slots_group = image_slot.reshape(seq_count, tok_rows)[:, 0]
    slot = lax.dynamic_slice_in_dim(slots_group, seq_place, 1)[0]
    row = lax.dynamic_slice_in_dim(modul, slot, 1)
    image_ids_own = jnp.arange(images, dtype=jnp.int32)
    rows_group = jnp.sum(
        jnp.where(
            (slots_group[:, None] == image_ids_own[None, :])[:, :, None], modul[None], 0.0
        ),
        axis=1,
    )
    shift_one, scale_one, gate_one, shift_two, scale_two, gate_two = jnp.split(row, 6, axis=1)

    grad_block = out_grad.astype(f32)
    grad_mix = grad_block * gate_two
    grad_low = grad_mix.astype(bf16)
    grads_low_group = (grads_group.astype(f32) * rows_group[:, None, 5 * width :]).astype(bf16)

    rows_float = patches.astype(f32)
    normed_one, root_one = norm_parts(rows_float)
    hidden_one = (normed_one * (1.0 + scale_one) + shift_one).astype(bf16)
    normed_group, _ = norm_parts(patches_group.astype(f32))
    hidden_group = (
        normed_group * (1.0 + rows_group[:, None, width : 2 * width]) + rows_group[:, None, :width]
    ).astype(bf16)
    group_rows = seq_count * tok_rows
    queries_heads = (
        matmul_low(hidden_one, qkv_full[:, :width]).astype(bf16).reshape(tok_rows, HEADS, head_dim)
    )
    kv_all = matmul_low(hidden_group.reshape(group_rows, width), qkv_full[:, width:]).astype(bf16)
    keys_all = kv_all[:, :width].reshape(group_rows, HEADS, head_dim)
    values_all = kv_all[:, width:].reshape(group_rows, HEADS, head_dim)
    scores = (
        jnp.einsum("qhd,khd->hqk", queries_heads, keys_all, preferred_element_type=f32)
        * score_scale
    )
    same_image = (slot == image_slot)[None, None, :]
    scores = jnp.where(same_image, scores, -1e30)
    row_max = jnp.max(scores, axis=-1, keepdims=True)
    exp_scores = jnp.exp(scores - row_max)
    probs = exp_scores / jnp.sum(exp_scores, axis=-1, keepdims=True)
    probs_low = probs.astype(bf16)
    mixed = (
        jnp.einsum("hqk,khd->qhd", probs_low, values_all, preferred_element_type=f32)
        .reshape(tok_rows, width)
        .astype(bf16)
    )
    branch = matmul_low(mixed, proj_full)
    after = rows_float + gate_one * branch
    normed_two, root_two = norm_parts(after)
    hidden_two = (normed_two * (1.0 + scale_two) + shift_two).astype(bf16)

    logits = matmul_low(hidden_two, router_full)
    expert_ids = jnp.arange(all_experts, dtype=jnp.int32)
    pick_zero = (routes[:, 0:1] == expert_ids[None, :]).astype(f32)
    pick_one = (routes[:, 1:2] == expert_ids[None, :]).astype(f32)
    pair_zero = jnp.sum(logits * pick_zero, axis=1, keepdims=True)
    pair_one = jnp.sum(logits * pick_one, axis=1, keepdims=True)
    pair_max = jnp.maximum(pair_zero, pair_one)
    exp_zero = jnp.exp(pair_zero - pair_max)
    exp_one = jnp.exp(pair_one - pair_max)
    gate_zero = exp_zero / (exp_zero + exp_one)
    gate_one_pick = exp_one / (exp_zero + exp_one)
    hits = pick_zero + pick_one
    place = jnp.cumsum(hits, axis=0) * hits
    gate_table = gate_zero * pick_zero + gate_one_pick * pick_one
    gate_high, gate_rest = two_parts(gate_table)
    extras = jnp.concatenate(
        [
            hidden_two,
            place.astype(bf16),
            gate_high,
            gate_rest,
            jnp.zeros((tok_rows, 128 - 3 * all_experts), bf16),
        ],
        axis=1,
    )
    gate_two_high, gate_two_rest = two_parts(gate_two)
    gate_two_last = (gate_two - gate_two_high.astype(f32) - gate_two_rest.astype(f32)).astype(bf16)
    gate_rows = jnp.pad(
        jnp.concatenate([gate_two_high, gate_two_rest, gate_two_last], axis=0), ((0, 13), (0, 128))
    )
    extras = jnp.concatenate([extras, gate_rows], axis=0)
    extras_all = lax.all_gather(extras, turned, axis=0, tiled=True)
    extras_group = gather_group(extras, 2)

    slot_ids = jnp.arange(1, capacity + 1, dtype=jnp.int32)[None, :, None]
    spread = (place.astype(jnp.int32).T[:, None, :] == slot_ids).astype(bf16)
    spread = spread.reshape(all_experts * capacity, tok_rows)
    first_expert = seq_place * local_experts

    def slot_gather(table, x_blocks, g_blocks):
        place_own = lax.dynamic_slice_in_dim(table, first_expert, local_experts, axis=2)
        high_own = lax.dynamic_slice_in_dim(table, first_expert + all_experts, local_experts, axis=2)
        rest_own = lax.dynamic_slice_in_dim(
            table, first_expert + 2 * all_experts, local_experts, axis=2
        )
        gate_own = high_own.astype(f32) + rest_own.astype(f32)
        picks = jnp.swapaxes(place_own.astype(jnp.int32), 1, 2)[:, :, None, :] == slot_ids[None]
        picks_low = picks.astype(bf16)
        pick_gate = jnp.sum(
            jnp.where(picks, jnp.swapaxes(gate_own, 1, 2)[:, :, None, :], 0.0), axis=3, keepdims=True
        )
        x_slots = jnp.einsum(
            "becd,bdw->becw", picks_low, x_blocks, preferred_element_type=f32
        ).astype(bf16)
        g_slots = (
            pick_gate
            * jnp.einsum("becd,bdw->becw", picks_low, g_blocks, preferred_element_type=f32)
        ).astype(bf16)
        return x_slots, g_slots

    inputs_in, grads_in = slot_gather(
        extras_group[:, :tok_rows, width:], extras_group[:, :tok_rows, :width], grads_low_group
    )
    inner = jnp.einsum("secd,edf->secf", inputs_in, expert_in, preferred_element_type=f32)
    active = gelu_curve(inner).astype(bf16)
    result = jnp.einsum("secf,efd->secd", active, expert_out, preferred_element_type=f32).astype(
        bf16
    )
    grad_act = jnp.einsum("secd,efd->secf", grads_in, expert_out, preferred_element_type=f32)
    grad_inner = (grad_act * gelu_slope(inner)).astype(bf16)
    grad_rows = jnp.einsum(
        "secf,edf->secd", grad_inner, expert_in, preferred_element_type=f32
    ).astype(bf16)
    back = lax.all_to_all(
        jnp.concatenate([result, grad_rows], axis=3), "seq", split_axis=0, concat_axis=0, tiled=True
    ).reshape(all_experts * capacity, 2 * width)

    shared_inner = jnp.einsum("td,qdf->qtf", hidden_two, inner_full, preferred_element_type=f32)
    shared_act = gelu_curve(shared_inner).astype(bf16)
    shared_val = jnp.einsum("qtf,qfd->td", shared_act, outer_full, preferred_element_type=f32)
    grad_shared_inner = (
        jnp.einsum("td,qfd->qtf", grad_low, outer_full, preferred_element_type=f32)
        * gelu_slope(shared_inner)
    ).astype(bf16)
    grad_hidden = jnp.einsum("qtf,qdf->td", grad_shared_inner, inner_full, preferred_element_type=f32)

    spread_zero = spread * pick_zero.T[:, None, :].repeat(capacity, axis=1).reshape(
        all_experts * capacity, tok_rows
    ).astype(bf16)
    spread_one = spread - spread_zero
    picked_zero = matmul_left_t(spread_zero, back[:, :width])
    picked_one = matmul_left_t(spread_one, back[:, :width])
    mixture = shared_val + gate_zero * picked_zero + gate_one_pick * picked_one
    block_out = (after + gate_two * mixture).astype(bf16)
    grad_gate_two = jnp.sum(grad_block * mixture, axis=0, keepdims=True)
    dot_zero = jnp.sum(grad_mix * picked_zero, axis=1, keepdims=True)
    dot_one = jnp.sum(grad_mix * picked_one, axis=1, keepdims=True)
    dot_both = gate_zero * dot_zero + gate_one_pick * dot_one
    grad_logits = (
        gate_zero * (dot_zero - dot_both) * pick_zero
        + gate_one_pick * (dot_one - dot_both) * pick_one
    ).astype(bf16)
    grad_router_w = matmul_left_t(hidden_two, grad_logits)
    grad_hidden = (
        grad_hidden
        + matmul_right_t(grad_logits, router_full)
        + matmul_left_t(spread, back[:, width:])
    )
    grad_scale_two = jnp.sum(grad_hidden * normed_two, axis=0, keepdims=True)
    grad_shift_two = jnp.sum(grad_hidden, axis=0, keepdims=True)
    grad_after = grad_block + norm_back(grad_hidden * (1.0 + scale_two), normed_two, root_two)
    grad_gate_one = jnp.sum(grad_after * branch, axis=0, keepdims=True)
    grad_branch = (grad_after * gate_one).astype(bf16)
    grad_proj_w = matmul_left_t(mixed, grad_branch)
    grad_mixed = matmul_right_t(grad_branch, proj_full).astype(bf16)
    grad_mixed_heads = grad_mixed.reshape(tok_rows, HEADS, head_dim)
    grad_probs = jnp.einsum(
        "qhd,khd->hqk", grad_mixed_heads, values_all, preferred_element_type=f32
    )
    row_dot = jnp.sum(probs * grad_probs, axis=-1, keepdims=True)
    grad_scores = (probs * (grad_probs - row_dot)).astype(bf16)
    grad_queries = (
        jnp.einsum("hqk,khd->qhd", grad_scores, keys_all, preferred_element_type=f32) * score_scale
    )
    grad_keys = (
        jnp.einsum("hqk,qhd->khd", grad_scores, queries_heads, preferred_element_type=f32)
        * score_scale
    )
    grad_values = jnp.einsum(
        "hqk,qhd->khd", probs_low, grad_mixed_heads, preferred_element_type=f32
    )
    grad_kv = settle_group(
        jnp.concatenate(
            [grad_keys.reshape(group_rows, width), grad_values.reshape(group_rows, width)], axis=1
        )
        .astype(bf16)
        .reshape(seq_count, tok_rows, 2 * width),
        3,
    )
    grad_project = jnp.concatenate(
        [grad_queries.reshape(tok_rows, width).astype(bf16), grad_kv], axis=1
    )
    grad_qkv_w = matmul_left_t(hidden_one, grad_project)
    grad_hidden_one = matmul_right_t(grad_project, qkv_full)
    grad_scale_one = jnp.sum(grad_hidden_one * normed_one, axis=0, keepdims=True)
    grad_shift_one = jnp.sum(grad_hidden_one, axis=0, keepdims=True)
    patch_grad = grad_after + norm_back(
        grad_hidden_one * (1.0 + scale_one), normed_one, root_one
    )

    dense_part = jnp.concatenate([grad_qkv_w, grad_proj_w], axis=1).astype(bf16)
    dense_part, extras_all = lax.optimization_barrier((dense_part, extras_all))
    dense_sum = lax.psum_scatter(dense_part, every, scatter_dimension=0, tiled=True).astype(f32)
    qkv_out = dense_sum[:, : 3 * width]
    proj_out = dense_sum[:, 3 * width :]

    tags = jnp.where(jnp.arange(128) < 1, slot.astype(f32), 0.0)[None, :]
    router_rows = jnp.concatenate(
        [
            grad_shift_one,
            grad_scale_one,
            grad_gate_one,
            grad_shift_two,
            grad_scale_two,
            grad_gate_two,
            tags,
            grad_router_w.reshape(1, width * all_experts),
        ],
        axis=1,
    )
    row_all = lax.all_gather(router_rows, every, axis=0, tiled=True)
    slots_all = row_all[:, 6 * width].astype(jnp.int32)
    image_of = (jnp.arange(devices, dtype=jnp.int32) // seq_count) * images + slots_all
    image_ids = jnp.arange(outer_count * images, dtype=jnp.int32)
    gather_rows = (image_ids[:, None] == image_of[None, :]).astype(f32)
    grad_modul = jnp.dot(gather_rows, row_all[:, : 6 * width], precision=highest)
    own_cols = width // devices
    cond_part = lax.dynamic_slice_in_dim(cond_all, place_all * own_cols, own_cols, axis=1)
    ada_out = lax.dot_general(
        cond_part.astype(f32), grad_modul, (((0,), (0,)), ((), ())), precision=highest
    )
    bias_cols = 6 * width // devices
    bias_out = lax.dynamic_slice_in_dim(jnp.sum(grad_modul, axis=0), place_all * bias_cols, bias_cols)
    router_sum = jnp.sum(row_all[:, 6 * width + 128 :], axis=0).reshape(width, all_experts)
    router_out = lax.dynamic_slice_in_dim(router_sum, place_all * own_cols, own_cols)
    bucket_rows = dp_count * images
    bucket_modul = lax.dynamic_slice_in_dim(
        grad_modul, lax.axis_index("bucket") * bucket_rows, bucket_rows
    )
    cond_rows = lax.dot_general(
        bucket_modul,
        ada_weight.astype(f32),
        (((1,), (1,)), ((), ())),
        precision=highest,
        preferred_element_type=f32,
    )
    cond_back = lax.all_to_all(cond_rows, "dp", split_axis=0, concat_axis=1, tiled=True)
    cond_cols_own = width // seq_count
    cond_out = lax.dynamic_slice_in_dim(
        cond_back * silu_slope(cond_float), seq_place * cond_cols_own, cond_cols_own, axis=1
    )

    extras_blocks = extras_all.reshape(devices, -1, width + 128)
    x_blocks = extras_blocks[:, :tok_rows, :width]
    gate_blocks = jnp.sum(extras_blocks[:, tok_rows : tok_rows + 3, :width].astype(f32), axis=1)
    g_blocks = (loads[:, :tok_rows].astype(f32) * gate_blocks[:, None, :]).astype(bf16)
    x_all = x_blocks.reshape(devices * tok_rows, width)
    grads_all = g_blocks.reshape(devices * tok_rows, width)
    x_slots, g_slots = slot_gather(extras_blocks[:, :tok_rows, width:], x_blocks, g_blocks)
    own_units = hidden // outer_count
    in_own = lax.dynamic_slice_in_dim(expert_in, outer_place * own_units, own_units, axis=2)
    out_own = lax.dynamic_slice_in_dim(expert_out, outer_place * own_units, own_units, axis=1)
    inner_own = jnp.einsum("becw,ewf->becf", x_slots, in_own, preferred_element_type=f32)
    active_own = gelu_curve(inner_own).astype(bf16)
    slope_own = (
        jnp.einsum("becw,efw->becf", g_slots, out_own, preferred_element_type=f32)
        * gelu_slope(inner_own)
    ).astype(bf16)
    expert_out_grad = jnp.einsum(
        "becf,becw->efw", active_own, g_slots, preferred_element_type=f32
    )
    expert_in_cols = jnp.einsum("becw,becf->ewf", x_slots, slope_own, preferred_element_type=f32)
    expert_in_grad = lax.all_to_all(
        expert_in_cols.astype(bf16), outer, split_axis=1, concat_axis=2, tiled=True
    ).astype(f32)

    own_shared = hidden // devices
    quarter = place_all // (width // own_shared)
    within = (place_all % (width // own_shared)) * own_shared
    shared_in_own = lax.dynamic_slice(
        inner_full, (quarter, 0, within), (1, width, own_shared)
    ).reshape(width, own_shared)
    shared_out_own = lax.dynamic_slice(
        outer_full, (quarter, within, 0), (1, own_shared, width)
    ).reshape(own_shared, width)
    inner_sh = matmul_low(x_all, shared_in_own)
    act_sh = gelu_curve(inner_sh).astype(bf16)
    slope_sh = (matmul_right_t(grads_all, shared_out_own) * gelu_slope(inner_sh)).astype(bf16)
    shared_out_grad = matmul_left_t(act_sh, grads_all)
    shared_in_cols = matmul_left_t(x_all, slope_sh)
    shared_in_grad = lax.all_to_all(
        shared_in_cols.astype(bf16), every, split_axis=0, concat_axis=1, tiled=True
    ).astype(f32)
    return (
        block_out,
        patch_grad,
        cond_out,
        ada_out,
        bias_out,
        qkv_out,
        proj_out,
        router_out,
        shared_in_grad,
        shared_out_grad,
        expert_in_grad,
        expert_out_grad,
    )


def solution(mesh):
    in_specs = (
        P(("bucket", "dp", "seq"), None),
        P(("bucket", "dp"), None),
        P(("bucket", "dp")),
        P(("bucket", "dp", "seq"), None),
        P("dp", None),
        P("dp"),
        P("dp", None),
        P("dp", None),
        P("dp", None),
        P("dp", None),
        P("dp", None),
        P("seq", None, None),
        P("seq", None, None),
        P(("bucket", "dp", "seq"), None),
    )
    out_specs = (
        P(("bucket", "dp", "seq"), None),
        P(("bucket", "dp", "seq"), None),
        P(("bucket", "dp"), "seq"),
        P(("bucket", "dp", "seq"), None),
        P(("bucket", "dp", "seq")),
        P(("bucket", "dp", "seq"), None),
        P(("bucket", "dp", "seq"), None),
        P(("bucket", "dp", "seq"), None),
        P(("bucket", "dp", "seq"), None),
        P(("bucket", "dp", "seq"), None),
        P("seq", ("bucket", "dp"), None),
        P("seq", ("bucket", "dp"), None),
    )
    shape = tuple(mesh.shape[name] for name in ("bucket", "dp", "seq"))
    body = body_tokens if shape == (2, 4, 4) else body_general
    return jax.shard_map(body, mesh=mesh, in_specs=in_specs, out_specs=out_specs, check_vma=False)
```

```python
import functools
import math

import jax
import jax.numpy as jnp
from jax import lax
from jax.experimental import pallas as pl
from jax.experimental.pallas import tpu as pltpu
from jax.sharding import PartitionSpec as P

HEADS = 12


highest = lax.Precision.HIGHEST
norm_eps = 1e-06
gelu_coef = 0.7978845608
cube_coef = 0.044715


def sigmoid_curve(inputs):
    return 1.0 / (1.0 + jnp.exp(-inputs))


def silu_curve(inputs):
    return inputs / (1.0 + jnp.exp(-inputs))


def silu_slope(inputs):
    sigma = sigmoid_curve(inputs)
    return sigma * (1.0 + inputs * (1.0 - sigma))


def gelu_curve(inputs):
    return (
        0.5 * inputs * (1.0 + jnp.tanh(gelu_coef * (inputs + cube_coef * inputs * inputs * inputs)))
    )


def gelu_slope(inputs):
    bent = jnp.tanh(gelu_coef * (inputs + cube_coef * inputs * inputs * inputs))
    return 0.5 * (1.0 + bent) + 0.5 * inputs * (1.0 - bent * bent) * gelu_coef * (
        1.0 + 3.0 * cube_coef * inputs * inputs
    )


def modulate(rows_in, scale_in, shift_in):
    centred = rows_in - jnp.mean(rows_in, axis=-1, keepdims=True)
    normed = centred * lax.rsqrt(jnp.mean(centred * centred, axis=-1, keepdims=True) + norm_eps)
    return normed * (1.0 + scale_in) + shift_in


def matmul_low(left, right):
    return jnp.dot(left, right, preferred_element_type=jnp.float32)


def matmul_left_t(left, right):
    return lax.dot_general(
        left, right, (((0,), (0,)), ((), ())), preferred_element_type=jnp.float32
    )


def matmul_right_t(left, right):
    return lax.dot_general(
        left, right, (((1,), (1,)), ((), ())), preferred_element_type=jnp.float32
    )


def order_rows(term, outer_count, inner_count):
    rows = term.shape[0]
    rest = term.shape[1:]
    blocks = term.reshape((outer_count, inner_count, rows // (outer_count * inner_count)) + rest)
    return jnp.swapaxes(blocks, 0, 1).reshape((rows,) + rest)

MESH = pl.DeviceIdType.MESH


def hand_over(src, dst, sems, index, where):
    return pltpu.make_async_remote_copy(
        src_ref=src,
        dst_ref=dst,
        send_sem=sems[0].at[index],
        recv_sem=sems[1].at[index],
        device_id=where,
        device_id_type=MESH,
    )


def greet(partners):
    barrier = pltpu.get_barrier_semaphore()
    for where in partners:
        pl.semaphore_signal(barrier, inc=1, device_id=where, device_id_type=MESH)
    pl.semaphore_wait(barrier, len(partners))


def own_place():
    bucket, dp, seq = (lax.axis_index(name) for name in ("bucket", "dp", "seq"))
    far = lax.rem(seq + 2, 4)
    twin = seq + 1 - 2 * lax.rem(seq, 2)
    return bucket, dp, seq, far, twin


class Spread:
    def __init__(self, ins, outs, whole, sems, own_sem):
        self.ins, self.outs, self.whole = ins, outs, whole
        self.sems, self.own_sem = sems, own_sem
        self.bucket, self.dp, self.seq, self.far, twin = own_place()
        self.to_bucket, self.to_far, self.to_twin = (
            {"bucket": 1 - self.bucket},
            {"seq": self.far},
            {"seq": twin},
        )
        self.to_dp = [None] + [{"dp": lax.rem(self.dp + k, 4)} for k in (1, 2, 3)]
        self.partners = [self.to_bucket, self.to_far, self.to_twin] + self.to_dp[1:]
        self.arrays = range(len(ins))

    def place(self, a, j, own_bucket, own_far, half=None):
        rows = self.ins[a].shape[0] // (8 if self.whole[a] else 1)
        slot = (
            lax.rem(self.dp + 4 - j, 4) * 8
            + (self.bucket if own_bucket else 1 - self.bucket) * 4
            + (self.seq if own_far else self.far)
        )
        cut = self.outs[a].at[pl.ds(pl.multiple_of(slot * rows, 8), rows)]
        if half is None:
            return cut
        columns = self.outs[a].shape[1]
        mid = columns // 256 * 128
        return cut.at[:, pl.ds(0, mid)] if half == 0 else cut.at[:, pl.ds(mid, columns - mid)]

    def own(self, a):
        if not self.whole[a]:
            return self.ins[a]
        rows = self.ins[a].shape[0] // 8
        at = pl.multiple_of((self.bucket * 4 + self.seq) * rows, 8)
        return self.ins[a].at[pl.ds(at, rows)]

    def copy(self, a, kind, j):
        if kind == "dp":
            return hand_over(
                self.own(a), self.place(a, 0, True, True), self.sems, (a, j - 1), self.to_dp[j]
            )
        first, where, view = {
            "bucket": (3, self.to_bucket, (True, True)),
            "far": (7, self.to_far, (True, True)),
            "twin": (11, self.to_twin, (True, True)),
            "corner_far": (15, self.to_far, (False, True, 0)),
            "corner_bucket": (19, self.to_bucket, (True, False, 1)),
            "twin_bucket": (23, self.to_twin, (False, True)),
            "twin_far": (27, self.to_twin, (True, False)),
            "twin_corner0": (31, self.to_twin, (False, False, 0)),
            "twin_corner1": (35, self.to_twin, (False, False, 1)),
        }[kind]
        dst = self.place(a, j, *view)
        src = self.own(a) if first <= 11 and j == 0 else dst
        return hand_over(src, dst, self.sems, (a, first + j), where)

    def keep(self, a):
        return pltpu.make_async_copy(
            self.own(a), self.place(a, 0, True, True), self.own_sem.at[a]
        )

    def start(self):
        for a in self.arrays:
            for kind in ("bucket", "far"):
                self.copy(a, kind, 0).start()
            for j in (1, 3, 2):
                self.copy(a, "dp", j).start()
            self.copy(a, "twin", 0).start()
            self.keep(a).start()

    def relay(self, step):
        if step < 4:
            for a in self.arrays:
                self.copy(a, "dp", step).wait_recv()
                for kind in ("bucket", "far", "twin"):
                    self.copy(a, kind, step).start()
        j = {1: 0, 3: 1, 2: 3, 4: 2}[step]
        for a in self.arrays:
            self.copy(a, "bucket", j).wait_recv()
            self.copy(a, "corner_far", j).start()
            self.copy(a, "twin_bucket", j).start()
            self.copy(a, "far", j).wait_recv()
            self.copy(a, "corner_bucket", j).start()
            self.copy(a, "twin_far", j).start()

    def corner(self, j):
        for a in self.arrays:
            self.copy(a, "corner_far", j).wait_recv()
            self.copy(a, "twin_corner0", j).start()
            self.copy(a, "corner_bucket", j).wait_recv()
            self.copy(a, "twin_corner1", j).start()

    def arrived(self, kind):
        for a in self.arrays:
            for j in range(4):
                self.copy(a, kind, j).wait_recv()

    def sent(self):
        kinds = ("bucket", "far", "corner_far", "corner_bucket")
        last = ("twin", "twin_bucket", "twin_far", "twin_corner0", "twin_corner1")
        for a in self.arrays:
            for j in range(4):
                if j:
                    self.copy(a, "dp", j).wait_send()
                for kind in kinds + last:
                    self.copy(a, kind, j).wait_send()

    def kept(self):
        for a in self.arrays:
            self.keep(a).wait()

    def finish(self):
        for j in (0, 1, 3, 2):
            self.corner(j)
        self.kept()
        for kind in ("twin", "twin_bucket", "twin_far", "twin_corner0", "twin_corner1"):
            self.arrived(kind)
        self.sent()


class Group:
    def __init__(self, x_ref, out_ref, parts, sems, own_sem):
        bucket, dp, seq, far, twin = own_place()
        to_far, to_twin = {"seq": far}, {"seq": twin}
        rows = x_ref.shape[0] // parts

        def cut(ref, p):
            return ref.at[pl.ds(p * rows, rows)]

        self.keep = pltpu.make_async_copy(x_ref, out_ref.at[seq], own_sem)
        self.fars = [
            hand_over(cut(x_ref, p), cut(out_ref.at[seq], p), sems, p, to_far)
            for p in range(parts)
        ]
        self.twins = hand_over(x_ref, out_ref.at[seq], sems, parts, to_twin)
        self.relays = [
            hand_over(cut(out_ref.at[far], p), cut(out_ref.at[far], p), sems, parts + 1 + p, to_twin)
            for p in range(parts)
        ]

    def start(self):
        for copy in self.fars:
            copy.start()
        self.twins.start()
        self.keep.start()

    def finish(self):
        for far, relay in zip(self.fars, self.relays):
            far.wait_recv()
            relay.start()
        self.keep.wait()
        self.twins.wait()
        for far, relay in zip(self.fars, self.relays):
            far.wait_send()
            relay.wait()


def opening_kernel(
    cond_ref,
    ada_ref,
    bias_ref,
    patches_ref,
    grad_ref,
    qkv_ref,
    small_ref,
    modul_ref,
    patches_out,
    grad_out,
    qkv_out,
    small_out,
    cond_in,
    part,
    part_in,
    send_sem,
    recv_sem,
    own_sem,
    side_send,
    side_recv,
    side_own,
    mod_send,
    mod_recv,
):
    bucket, dp, seq, far, twin = own_place()
    spread = Spread(
        (qkv_ref, small_ref), (qkv_out, small_out), (True, True), (send_sem, recv_sem), own_sem
    )
    sides = [
        Group(ref, out, 2, (side_send.at[i], side_recv.at[i]), side_own.at[i])
        for i, (ref, out) in enumerate(((patches_ref, patches_out), (grad_ref, grad_out)))
    ]
    greet(spread.partners)
    mods = (mod_send, mod_recv)
    conds = [
        hand_over(cond_ref.at[lax.rem(dp + k, 4)], cond_in.at[k - 1], mods, (0, k - 1), spread.to_dp[k])
        for k in (1, 2, 3)
    ]
    for copy in conds:
        copy.start()
    sides[0].start()
    spread.start()
    sides[1].start()
    for copy in conds:
        copy.wait_recv()
    images = cond_ref.shape[1]
    width = ada_ref.shape[1]
    chunk = width // 4
    for k in range(4):
        rows = cond_ref[dp] if k == 0 else cond_in[k - 1]
        for c in range(4):
            here = pl.ds(c * chunk, chunk)
            share = jnp.dot(
                rows.astype(jnp.bfloat16), ada_ref[:, here], preferred_element_type=jnp.float32
            )
            part[k, :, here] = share
        at = pl.ds(pl.multiple_of(dp * chunk, 128), chunk)
        part[k, :, at] = part[k, :, at] + bias_ref[...]
    shares = [
        hand_over(part.at[k], part_in.at[k - 1], mods, (1, k - 1), spread.to_dp[4 - k])
        for k in (1, 2, 3)
    ]
    for copy in shares:
        copy.start()
    spread.relay(1)
    spread.relay(3)
    for copy in shares:
        copy.wait_recv()
    modul_ref[...] = part[0] + part_in[0] + part_in[1] + part_in[2]
    spread.relay(2)
    spread.relay(4)
    sides[0].finish()
    spread.finish()
    sides[1].finish()
    for copy in conds + shares:
        copy.wait_send()


def opening(cond_cols, ada_weight, bias, patches, out_grad, qkv_weight, small, number):
    _, images, columns = cond_cols.shape
    width = ada_weight.shape[1]
    anywhere = pl.BlockSpec(memory_space=pl.ANY)
    inside = pl.BlockSpec(memory_space=pltpu.VMEM)
    dma = pltpu.SemaphoreType.DMA
    return pl.pallas_call(
        opening_kernel,
        out_shape=(
            jax.ShapeDtypeStruct((images, width), jnp.float32),
            jax.ShapeDtypeStruct((4,) + patches.shape, patches.dtype),
            jax.ShapeDtypeStruct((4,) + out_grad.shape, out_grad.dtype),
            jax.ShapeDtypeStruct((4 * qkv_weight.shape[0], qkv_weight.shape[1]), qkv_weight.dtype),
            jax.ShapeDtypeStruct((4 * small.shape[0], small.shape[1]), small.dtype),
        ),
        in_specs=[inside] * 3 + [anywhere] * 4,
        out_specs=(inside,) + (anywhere,) * 4,
        scratch_shapes=[
            pltpu.VMEM((3, images, columns), jnp.float32),
            pltpu.VMEM((4, images, width), jnp.float32),
            pltpu.VMEM((3, images, width), jnp.float32),
            dma((2, 39)),
            dma((2, 39)),
            dma((2,)),
            dma((2, 5)),
            dma((2, 5)),
            dma((2,)),
            dma((2, 3)),
            dma((2, 3)),
        ],
        compiler_params=pltpu.CompilerParams(
            collective_id=number, has_side_effects=True, vmem_limit_bytes=16 * 2**20
        ),
    )(cond_cols, ada_weight, bias, patches, out_grad, qkv_weight, small)


def bent_parts(inputs):
    square = inputs * inputs
    bent = jnp.tanh(gelu_coef * (inputs + cube_coef * square * inputs))
    half = 0.5 * (1.0 + bent)
    slope = half + 0.5 * inputs * (1.0 - bent * bent) * gelu_coef * (1.0 + 3.0 * cube_coef * square)
    return half * inputs, slope


def units_kernel(
    capacity,
    all_experts,
    extras_ref,
    row_ref,
    grads_ref,
    in_ref,
    out_ref,
    shared_in_ref,
    shared_out_ref,
    in_grad_ref,
    out_grad_ref,
    shared_in_grad_ref,
    shared_out_grad_ref,
    rows_ref,
    everyone,
    grads_in,
    grads_low,
    table,
    x_slots,
    g_slots,
    in_sum,
    load_sem,
    send_sem,
    recv_sem,
    own_sem,
):
    f32, bf16 = jnp.float32, jnp.bfloat16
    blocks, columns, tok_rows, width = grads_ref.shape
    block_rows = extras_ref.shape[0]
    local_experts = out_ref.shape[0]
    spread = Spread(
        (extras_ref, row_ref),
        (everyone, rows_ref),
        (False, False),
        (send_sem, recv_sem),
        own_sem,
    )
    bucket, dp, seq, far, twin = own_place()
    far_twin = lax.rem(twin + 2, 4)
    greet(spread.partners)
    spread.start()

    def column(step):
        at_bucket = jnp.where(
            (step == 1) | (step == 4) | (step == 5) | (step == 7), 1 - bucket, bucket
        )
        far_step = (step == 2) | (step == 4) | (step == 6) | (step == 7)
        twin_step = (step == 3) | (step >= 5)
        at_seq = jnp.where(
            twin_step, jnp.where(far_step, far_twin, twin), jnp.where(far_step, far, seq)
        )
        return at_bucket * 4 + at_seq

    def load(step, slot):
        return pltpu.make_async_copy(
            grads_ref.at[:, column(step)], grads_in.at[slot], load_sem.at[slot]
        )

    load(0, 0).start()
    in_sum[...] = jnp.zeros_like(in_sum)
    out_grad_ref[...] = jnp.zeros_like(out_grad_ref)
    shared_in_grad_ref[...] = jnp.zeros_like(shared_in_grad_ref)
    shared_out_grad_ref[...] = jnp.zeros_like(shared_out_grad_ref)
    first_expert = seq * local_experts
    slot_ids = (lax.broadcasted_iota(jnp.int32, (capacity, tok_rows), 0) + 1).astype(f32)
    for step in (1, 3, 2):
        spread.relay(step)
    spread.kept()

    @pl.loop(0, columns)
    def _(step):
        slot = lax.rem(step, 2)

        @pl.when(step + 1 < columns)
        def _():
            load(step + 1, 1 - slot).start()

        @pl.when(step == 3)
        def _():
            spread.arrived("twin")

        @pl.when(step == 5)
        def _():
            spread.arrived("twin_bucket")

        @pl.when(step == 6)
        def _():
            spread.arrived("twin_far")

        @pl.when(step == 7)
        def _():
            spread.arrived("twin_corner0")
            spread.arrived("twin_corner1")

        load(step, slot).wait()
        at_column = column(step)

        @pl.loop(0, blocks)
        def _(b):
            start = pl.multiple_of((b * columns + at_column) * block_rows, 16)
            features = everyone[pl.ds(start, tok_rows), :]
            table[...] = everyone[pl.ds(start + tok_rows, block_rows - tok_rows), :].astype(f32)
            gate_two = table[8:9, :] + table[9:10, :] + table[10:11, :]
            grads_low[...] = (grads_in[slot, b].astype(f32) * gate_two).astype(bf16)
            here = pl.ds(pl.multiple_of(b * capacity, 32), capacity)
            for e in range(local_experts):
                entry = table[pl.ds(first_expert + e, 1), :]
                gate = entry[:, tok_rows : 2 * tok_rows] + entry[:, 2 * tok_rows :]
                hit = slot_ids == entry[:, :tok_rows]
                pick = jnp.where(hit, 1.0, 0.0).astype(bf16)
                slot_gate = jnp.sum(jnp.where(hit, gate, 0.0), axis=1, keepdims=True)
                x_slots[e, here, :] = matmul_low(pick, features).astype(bf16)
                g_slots[e, here, :] = (slot_gate * matmul_low(pick, grads_low[...])).astype(bf16)
            active, slope = bent_parts(matmul_low(features, shared_in_ref[...]))
            slope = (matmul_right_t(grads_low[...], shared_out_ref[...]) * slope).astype(bf16)
            shared_in_grad_ref[...] += matmul_left_t(slope, features)
            shared_out_grad_ref[...] += matmul_left_t(active.astype(bf16), grads_low[...])

        for e in range(local_experts):
            active, slope = bent_parts(matmul_low(x_slots[e], in_ref[e]))
            slope = (matmul_right_t(g_slots[e], out_ref[e]) * slope).astype(bf16)
            out_grad_ref[e] += matmul_left_t(active.astype(bf16), g_slots[e])
            in_sum[e] += matmul_left_t(slope, x_slots[e])

        @pl.when(step == 0)
        def _():
            spread.relay(4)

        @pl.when(step == 1)
        def _():
            spread.corner(0)
            spread.corner(1)

        @pl.when(step == 2)
        def _():
            spread.corner(3)
            spread.corner(2)

    shards, _, rows, _ = in_grad_ref.shape
    for e in range(local_experts):
        for s in range(shards):
            in_grad_ref[s, e] = jnp.transpose(in_sum[e, :, s * rows : (s + 1) * rows]).astype(bf16)
    spread.sent()


def unit_gradients(
    extras, row_block, grads, in_own, out_own, shared_in_own, shared_out_own, capacity, all_experts, shards, number
):
    blocks, columns, tok_rows, width = grads.shape
    local_experts, units, _ = out_own.shape
    shared_units = shared_out_own.shape[0]
    devices = blocks * columns
    bf16, f32 = jnp.bfloat16, jnp.float32
    anywhere = pl.BlockSpec(memory_space=pl.ANY)
    inside = pl.BlockSpec(memory_space=pltpu.VMEM)
    dma = pltpu.SemaphoreType.DMA
    shape = jax.ShapeDtypeStruct
    return pl.pallas_call(
        functools.partial(units_kernel, capacity, all_experts),
        out_shape=(
            shape((shards, local_experts, width // shards, units), bf16),
            shape((local_experts, units, width), f32),
            shape((shared_units, width), f32),
            shape((shared_units, width), f32),
            shape((devices * row_block.shape[0], row_block.shape[1]), f32),
        ),
        in_specs=[anywhere] * 3 + [inside] * 4,
        out_specs=(inside,) * 4 + (anywhere,),
        scratch_shapes=[
            pltpu.VMEM((devices * extras.shape[0], width), bf16),
            pltpu.VMEM((2, blocks, tok_rows, width), bf16),
            pltpu.VMEM((tok_rows, width), bf16),
            pltpu.VMEM((16, width), f32),
            pltpu.VMEM((local_experts, blocks * capacity, width), bf16),
            pltpu.VMEM((local_experts, blocks * capacity, width), bf16),
            pltpu.VMEM((local_experts, units, width), f32),
            dma((2,)),
            dma((2, 39)),
            dma((2, 39)),
            dma((2,)),
        ],
        compiler_params=pltpu.CompilerParams(
            collective_id=number, has_side_effects=True, vmem_limit_bytes=50 * 2**20
        ),
        cost_estimate=pl.CostEstimate(
            flops=70_000_000_000, bytes_accessed=40_000_000, transcendentals=4_000_000
        ),
    )(extras, row_block, grads, in_own, out_own, shared_in_own, shared_out_own)


def norm_rows(rows):
    centred = rows - jnp.mean(rows, axis=-1, keepdims=True)
    root = lax.rsqrt(jnp.mean(centred * centred, axis=-1, keepdims=True) + norm_eps)
    return centred * root, root


def half_masks(rows):
    lane = lax.broadcasted_iota(jnp.int32, (rows, 128), 1)
    return lane, (lane < 64, lane >= 64)


def forward_kernel(
    all_experts,
    bias_ref,
    patches_ref,
    rows_ref,
    qkv_ref,
    small_ref,
    routes_ref,
    hidden_ref,
    q_ref,
    kv_ref,
    mixed_ref,
    stats_ref,
    branch_ref,
    after_ref,
    gates_ref,
    extras_ref,
    stats,
):
    f32, bf16 = jnp.float32, jnp.bfloat16
    seq = lax.axis_index("seq")
    sources, tok_rows, width = patches_ref.shape

    def row(j, part):
        return rows_ref[pl.ds(j, 1), part * width : (part + 1) * width]

    def hidden_of(j):
        normed, _ = norm_rows(patches_ref[j].astype(f32))
        return (normed * (1.0 + row(j, 1)) + row(j, 0)).astype(bf16)

    @pl.loop(0, sources)
    def _(j):
        here = pl.ds(pl.multiple_of(j * tok_rows, tok_rows), tok_rows)
        kv_ref[here, :] = matmul_low(hidden_of(j), qkv_ref[:, width:]).astype(bf16)

    hidden_ref[...] = hidden_of(seq)
    q_ref[...] = matmul_low(hidden_ref[...], qkv_ref[:, :width]).astype(bf16)
    stats[...] = jnp.zeros_like(stats)
    lane, halves = half_masks(tok_rows)
    score_scale = 1.0 / math.sqrt(64)

    @pl.loop(0, HEADS // 2)
    def _(p):
        cols = pl.ds(pl.multiple_of(p * 128, 128), 128)
        value_cols = pl.ds(pl.multiple_of(width + p * 128, 128), 128)
        pair = (q_ref[:, cols].astype(f32) * score_scale).astype(bf16)
        outs = []
        for h in range(2):
            query = jnp.where(halves[h], pair, jnp.zeros_like(pair))
            scores = [
                matmul_right_t(query, kv_ref[j * tok_rows : (j + 1) * tok_rows, cols]) + bias_ref[j]
                for j in range(sources)
            ]
            top = jnp.max(scores[0], axis=-1, keepdims=True)
            for score in scores[1:]:
                top = jnp.maximum(top, jnp.max(score, axis=-1, keepdims=True))
            powers = [jnp.exp(score - top) for score in scores]
            total = jnp.sum(powers[0], axis=-1, keepdims=True)
            for power in powers[1:]:
                total = total + jnp.sum(power, axis=-1, keepdims=True)
            part = 1.0 / total
            out = jnp.zeros((tok_rows, 128), f32)
            for j in range(sources):
                out = out + matmul_low(
                    (powers[j] * part).astype(bf16),
                    kv_ref[j * tok_rows : (j + 1) * tok_rows, value_cols],
                )
            outs.append(out)
            head = 2 * p + h
            stats[...] = jnp.where(
                lane == head, top, jnp.where(lane == head + 64, part, stats[...])
            )
        mixed_ref[:, cols] = jnp.where(halves[0], outs[0], outs[1])

    stats_ref[...] = jnp.transpose(stats[...])
    branch = matmul_low(mixed_ref[...].astype(bf16), small_ref[:, :width])
    branch_ref[...] = branch
    after = patches_ref[seq].astype(f32) + row(seq, 2) * branch
    after_ref[...] = after
    normed, _ = norm_rows(after)
    hidden_two = (normed * (1.0 + row(seq, 4)) + row(seq, 3)).astype(bf16)
    extras_ref[:tok_rows, :] = hidden_two
    logits = matmul_low(hidden_two, small_ref[:, width:])
    picks = [lane == routes_ref[:, k : k + 1] for k in range(2)]
    pair = [jnp.sum(jnp.where(pick, logits, 0.0), axis=-1, keepdims=True) for pick in picks]
    pair_max = jnp.maximum(pair[0], pair[1])
    exps = [jnp.exp(value - pair_max) for value in pair]
    gates = [value / (exps[0] + exps[1]) for value in exps]
    hits = jnp.where(jnp.logical_or(picks[0], picks[1]), 1.0, 0.0)
    rows_at = lax.broadcasted_iota(jnp.int32, (tok_rows, tok_rows), 0)
    cols_at = lax.broadcasted_iota(jnp.int32, (tok_rows, tok_rows), 1)
    upto = jnp.where(cols_at <= rows_at, 1.0, 0.0).astype(bf16)
    place = matmul_low(upto, hits.astype(bf16)) * hits
    gate_table = jnp.where(picks[0], gates[0], jnp.where(picks[1], gates[1], 0.0))
    gates_ref[...] = gate_table
    high = gate_table.astype(bf16).astype(f32)
    rest = gate_table - high
    gate_two = row(seq, 5)
    first = gate_two.astype(bf16).astype(f32)
    second = (gate_two - first).astype(bf16).astype(f32)
    third = gate_two - first - second
    turned = [jnp.transpose(term)[:all_experts] for term in (place, high, rest)]
    at = lax.broadcasted_iota(jnp.int32, (8, width), 0)
    gate_rows = jnp.where(at == 0, first, jnp.where(at == 1, second, jnp.where(at == 2, third, 0.0)))
    extras_ref[tok_rows:, :] = jnp.concatenate(
        [jnp.concatenate(turned, axis=1), gate_rows], axis=0
    ).astype(bf16)


def forward_block(bias, patches_group, rows_group, qkv_full, small_full, routes, all_experts):
    sources, tok_rows, width = patches_group.shape
    f32, bf16 = jnp.float32, jnp.bfloat16
    inside = pl.BlockSpec(memory_space=pltpu.VMEM)
    shape = jax.ShapeDtypeStruct
    return pl.pallas_call(
        functools.partial(forward_kernel, all_experts),
        out_shape=(
            shape((tok_rows, width), bf16),
            shape((tok_rows, width), bf16),
            shape((sources * tok_rows, 2 * width), bf16),
            shape((tok_rows, width), f32),
            shape((128, tok_rows), f32),
            shape((tok_rows, width), f32),
            shape((tok_rows, width), f32),
            shape((tok_rows, 128), f32),
            shape((tok_rows + 16, width), bf16),
        ),
        in_specs=[pl.BlockSpec(memory_space=pltpu.SMEM)] + [inside] * 5,
        out_specs=(inside,) * 9,
        scratch_shapes=[pltpu.VMEM((tok_rows, 128), f32)],
        compiler_params=pltpu.CompilerParams(vmem_limit_bytes=40 * 2**20),
        cost_estimate=pl.CostEstimate(
            flops=12_000_000_000, bytes_accessed=12_000_000, transcendentals=4_000_000
        ),
    )(bias, patches_group, rows_group, qkv_full, small_full, routes)


def middle_kernel(
    capacity,
    all_experts,
    extras_ref,
    own_ref,
    grads_ref,
    gates_ref,
    expert_in_ref,
    expert_out_ref,
    shared_ref,
    back_ref,
    shared_val_ref,
    grad_hidden_ref,
    expert_in,
    expert_out,
    shared_in,
    shared_out,
    extras,
    features,
    grads_low,
    table,
    x_slots,
    g_slots,
    value_sum,
    row_sum,
    outgo,
    weight_sem,
    group_send,
    group_recv,
    own_sem,
    back_send,
    back_recv,
    keep_sem,
):
    f32, bf16 = jnp.float32, jnp.bfloat16
    bucket, dp, seq, far, twin = own_place()
    far_twin = lax.rem(twin + 2, 4)
    sources, tok_rows, width = grads_ref.shape
    local_experts = expert_in.shape[0]
    hidden = expert_in.shape[2]
    group = Group(extras_ref, extras, 2, (group_send, group_recv), own_sem)
    greet([{"seq": far}, {"seq": twin}, {"seq": far_twin}])
    group.start()
    loads = []
    for e in range(local_experts):
        loads.append(
            (
                pltpu.make_async_copy(expert_in_ref.at[e], expert_in.at[e], weight_sem.at[0, e]),
                pltpu.make_async_copy(expert_out_ref.at[e], expert_out.at[e], weight_sem.at[1, e]),
            )
        )
    columns = shared_in.shape[0]
    ranks, side = shared_ref.shape[0], shared_ref.shape[3]
    row_step = shared_in.shape[2]
    unit_step = shared_out.shape[2]
    shared_loads = [
        pltpu.make_async_copy(
            shared_ref.at[:, k, pl.ds(0, row_step), :], shared_in.at[k], weight_sem.at[2, k]
        )
        for k in range(columns)
    ] + [
        pltpu.make_async_copy(
            shared_ref.at[r, :, pl.ds(row_step + h * unit_step, unit_step), :],
            shared_out.at[h, pl.ds(r * columns, columns)],
            weight_sem.at[3, h * ranks + r],
        )
        for h in range(2)
        for r in range(ranks)
    ]
    for copy in shared_loads:
        copy.start()
    for pair in loads:
        for copy in pair:
            copy.start()
    for j in range(sources):
        grads_low[j] = (grads_ref[j].astype(f32) * gates_ref[j : j + 1, :]).astype(bf16)
    for copy in shared_loads:
        copy.wait()
    shared_val_ref[...] = jnp.zeros_like(shared_val_ref)
    grad_hidden_ref[...] = jnp.zeros_like(grad_hidden_ref)
    features[...] = own_ref[:tok_rows, :]

    def shared_part(k):
        grads = grads_low[seq]
        weight = shared_in[k].reshape(width, side)
        at = pl.ds(pl.multiple_of(k * (side // unit_step), 4), side // unit_step)
        lower = shared_out[0, at].reshape(side, side)
        upper = shared_out[1, at].reshape(side, side)
        active, slope = bent_parts(matmul_low(features[...], weight))
        active = active.astype(bf16)
        back = matmul_right_t(grads[:, :side], lower) + matmul_right_t(grads[:, side:], upper)
        slope = (back * slope).astype(bf16)
        shared_val_ref[:, :side] += matmul_low(active, lower)
        shared_val_ref[:, side:] += matmul_low(active, upper)
        grad_hidden_ref[...] += matmul_right_t(slope, weight)

    early = columns * 5 // 8
    pl.loop(0, early)(shared_part)
    group.finish()
    first_expert = seq * local_experts
    slot_ids = (lax.broadcasted_iota(jnp.int32, (capacity, tok_rows), 0) + 1).astype(f32)

    @pl.loop(0, sources)
    def _(j):
        table[...] = extras[j, tok_rows:, :].astype(f32)
        here = pl.ds(pl.multiple_of(j * capacity, 32), capacity)
        for e in range(local_experts):
            entry = table[pl.ds(first_expert + e, 1), :]
            gate = entry[:, tok_rows : 2 * tok_rows] + entry[:, 2 * tok_rows :]
            hit = slot_ids == entry[:, :tok_rows]
            pick = jnp.where(hit, 1.0, 0.0).astype(bf16)
            slot_gate = jnp.sum(jnp.where(hit, gate, 0.0), axis=1, keepdims=True)
            x_slots[e, here, :] = matmul_low(pick, extras[j, :tok_rows, :]).astype(bf16)
            g_slots[e, here, :] = (slot_gate * matmul_low(pick, grads_low[j])).astype(bf16)

    sends = []
    for e in range(local_experts):
        for copy in loads[e]:
            copy.wait()
        value_sum[...] = jnp.zeros_like(value_sum)
        row_sum[...] = jnp.zeros_like(row_sum)

        @pl.loop(0, hidden // width)
        def _(c):
            cols = pl.ds(pl.multiple_of(c * width, 256), width)
            active, slope = bent_parts(matmul_low(x_slots[e], expert_in[e, :, cols]))
            slope = (matmul_right_t(g_slots[e], expert_out[e, cols, :]) * slope).astype(bf16)
            value_sum[...] += matmul_low(active.astype(bf16), expert_out[e, cols, :])
            row_sum[...] += matmul_right_t(slope, expert_in[e, :, cols])

        for j in range(sources):
            here = slice(j * capacity, (j + 1) * capacity)
            outgo[e, j, :, :width] = value_sum[here].astype(bf16)
            outgo[e, j, :, width:] = row_sum[here].astype(bf16)
        for k, to in enumerate((far_twin, far, twin)):
            copy = hand_over(
                outgo.at[e, to], back_ref.at[seq, e], (back_send, back_recv), (e, k), {"seq": to}
            )
            copy.start()
            sends.append(copy)
        keep = pltpu.make_async_copy(outgo.at[e, seq], back_ref.at[seq, e], keep_sem.at[e])
        keep.start()
        sends.append(keep)

    pl.loop(early, columns)(shared_part)
    for copy in sends:
        copy.wait()


def middle(extras, grads_group, gates_group, expert_in, expert_out, shared_all, capacity, all_experts, number):
    sources, tok_rows, width = grads_group.shape
    local_experts, _, hidden = expert_in.shape
    f32, bf16 = jnp.float32, jnp.bfloat16
    ranks, columns, rows, side = shared_all.shape
    row_step = width // ranks
    unit_step = (rows - row_step) // 2
    anywhere = pl.BlockSpec(memory_space=pl.ANY)
    inside = pl.BlockSpec(memory_space=pltpu.VMEM)
    dma = pltpu.SemaphoreType.DMA
    slots = sources * capacity
    return pl.pallas_call(
        functools.partial(middle_kernel, capacity, all_experts),
        out_shape=(
            jax.ShapeDtypeStruct((sources, local_experts, capacity, 2 * width), bf16),
            jax.ShapeDtypeStruct((tok_rows, width), f32),
            jax.ShapeDtypeStruct((tok_rows, width), f32),
        ),
        in_specs=[anywhere, inside, inside, inside, anywhere, anywhere, anywhere],
        out_specs=(anywhere, inside, inside),
        scratch_shapes=[
            pltpu.VMEM(expert_in.shape, bf16),
            pltpu.VMEM(expert_out.shape, bf16),
            pltpu.VMEM((columns, ranks, row_step, side), bf16),
            pltpu.VMEM((2, ranks * columns, unit_step, side), bf16),
            pltpu.VMEM((sources,) + extras.shape, bf16),
            pltpu.VMEM((tok_rows, width), bf16),
            pltpu.VMEM((sources, tok_rows, width), bf16),
            pltpu.VMEM((16, width), f32),
            pltpu.VMEM((local_experts, slots, width), bf16),
            pltpu.VMEM((local_experts, slots, width), bf16),
            pltpu.VMEM((slots, width), f32),
            pltpu.VMEM((slots, width), f32),
            pltpu.VMEM((local_experts, sources, capacity, 2 * width), bf16),
            dma((4, 8)),
            dma((5,)),
            dma((5,)),
            dma,
            dma((local_experts, 3)),
            dma((local_experts, 3)),
            dma((local_experts,)),
        ],
        compiler_params=pltpu.CompilerParams(
            collective_id=number, has_side_effects=True, vmem_limit_bytes=58 * 2**20
        ),
        cost_estimate=pl.CostEstimate(
            flops=50_000_000_000, bytes_accessed=40_000_000, transcendentals=4_000_000
        ),
    )(extras, extras, grads_group, gates_group, expert_in, expert_out, shared_all)


def home_kernel(
    capacity,
    all_experts,
    extras_ref,
    gates_ref,
    back_ref,
    shared_val_ref,
    grad_hidden_ref,
    out_grad_ref,
    after_ref,
    branch_ref,
    row_ref,
    small_ref,
    block_ref,
    grad_after_ref,
    grad_branch_ref,
    grad_mixed_ref,
    sums_ref,
    router_ref,
    table,
    grad_mix,
    mixture,
    grad_hidden,
    dots,
):
    f32, bf16 = jnp.float32, jnp.bfloat16
    tok_rows, width = out_grad_ref.shape
    local_experts = back_ref.shape[1]

    def row(part):
        return row_ref[:, part * width : (part + 1) * width]

    table[...] = extras_ref[tok_rows:, :].astype(f32)
    lane = lax.broadcasted_iota(jnp.int32, (tok_rows, 128), 1)
    gates = gates_ref[...]
    slot_ids = (lax.broadcasted_iota(jnp.int32, (capacity, tok_rows), 0) + 1).astype(f32)
    grad_block = out_grad_ref[...].astype(f32)
    grad_mix[...] = grad_block * row(5)
    mixture[...] = shared_val_ref[...]
    grad_hidden[...] = grad_hidden_ref[...]
    dots[...] = jnp.zeros_like(dots)

    @pl.loop(0, all_experts)
    def _(e):
        pick = jnp.where(slot_ids == table[pl.ds(e, 1), :tok_rows], 1.0, 0.0).astype(bf16)
        got = back_ref[e // local_experts, lax.rem(e, local_experts)]
        value = matmul_left_t(pick, got[:, :width])
        gate = jnp.sum(jnp.where(lane == e, gates, 0.0), axis=-1, keepdims=True)
        mixture[...] += gate * value
        dot = jnp.sum(grad_mix[...] * value, axis=-1, keepdims=True)
        dots[...] = jnp.where(lane == e, dot, dots[...])
        grad_hidden[...] += matmul_left_t(pick, got[:, width:])

    both = jnp.sum(gates * dots[...], axis=-1, keepdims=True)
    grad_logits = (gates * (dots[...] - both)).astype(bf16)
    hidden_two = extras_ref[:tok_rows, :]
    router_ref[...] = matmul_left_t(grad_logits, hidden_two)
    grads = grad_hidden[...] + matmul_right_t(grad_logits, small_ref[:, width:])
    after = after_ref[...]
    block_ref[...] = (after + row(5) * mixture[...]).astype(bf16)
    normed, root = norm_rows(after)
    grad_after = grad_block + norm_back(grads * (1.0 + row(4)), normed, root)
    grad_after_ref[...] = grad_after
    grad_branch = (grad_after * row(2)).astype(bf16)
    grad_branch_ref[...] = grad_branch
    grad_mixed_ref[...] = matmul_right_t(grad_branch, small_ref[:, :width]).astype(bf16)
    sums_ref[...] = jnp.zeros_like(sums_ref)
    for at, term in enumerate(
        (
            grad_after * branch_ref[...],
            grads,
            grads * normed,
            grad_block * mixture[...],
        )
    ):
        sums_ref[at : at + 1, :] = jnp.sum(term, axis=0, keepdims=True)


def home(extras, gates, back, shared_val, grad_hidden, out_grad, after, branch, row, small_full, all_experts):
    tok_rows, width = out_grad.shape
    f32, bf16 = jnp.float32, jnp.bfloat16
    inside = pl.BlockSpec(memory_space=pltpu.VMEM)
    shape = jax.ShapeDtypeStruct
    return pl.pallas_call(
        functools.partial(home_kernel, back.shape[2], all_experts),
        out_shape=(
            shape((tok_rows, width), bf16),
            shape((tok_rows, width), f32),
            shape((tok_rows, width), bf16),
            shape((tok_rows, width), bf16),
            shape((8, width), f32),
            shape((128, width), f32),
        ),
        in_specs=[inside] * 10,
        out_specs=(inside,) * 6,
        scratch_shapes=[
            pltpu.VMEM((16, width), f32),
            pltpu.VMEM((tok_rows, width), f32),
            pltpu.VMEM((tok_rows, width), f32),
            pltpu.VMEM((tok_rows, width), f32),
            pltpu.VMEM((tok_rows, 128), f32),
        ],
        compiler_params=pltpu.CompilerParams(vmem_limit_bytes=32 * 2**20),
        cost_estimate=pl.CostEstimate(
            flops=10_000_000_000, bytes_accessed=12_000_000, transcendentals=10_000
        ),
    )(extras, gates, back, shared_val, grad_hidden, out_grad, after, branch, row, small_full)


def last_kernel(
    parts,
    bias_ref,
    q_ref,
    kv_ref,
    grad_ref,
    mixed_ref,
    stats_ref,
    hidden_ref,
    grad_branch_ref,
    grad_after_ref,
    patches_ref,
    row_ref,
    qkv_ref,
    dense_ref,
    patch_grad_ref,
    sums_ref,
    dots,
    dq_sum,
    dkv,
    from_twin,
    outgo,
    from_far,
    grad_project,
    send_sem,
    recv_sem,
):
    f32, bf16 = jnp.float32, jnp.bfloat16
    bucket, dp, seq, far, twin = own_place()
    far_twin = lax.rem(twin + 2, 4)
    to_far, to_twin = {"seq": far}, {"seq": twin}
    greet([to_far, to_twin])
    sems = (send_sem, recv_sem)
    tok_rows, width = q_ref.shape
    sources = kv_ref.shape[0] // tok_rows
    rows = tok_rows // parts

    def cut(ref, p):
        return ref.at[pl.ds(p * rows, rows)]

    first = [
        hand_over(cut(dkv.at[far_twin], p), cut(from_twin.at[0], p), sems, p, to_twin)
        for p in range(parts)
    ]
    second = hand_over(dkv.at[twin], from_twin.at[1], sems, parts, to_twin)
    third = [
        hand_over(cut(outgo, p), cut(from_far, p), sems, parts + 1 + p, to_far)
        for p in range(parts)
    ]
    score_scale = 1.0 / math.sqrt(64)
    lane, halves = half_masks(tok_rows)
    head_of = lax.broadcasted_iota(jnp.int32, (128, width), 1) // 64
    chosen = (head_of == lax.broadcasted_iota(jnp.int32, (128, width), 0)).astype(f32)
    dots[...] = lax.dot_general(
        chosen,
        mixed_ref[...] * grad_ref[...].astype(f32),
        (((1,), (1,)), ((), ())),
        precision=highest,
        preferred_element_type=f32,
    )
    dq_sum[...] = jnp.zeros_like(dq_sum)

    @pl.loop(0, sources)
    def _(step):
        j = jnp.where(
            step == 0, far_twin, jnp.where(step == 1, far, jnp.where(step == 2, twin, seq))
        )
        here = pl.ds(pl.multiple_of(j * tok_rows, tok_rows), tok_rows)

        @pl.loop(0, HEADS // 2)
        def _(p):
            cols = pl.ds(pl.multiple_of(p * 128, 128), 128)
            value_cols = pl.ds(pl.multiple_of(width + p * 128, 128), 128)
            queries = (q_ref[:, cols].astype(f32) * score_scale).astype(bf16)
            grads = grad_ref[:, cols]
            keys, values = kv_ref[here, cols], kv_ref[here, value_cols]
            grad_keys = jnp.zeros((tok_rows, 128), f32)
            grad_values = jnp.zeros((tok_rows, 128), f32)
            grad_queries = jnp.zeros((tok_rows, 128), f32)
            for h in range(2):
                head = 2 * p + h
                query = jnp.where(halves[h], queries, jnp.zeros_like(queries))
                grad = jnp.where(halves[h], grads, jnp.zeros_like(grads))
                scores = matmul_right_t(keys, query) + bias_ref[j]
                probs = jnp.exp(scores - stats_ref[pl.ds(head, 1), :]) * stats_ref[pl.ds(head + 64, 1), :]
                back = probs * (matmul_right_t(values, grad) - dots[pl.ds(head, 1), :])
                back = back.astype(bf16)
                grad_keys = grad_keys + matmul_low(back, query)
                grad_values = grad_values + matmul_low(probs.astype(bf16), grad)
                grad_queries = grad_queries + jnp.where(halves[h], matmul_left_t(back, keys), 0.0)
            dkv[j, :, cols] = grad_keys.astype(bf16)
            dkv[j, :, value_cols] = grad_values.astype(bf16)
            dq_sum[:, cols] += grad_queries

        @pl.when(step == 0)
        def _():
            for copy in first:
                copy.start()

        @pl.when(step == 1)
        def _():
            for p in range(parts):
                first[p].wait_recv()
                cuts = pl.ds(p * rows, rows)
                outgo[cuts] = (
                    dkv[far, cuts].astype(f32) + from_twin[0, cuts].astype(f32)
                ).astype(bf16)
                third[p].start()

        @pl.when(step == 2)
        def _():
            second.start()

    grad_project[:, :width] = (dq_sum[...] * score_scale).astype(bf16)
    dense_ref[:, 3 * width :] = matmul_left_t(
        mixed_ref[...].astype(bf16), grad_branch_ref[...]
    ).astype(bf16)
    dense_ref[:, :width] = matmul_left_t(hidden_ref[...], grad_project[:, :width]).astype(bf16)
    second.wait_recv()
    for p in range(parts):
        cuts = pl.ds(p * rows, rows)
        third[p].wait_recv()
        grad_project[cuts, width:] = (
            dkv[seq, cuts].astype(f32)
            + from_twin[1, cuts].astype(f32)
            + from_far[cuts].astype(f32)
        ).astype(bf16)
    dense_ref[:, width : 3 * width] = matmul_left_t(
        hidden_ref[...], grad_project[:, width:]
    ).astype(bf16)
    grads = matmul_right_t(grad_project[...], qkv_ref[...])
    normed, root = norm_rows(patches_ref[...].astype(f32))
    patch_grad_ref[...] = grad_after_ref[...] + norm_back(
        grads * (1.0 + row_ref[:, width : 2 * width]), normed, root
    )
    sums_ref[...] = jnp.zeros_like(sums_ref)
    sums_ref[0:1, :] = jnp.sum(grads, axis=0, keepdims=True)
    sums_ref[1:2, :] = jnp.sum(grads * normed, axis=0, keepdims=True)
    second.wait_send()
    for p in range(parts):
        first[p].wait_send()
        third[p].wait_send()


def last_block(bias, q, kv, grad_mixed, mixed, stats, hidden, grad_branch, grad_after, patches, row, qkv_full, number, parts=4):
    tok_rows, width = q.shape
    sources = kv.shape[0] // tok_rows
    f32, bf16 = jnp.float32, jnp.bfloat16
    inside = pl.BlockSpec(memory_space=pltpu.VMEM)
    dma = pltpu.SemaphoreType.DMA
    return pl.pallas_call(
        functools.partial(last_kernel, parts),
        out_shape=(
            jax.ShapeDtypeStruct((width, 4 * width), bf16),
            jax.ShapeDtypeStruct((tok_rows, width), f32),
            jax.ShapeDtypeStruct((8, width), f32),
        ),
        in_specs=[pl.BlockSpec(memory_space=pltpu.SMEM)] + [inside] * 11,
        out_specs=(inside,) * 3,
        scratch_shapes=[
            pltpu.VMEM((128, tok_rows), f32),
            pltpu.VMEM((tok_rows, width), f32),
            pltpu.VMEM((sources, tok_rows, 2 * width), bf16),
            pltpu.VMEM((2, tok_rows, 2 * width), bf16),
            pltpu.VMEM((tok_rows, 2 * width), bf16),
            pltpu.VMEM((tok_rows, 2 * width), bf16),
            pltpu.VMEM((tok_rows, 3 * width), bf16),
            dma((2 * parts + 1,)),
            dma((2 * parts + 1,)),
        ],
        compiler_params=pltpu.CompilerParams(
            collective_id=number, has_side_effects=True, vmem_limit_bytes=44 * 2**20
        ),
        cost_estimate=pl.CostEstimate(
            flops=30_000_000_000, bytes_accessed=20_000_000, transcendentals=4_000_000
        ),
    )(bias, q, kv, grad_mixed, mixed, stats, hidden, grad_branch, grad_after, patches, row, qkv_full)


def body_general(
    patches,
    conditioning,
    image_slot,
    routes,
    ada_weight,
    ada_bias,
    qkv_weight,
    out_weight,
    router_weight,
    shared_in,
    shared_out,
    expert_in,
    expert_out,
    out_grad,
):
    seq_count = lax.axis_size("seq")
    seq_place = lax.axis_index("seq")
    outer_count = lax.axis_size(("bucket", "dp"))
    tok_rows = patches.shape[0]
    width = patches.shape[1]
    images = conditioning.shape[0]
    local_experts = expert_in.shape[0]
    all_experts = local_experts * seq_count
    capacity = 3 * tok_rows // all_experts
    head_dim = width // HEADS
    score_scale = 1.0 / math.sqrt(head_dim)
    dense = (
        lax.all_gather(ada_weight, "dp", axis=0, tiled=True),
        lax.all_gather(ada_bias, "dp", axis=0, tiled=True),
        lax.all_gather(qkv_weight, "dp", axis=0, tiled=True),
        lax.all_gather(out_weight, "dp", axis=0, tiled=True),
        lax.all_gather(router_weight, "dp", axis=0, tiled=True),
        lax.all_gather(shared_in, "dp", axis=0, tiled=True),
        lax.all_gather(shared_out, "dp", axis=0, tiled=True),
    )
    ada_full, bias_full, qkv_full, proj_full, router_full, inner_full, outer_full = dense
    cond_float = conditioning.astype(jnp.float32)
    cond_act = silu_curve(cond_float).astype(jnp.bfloat16)
    modul = matmul_low(cond_act, ada_full) + bias_full.astype(jnp.float32)
    own_slots = lax.dynamic_slice_in_dim(image_slot, seq_place * tok_rows, tok_rows)
    image_ids = jnp.arange(images, dtype=jnp.int32)
    onehot = (own_slots[:, None] == image_ids[None, :]).astype(jnp.float32)
    per_row = jnp.dot(onehot, modul, precision=highest)
    shift_one, scale_one, gate_one, shift_two, scale_two, gate_two = jnp.split(per_row, 6, axis=1)
    rows_float = patches.astype(jnp.float32)
    hidden_one_f, norm_one_pull = jax.vjp(modulate, rows_float, scale_one, shift_one)
    hidden_one = hidden_one_f.astype(jnp.bfloat16)
    project = matmul_low(hidden_one, qkv_full).astype(jnp.bfloat16)
    queries_heads = project[:, :width].reshape(tok_rows, HEADS, head_dim)
    key_value = project[:, width:]
    kv_all = lax.all_gather(key_value, "seq", axis=0, tiled=True)
    group_rows = kv_all.shape[0]
    keys_all = kv_all[:, :width].reshape(group_rows, HEADS, head_dim)
    values_all = kv_all[:, width:].reshape(group_rows, HEADS, head_dim)
    scores = (
        jnp.einsum("qhd,khd->hqk", queries_heads, keys_all, preferred_element_type=jnp.float32)
        * score_scale
    )
    same_image = own_slots[:, None] == image_slot[None, :]
    scores = jnp.where(same_image[None, :, :], scores, -1e30)
    row_max = jnp.max(scores, axis=-1, keepdims=True)
    exp_scores = jnp.exp(scores - row_max)
    probs = exp_scores / jnp.sum(exp_scores, axis=-1, keepdims=True)
    probs_low = probs.astype(jnp.bfloat16)
    mixed = (
        jnp.einsum("hqk,khd->qhd", probs_low, values_all, preferred_element_type=jnp.float32)
        .reshape(tok_rows, width)
        .astype(jnp.bfloat16)
    )
    branch = matmul_low(mixed, proj_full)
    after = rows_float + gate_one * branch
    hidden_two_f, norm_two_pull = jax.vjp(modulate, after, scale_two, shift_two)
    hidden_two = hidden_two_f.astype(jnp.bfloat16)
    shared_inner = matmul_low(hidden_two, inner_full)
    shared_act = gelu_curve(shared_inner).astype(jnp.bfloat16)
    shared_val = matmul_low(shared_act, outer_full)
    logits = matmul_low(hidden_two, router_full)
    expert_ids = jnp.arange(all_experts, dtype=jnp.int32)
    pick_zero = (routes[:, 0:1] == expert_ids[None, :]).astype(jnp.float32)
    pick_one = (routes[:, 1:2] == expert_ids[None, :]).astype(jnp.float32)
    pair = jnp.stack(
        [jnp.sum(logits * pick_zero, axis=1), jnp.sum(logits * pick_one, axis=1)], axis=1
    )
    pair_max = jnp.max(pair, axis=1, keepdims=True)
    pair_exp = jnp.exp(pair - pair_max)
    gates = pair_exp / jnp.sum(pair_exp, axis=1, keepdims=True)
    flat_routes = routes.reshape(-1)
    pair_hits = (flat_routes[:, None] == expert_ids[None, :]).astype(jnp.int32)
    running = jnp.cumsum(pair_hits, axis=0)
    place = jnp.sum(running * pair_hits, axis=1) - 1
    slot_of = flat_routes * capacity + place
    slot_ids = jnp.arange(all_experts * capacity, dtype=jnp.int32)
    spread = (slot_ids[:, None] == slot_of[None, :]).astype(jnp.bfloat16)
    spread_pairs = spread.reshape(all_experts * capacity, tok_rows, 2)
    dispatch_mat = spread_pairs[:, :, 0] + spread_pairs[:, :, 1]
    send = (
        matmul_low(dispatch_mat, hidden_two)
        .astype(jnp.bfloat16)
        .reshape(seq_count, local_experts, capacity, width)
    )
    inner = jnp.einsum(
        "secd,edf->secf",
        lax.all_to_all(send, "seq", split_axis=0, concat_axis=0, tiled=True),
        expert_in,
        preferred_element_type=jnp.float32,
    )
    active = gelu_curve(inner).astype(jnp.bfloat16)
    result = jnp.einsum(
        "secf,efd->secd", active, expert_out, preferred_element_type=jnp.float32
    ).astype(jnp.bfloat16)
    returned = lax.all_to_all(result, "seq", split_axis=0, concat_axis=0, tiled=True)
    slot_values = returned.reshape(all_experts * capacity, width)
    picked_zero = matmul_left_t(spread_pairs[:, :, 0], slot_values)
    picked_one = matmul_left_t(spread_pairs[:, :, 1], slot_values)
    mixture = shared_val + gates[:, 0:1] * picked_zero + gates[:, 1:2] * picked_one
    block_out = (after + gate_two * mixture).astype(jnp.bfloat16)
    grad_block = out_grad.astype(jnp.float32)
    grad_gate_two = grad_block * mixture
    grad_mix = grad_block * gate_two
    back_dense = (
        lax.all_gather(ada_weight, "dp", axis=0, tiled=True),
        lax.all_gather(qkv_weight, "dp", axis=0, tiled=True),
        lax.all_gather(out_weight, "dp", axis=0, tiled=True),
        lax.all_gather(router_weight, "dp", axis=0, tiled=True),
        lax.all_gather(shared_in, "dp", axis=0, tiled=True),
        lax.all_gather(shared_out, "dp", axis=0, tiled=True),
    )
    ada_back, qkv_back, proj_back, router_back, inner_back, outer_back = back_dense
    grad_shared = grad_mix.astype(jnp.bfloat16)
    grad_shared_act = matmul_right_t(grad_shared, outer_back)
    grad_shared_inner = (grad_shared_act * gelu_slope(shared_inner)).astype(jnp.bfloat16)
    grad_outer_w = matmul_left_t(shared_act, grad_shared)
    grad_inner_w = matmul_left_t(hidden_two, grad_shared_inner)
    grad_hidden = matmul_right_t(grad_shared_inner, inner_back)
    grad_gates = jnp.stack(
        [jnp.sum(grad_mix * picked_zero, axis=1), jnp.sum(grad_mix * picked_one, axis=1)], axis=1
    )
    grad_pair = gates * (grad_gates - jnp.sum(gates * grad_gates, axis=1, keepdims=True))
    grad_logits = (grad_pair[:, 0:1] * pick_zero + grad_pair[:, 1:2] * pick_one).astype(
        jnp.bfloat16
    )
    grad_router_w = matmul_left_t(hidden_two, grad_logits)
    grad_hidden = grad_hidden + matmul_right_t(grad_logits, router_back)
    grad_pairs = (
        jnp.stack([gates[:, 0:1] * grad_mix, gates[:, 1:2] * grad_mix], axis=1)
        .reshape(2 * tok_rows, width)
        .astype(jnp.bfloat16)
    )
    grad_send = (
        matmul_low(spread, grad_pairs)
        .astype(jnp.bfloat16)
        .reshape(seq_count, local_experts, capacity, width)
    )
    inputs_in = lax.all_to_all(send, "seq", split_axis=0, concat_axis=0, tiled=True)
    grads_in = lax.all_to_all(grad_send, "seq", split_axis=0, concat_axis=0, tiled=True)
    inner = jnp.einsum("secd,edf->secf", inputs_in, expert_in, preferred_element_type=jnp.float32)
    active = gelu_curve(inner).astype(jnp.bfloat16)
    grad_act = jnp.einsum(
        "secd,efd->secf", grads_in, expert_out, preferred_element_type=jnp.float32
    )
    grad_inner = (grad_act * gelu_slope(inner)).astype(jnp.bfloat16)
    grad_rows = jnp.einsum(
        "secf,edf->secd", grad_inner, expert_in, preferred_element_type=jnp.float32
    ).astype(jnp.bfloat16)
    sent_back = lax.all_to_all(grad_rows, "seq", split_axis=0, concat_axis=0, tiled=True)
    grad_expert_in = jnp.einsum(
        "secd,secf->edf", inputs_in, grad_inner, preferred_element_type=jnp.float32
    )
    grad_expert_out = jnp.einsum(
        "secf,secd->efd", active, grads_in, preferred_element_type=jnp.float32
    )
    grad_hidden = grad_hidden + matmul_left_t(
        dispatch_mat, sent_back.reshape(all_experts * capacity, width)
    )
    grad_after_norm, grad_scale_two, grad_shift_two = norm_two_pull(grad_hidden)
    grad_after = grad_block + grad_after_norm
    grad_gate_one = grad_after * branch
    grad_branch = (grad_after * gate_one).astype(jnp.bfloat16)
    grad_proj_w = matmul_left_t(mixed, grad_branch)
    grad_mixed = matmul_right_t(grad_branch, proj_back).astype(jnp.bfloat16)
    grad_mixed_heads = grad_mixed.reshape(tok_rows, HEADS, head_dim)
    grad_probs = jnp.einsum(
        "qhd,khd->hqk", grad_mixed_heads, values_all, preferred_element_type=jnp.float32
    )
    row_dot = jnp.sum(probs * grad_probs, axis=-1, keepdims=True)
    grad_scores = (probs * (grad_probs - row_dot)).astype(jnp.bfloat16)
    grad_queries = (
        jnp.einsum("hqk,khd->qhd", grad_scores, keys_all, preferred_element_type=jnp.float32)
        * score_scale
    )
    grad_keys = (
        jnp.einsum("hqk,qhd->khd", grad_scores, queries_heads, preferred_element_type=jnp.float32)
        * score_scale
    )
    grad_values = jnp.einsum(
        "hqk,qhd->khd", probs_low, grad_mixed_heads, preferred_element_type=jnp.float32
    )
    grad_kv = lax.psum_scatter(
        jnp.concatenate(
            [
                grad_keys.reshape(lax.axis_size("seq") * tok_rows, width),
                grad_values.reshape(lax.axis_size("seq") * tok_rows, width),
            ],
            axis=1,
        ).astype(jnp.bfloat16),
        "seq",
        scatter_dimension=0,
        tiled=True,
    ).astype(jnp.float32)
    grad_project = jnp.concatenate([grad_queries.reshape(tok_rows, width), grad_kv], axis=1).astype(
        jnp.bfloat16
    )
    grad_qkv_w = matmul_left_t(hidden_one, grad_project)
    grad_hidden_one = matmul_right_t(grad_project, qkv_back)
    grad_rows, grad_scale_one, grad_shift_one = norm_one_pull(grad_hidden_one)
    patch_grad = grad_after + grad_rows
    grad_per_row = jnp.concatenate(
        [
            grad_shift_one,
            grad_scale_one,
            grad_gate_one,
            grad_shift_two,
            grad_scale_two,
            grad_gate_two,
        ],
        axis=1,
    )
    grad_modul = lax.dot_general(onehot, grad_per_row, (((0,), (0,)), ((), ())), precision=highest)
    grad_ada_w = lax.dot_general(
        cond_act.astype(jnp.float32), grad_modul, (((0,), (0,)), ((), ())), precision=highest
    )
    grad_ada_b = jnp.sum(grad_modul, axis=0)
    grad_cond_part = lax.dot_general(
        grad_modul,
        ada_back,
        (((1,), (1,)), ((), ())),
        precision=highest,
        preferred_element_type=jnp.float32,
    ) * silu_slope(cond_float)
    dense_terms = (
        grad_ada_w,
        grad_ada_b,
        grad_qkv_w,
        grad_proj_w,
        grad_router_w,
        grad_inner_w,
        grad_outer_w,
    )
    ordered = tuple((order_rows(term, outer_count, seq_count) for term in dense_terms))
    first_sums = (
        lax.psum_scatter(
            grad_cond_part.astype(jnp.bfloat16), "seq", scatter_dimension=1, tiled=True
        ).astype(jnp.float32),
        lax.psum_scatter(
            ordered[0].astype(jnp.bfloat16), "seq", scatter_dimension=0, tiled=True
        ).astype(jnp.float32),
        lax.psum_scatter(
            ordered[1].astype(jnp.bfloat16), "seq", scatter_dimension=0, tiled=True
        ).astype(jnp.float32),
        lax.psum_scatter(
            ordered[2].astype(jnp.bfloat16), "seq", scatter_dimension=0, tiled=True
        ).astype(jnp.float32),
        lax.psum_scatter(
            ordered[3].astype(jnp.bfloat16), "seq", scatter_dimension=0, tiled=True
        ).astype(jnp.float32),
        lax.psum_scatter(
            ordered[4].astype(jnp.bfloat16), "seq", scatter_dimension=0, tiled=True
        ).astype(jnp.float32),
        lax.psum_scatter(
            ordered[5].astype(jnp.bfloat16), "seq", scatter_dimension=0, tiled=True
        ).astype(jnp.float32),
        lax.psum_scatter(
            ordered[6].astype(jnp.bfloat16), "seq", scatter_dimension=0, tiled=True
        ).astype(jnp.float32),
    )
    cond_grad = first_sums[0]
    second_sums = (
        lax.psum_scatter(first_sums[1], ("bucket", "dp"), scatter_dimension=0, tiled=True),
        lax.psum_scatter(first_sums[2], ("bucket", "dp"), scatter_dimension=0, tiled=True),
        lax.psum_scatter(first_sums[3], ("bucket", "dp"), scatter_dimension=0, tiled=True),
        lax.psum_scatter(first_sums[4], ("bucket", "dp"), scatter_dimension=0, tiled=True),
        lax.psum_scatter(first_sums[5], ("bucket", "dp"), scatter_dimension=0, tiled=True),
        lax.psum_scatter(first_sums[6], ("bucket", "dp"), scatter_dimension=0, tiled=True),
        lax.psum_scatter(first_sums[7], ("bucket", "dp"), scatter_dimension=0, tiled=True),
        lax.psum_scatter(grad_expert_in, ("bucket", "dp"), scatter_dimension=1, tiled=True),
        lax.psum_scatter(grad_expert_out, ("bucket", "dp"), scatter_dimension=1, tiled=True),
    )
    dense_out = second_sums[:7]
    expert_sums = second_sums[7:]
    return (
        block_out,
        patch_grad,
        cond_grad,
        dense_out[0],
        dense_out[1],
        dense_out[2],
        dense_out[3],
        dense_out[4],
        dense_out[5],
        dense_out[6],
        expert_sums[0],
        expert_sums[1],
    )


def norm_parts(rows_in):
    centred = rows_in - jnp.mean(rows_in, axis=-1, keepdims=True)
    scale = lax.rsqrt(jnp.mean(centred * centred, axis=-1, keepdims=True) + norm_eps)
    return centred * scale, scale


def norm_back(grad_normed, normed, scale):
    mean_grad = jnp.mean(grad_normed, axis=-1, keepdims=True)
    mean_prod = jnp.mean(grad_normed * normed, axis=-1, keepdims=True)
    return scale * (grad_normed - mean_grad - normed * mean_prod)


def two_parts(value):
    high = value.astype(jnp.bfloat16)
    return high, (value - high.astype(jnp.float32)).astype(jnp.bfloat16)


def body_tokens(
    patches,
    conditioning,
    image_slot,
    routes,
    ada_weight,
    ada_bias,
    qkv_weight,
    out_weight,
    router_weight,
    shared_in,
    shared_out,
    expert_in,
    expert_out,
    out_grad,
):
    bf16, f32 = jnp.bfloat16, jnp.float32
    every = ("bucket", "dp", "seq")
    outer = ("bucket", "dp")
    spare = ("bucket", "seq")
    seq_count = lax.axis_size("seq")
    dp_count = lax.axis_size("dp")
    outer_count = lax.axis_size(outer)
    spare_count = lax.axis_size(spare)
    devices = outer_count * seq_count
    seq_place = lax.axis_index("seq")
    dp_place = lax.axis_index("dp")
    outer_place = lax.axis_index(outer)
    place_all = lax.axis_index(every)
    spare_place = lax.axis_index(spare)
    tok_rows, width = patches.shape
    images = conditioning.shape[0]
    hidden = shared_in.shape[1]
    local_experts = expert_in.shape[0]
    all_experts = local_experts * seq_count
    capacity = 3 * tok_rows // all_experts
    head_dim = width // HEADS
    score_scale = 1.0 / math.sqrt(head_dim)

    def piece(weight):
        rows = weight.shape[0] // spare_count
        return lax.dynamic_slice_in_dim(weight, spare_place * rows, rows)

    turned = ("dp", "bucket", "seq")
    side = hidden // spare_count
    unit_rows = shared_out.shape[0] // spare_count
    out_piece = piece(shared_out)
    load = jnp.concatenate(
        [
            lax.dynamic_slice_in_dim(shared_in, spare_place * side, side, axis=1),
            out_piece[:, :side],
            out_piece[:, side:],
        ],
        axis=0,
    )
    shared_all = lax.all_gather(load, turned, axis=0, tiled=True).reshape(
        dp_count, spare_count, -1, side
    )
    grads_all = lax.all_gather(out_grad, turned, axis=0, tiled=True).reshape(
        dp_count, spare_count, tok_rows, width
    )

    cond_float = conditioning.astype(f32)
    cond_act = silu_curve(cond_float).astype(bf16)
    cond_cols = jnp.swapaxes(cond_act.astype(f32).reshape(images, dp_count, -1), 0, 1)
    small = jnp.concatenate(
        [out_weight, jnp.pad(router_weight, ((0, 0), (0, 128 - all_experts)))], axis=1
    )
    modul, patches_group, grads_group, qkv_full, small_full = opening(
        cond_cols,
        ada_weight,
        ada_bias.astype(f32)[None, :],
        patches,
        out_grad,
        qkv_weight,
        small,
        1,
    )
    proj_full = small_full[:, :width]
    router_full = small_full[:, width : width + all_experts]
    slots_group = image_slot.reshape(seq_count, tok_rows)[:, 0]
    slot = lax.dynamic_slice_in_dim(slots_group, seq_place, 1)[0]
    row = lax.dynamic_slice_in_dim(modul, slot, 1)
    image_ids_own = jnp.arange(images, dtype=jnp.int32)
    rows_group = jnp.sum(
        jnp.where(
            (slots_group[:, None] == image_ids_own[None, :])[:, :, None], modul[None], 0.0
        ),
        axis=1,
    )
    shift_one, scale_one, gate_one, shift_two, scale_two, gate_two = jnp.split(row, 6, axis=1)

    hidden_seen = jnp.where(slots_group == slot, 0.0, -1e30)
    hidden_one, queries, kv_all, mixed, stats, branch, after, gates, extras = forward_block(
        hidden_seen, patches_group, rows_group, qkv_full, small_full, routes, all_experts
    )
    back, shared_val, grad_hidden = middle(
        extras,
        grads_group,
        rows_group[:, 5 * width :],
        expert_in,
        expert_out,
        shared_all,
        capacity,
        all_experts,
        2,
    )
    block_out, grad_after, grad_branch, grad_mixed, sums_two, router_part = home(
        extras,
        gates,
        back,
        shared_val,
        grad_hidden,
        out_grad,
        after,
        branch,
        row,
        small_full,
        all_experts,
    )
    dense_part, patch_grad, sums_one = last_block(
        hidden_seen,
        queries,
        kv_all,
        grad_mixed,
        mixed,
        stats,
        hidden_one,
        grad_branch,
        grad_after,
        patches,
        row,
        qkv_full,
        3,
    )

    own_cols = width // devices
    dense_sum = lax.psum_scatter(dense_part, every, scatter_dimension=0, tiled=True).astype(f32)
    qkv_out = dense_sum[:, : 3 * width]
    proj_out = dense_sum[:, 3 * width :]

    tags = jnp.where(jnp.arange(128) < 1, slot.astype(f32), 0.0)[None, :]
    row_parts = jnp.concatenate(
        [
            sums_one[:2].reshape(1, 2 * width),
            sums_two[:4].reshape(1, 4 * width),
            tags,
            cond_act.astype(f32).reshape(1, images * width),
            router_part[:all_experts].reshape(1, width * all_experts),
        ],
        axis=1,
    )
    row_size = row_parts.shape[1]
    row_columns = -(-row_size // 1024) * 128
    row_block = jnp.pad(row_parts, ((0, 0), (0, 8 * row_columns - row_size))).reshape(8, row_columns)
    own_units = hidden // outer_count
    in_own = lax.dynamic_slice_in_dim(expert_in, outer_place * own_units, own_units, axis=2)
    out_own = lax.dynamic_slice_in_dim(expert_out, outer_place * own_units, own_units, axis=1)
    own_shared = hidden // devices
    first_unit = place_all * own_shared
    in_rank = shared_in.shape[0]
    shared_in_own = lax.dynamic_slice(
        shared_all, (0, first_unit // side, 0, first_unit % side), (dp_count, 1, in_rank, own_shared)
    ).reshape(width, own_shared)
    shared_out_own = lax.dynamic_slice(
        shared_all.reshape(devices, -1, side),
        (first_unit // unit_rows, in_rank, 0),
        (1, 2 * unit_rows, side),
    )
    shared_out_own = jnp.concatenate(
        [shared_out_own[0, :unit_rows], shared_out_own[0, unit_rows:]], axis=1
    )
    in_shares, expert_out_grad, shared_in_turned, shared_out_grad, row_all = unit_gradients(
        extras,
        row_block,
        grads_all,
        in_own,
        out_own,
        jnp.pad(shared_in_own, ((0, 0), (0, 128 - own_shared))),
        jnp.pad(shared_out_own, ((0, 128 - own_shared), (0, 0))),
        capacity,
        all_experts,
        outer_count,
        4,
    )
    row_all = jnp.swapaxes(
        row_all.reshape(devices, 8 * row_columns).reshape(dp_count, outer_count // dp_count, seq_count, -1), 0, 1
    ).reshape(devices, -1)
    cond_at = 6 * width + 128
    router_at = cond_at + images * width
    cond_all = row_all[::seq_count, cond_at:router_at].reshape(outer_count * images, width)
    slots_all = row_all[:, 6 * width].astype(jnp.int32)
    image_of = (jnp.arange(devices, dtype=jnp.int32) // seq_count) * images + slots_all
    image_ids = jnp.arange(outer_count * images, dtype=jnp.int32)
    gather_rows = (image_ids[:, None] == image_of[None, :]).astype(f32)
    grad_modul = jnp.dot(gather_rows, row_all[:, : 6 * width], precision=highest)
    cond_part = lax.dynamic_slice_in_dim(cond_all, place_all * own_cols, own_cols, axis=1)
    ada_out = lax.dot_general(
        cond_part.astype(f32), grad_modul, (((0,), (0,)), ((), ())), precision=highest
    )
    bias_cols = 6 * width // devices
    bias_out = lax.dynamic_slice_in_dim(jnp.sum(grad_modul, axis=0), place_all * bias_cols, bias_cols)
    router_sum = jnp.sum(
        row_all[:, router_at : router_at + width * all_experts], axis=0
    ).reshape(all_experts, width)
    router_out = jnp.transpose(
        lax.dynamic_slice_in_dim(router_sum, place_all * own_cols, own_cols, axis=1)
    )
    bucket_rows = dp_count * images
    bucket_modul = lax.dynamic_slice_in_dim(
        grad_modul, lax.axis_index("bucket") * bucket_rows, bucket_rows
    )
    cond_rows = lax.dot_general(
        bucket_modul,
        ada_weight.astype(f32),
        (((1,), (1,)), ((), ())),
        precision=highest,
        preferred_element_type=f32,
    )
    cond_back = lax.all_to_all(cond_rows, "dp", split_axis=0, concat_axis=1, tiled=True)
    cond_cols_own = width // seq_count
    cond_out = lax.dynamic_slice_in_dim(
        cond_back * silu_slope(cond_float), seq_place * cond_cols_own, cond_cols_own, axis=1
    )

    shared_out_grad = shared_out_grad[:own_shared]
    in_shares = lax.all_to_all(in_shares, outer, split_axis=0, concat_axis=0, tiled=True)
    expert_in_grad = (
        jnp.transpose(in_shares, (1, 2, 0, 3))
        .reshape(local_experts, width // outer_count, hidden)
        .astype(f32)
    )
    shared_shares = lax.all_to_all(
        jnp.transpose(
            shared_in_turned[:own_shared].astype(bf16).reshape(own_shared, devices, own_cols),
            (1, 2, 0),
        ),
        every,
        split_axis=0,
        concat_axis=0,
        tiled=True,
    )
    shared_in_grad = jnp.transpose(shared_shares, (1, 0, 2)).reshape(own_cols, hidden).astype(f32)
    return (
        block_out,
        patch_grad,
        cond_out,
        ada_out,
        bias_out,
        qkv_out,
        proj_out,
        router_out,
        shared_in_grad,
        shared_out_grad,
        expert_in_grad,
        expert_out_grad,
    )


def solution(mesh):
    in_specs = (
        P(("bucket", "dp", "seq"), None),
        P(("bucket", "dp"), None),
        P(("bucket", "dp")),
        P(("bucket", "dp", "seq"), None),
        P("dp", None),
        P("dp"),
        P("dp", None),
        P("dp", None),
        P("dp", None),
        P("dp", None),
        P("dp", None),
        P("seq", None, None),
        P("seq", None, None),
        P(("bucket", "dp", "seq"), None),
    )
    out_specs = (
        P(("bucket", "dp", "seq"), None),
        P(("bucket", "dp", "seq"), None),
        P(("bucket", "dp"), "seq"),
        P(("bucket", "dp", "seq"), None),
        P(("bucket", "dp", "seq")),
        P(("bucket", "dp", "seq"), None),
        P(("bucket", "dp", "seq"), None),
        P(("bucket", "dp", "seq"), None),
        P(("bucket", "dp", "seq"), None),
        P(("bucket", "dp", "seq"), None),
        P("seq", ("bucket", "dp"), None),
        P("seq", ("bucket", "dp"), None),
    )
    shape = tuple(mesh.shape[name] for name in ("bucket", "dp", "seq"))
    body = body_tokens if shape == (2, 4, 4) else body_general
    return jax.shard_map(body, mesh=mesh, in_specs=in_specs, out_specs=out_specs, check_vma=False)
```

```python
import functools
import math

import jax
import jax.numpy as jnp
from jax import lax
from jax.experimental import pallas as pl
from jax.experimental.pallas import tpu as pltpu
from jax.sharding import PartitionSpec as P

HEADS = 12


highest = lax.Precision.HIGHEST
norm_eps = 1e-06
gelu_coef = 0.7978845608
cube_coef = 0.044715


def sigmoid_curve(inputs):
    return 1.0 / (1.0 + jnp.exp(-inputs))


def silu_curve(inputs):
    return inputs / (1.0 + jnp.exp(-inputs))


def silu_slope(inputs):
    sigma = sigmoid_curve(inputs)
    return sigma * (1.0 + inputs * (1.0 - sigma))


def gelu_curve(inputs):
    return (
        0.5 * inputs * (1.0 + jnp.tanh(gelu_coef * (inputs + cube_coef * inputs * inputs * inputs)))
    )


def gelu_slope(inputs):
    bent = jnp.tanh(gelu_coef * (inputs + cube_coef * inputs * inputs * inputs))
    return 0.5 * (1.0 + bent) + 0.5 * inputs * (1.0 - bent * bent) * gelu_coef * (
        1.0 + 3.0 * cube_coef * inputs * inputs
    )


def modulate(rows_in, scale_in, shift_in):
    centred = rows_in - jnp.mean(rows_in, axis=-1, keepdims=True)
    normed = centred * lax.rsqrt(jnp.mean(centred * centred, axis=-1, keepdims=True) + norm_eps)
    return normed * (1.0 + scale_in) + shift_in


def matmul_low(left, right):
    return jnp.dot(left, right, preferred_element_type=jnp.float32)


def matmul_left_t(left, right):
    return lax.dot_general(
        left, right, (((0,), (0,)), ((), ())), preferred_element_type=jnp.float32
    )


def matmul_right_t(left, right):
    return lax.dot_general(
        left, right, (((1,), (1,)), ((), ())), preferred_element_type=jnp.float32
    )


def order_rows(term, outer_count, inner_count):
    rows = term.shape[0]
    rest = term.shape[1:]
    blocks = term.reshape((outer_count, inner_count, rows // (outer_count * inner_count)) + rest)
    return jnp.swapaxes(blocks, 0, 1).reshape((rows,) + rest)

MESH = pl.DeviceIdType.MESH


def hand_over(src, dst, sems, index, where):
    return pltpu.make_async_remote_copy(
        src_ref=src,
        dst_ref=dst,
        send_sem=sems[0].at[index],
        recv_sem=sems[1].at[index],
        device_id=where,
        device_id_type=MESH,
    )


def greet(partners):
    barrier = pltpu.get_barrier_semaphore()
    for where in partners:
        pl.semaphore_signal(barrier, inc=1, device_id=where, device_id_type=MESH)
    pl.semaphore_wait(barrier, len(partners))


def own_place():
    bucket, dp, seq = (lax.axis_index(name) for name in ("bucket", "dp", "seq"))
    far = lax.rem(seq + 2, 4)
    twin = seq + 1 - 2 * lax.rem(seq, 2)
    return bucket, dp, seq, far, twin


class Spread:
    def __init__(self, ins, outs, whole, sems, own_sem):
        self.ins, self.outs, self.whole = ins, outs, whole
        self.sems, self.own_sem = sems, own_sem
        self.bucket, self.dp, self.seq, self.far, twin = own_place()
        self.to_bucket, self.to_far, self.to_twin = (
            {"bucket": 1 - self.bucket},
            {"seq": self.far},
            {"seq": twin},
        )
        dp = self.dp
        self.at_dp = [dp, dp + 1 - 2 * lax.rem(dp, 2), lax.rem(dp + 2, 4), 3 - dp]
        self.to_dp = [{"dp": at} for at in self.at_dp]
        self.partners = [self.to_bucket, self.to_far, self.to_twin] + self.to_dp[1:]
        self.arrays = range(len(ins))

    def place(self, a, j, own_bucket, own_far, half=None):
        rows = self.ins[a].shape[0] // (8 if self.whole[a] else 1)
        slot = (
            self.at_dp[j] * 8
            + (self.bucket if own_bucket else 1 - self.bucket) * 4
            + (self.seq if own_far else self.far)
        )
        cut = self.outs[a].at[pl.ds(pl.multiple_of(slot * rows, 8), rows)]
        if half is None:
            return cut
        columns = self.outs[a].shape[1]
        mid = columns // 256 * 128
        return cut.at[:, pl.ds(0, mid)] if half == 0 else cut.at[:, pl.ds(mid, columns - mid)]

    def own(self, a):
        if not self.whole[a]:
            return self.ins[a]
        rows = self.ins[a].shape[0] // 8
        at = pl.multiple_of((self.bucket * 4 + self.seq) * rows, 8)
        return self.ins[a].at[pl.ds(at, rows)]

    def copy(self, a, kind, j):
        if kind == "dp":
            return hand_over(
                self.own(a), self.place(a, 0, True, True), self.sems, (a, j - 1), self.to_dp[j]
            )
        first, where, view = {
            "bucket": (3, self.to_bucket, (True, True)),
            "far": (7, self.to_far, (True, True)),
            "twin": (11, self.to_twin, (True, True)),
            "corner_far": (15, self.to_far, (False, True, 0)),
            "corner_bucket": (19, self.to_bucket, (True, False, 1)),
            "twin_bucket": (23, self.to_twin, (False, True)),
            "twin_far": (27, self.to_twin, (True, False)),
            "twin_corner0": (31, self.to_twin, (False, False, 0)),
            "twin_corner1": (35, self.to_twin, (False, False, 1)),
        }[kind]
        dst = self.place(a, j, *view)
        src = self.own(a) if first <= 11 and j == 0 else dst
        return hand_over(src, dst, self.sems, (a, first + j), where)

    def keep(self, a):
        return pltpu.make_async_copy(
            self.own(a), self.place(a, 0, True, True), self.own_sem.at[a]
        )

    def start(self):
        for a in self.arrays:
            for kind in ("bucket", "far"):
                self.copy(a, kind, 0).start()
            for j in (1, 2):
                self.copy(a, "dp", j).start()
            self.copy(a, "twin", 0).start()
            self.keep(a).start()

    def from_dp(self, j):
        for a in self.arrays:
            self.copy(a, "dp", j).wait_recv()
            for kind in ("bucket", "far", "twin"):
                self.copy(a, kind, j).start()
            if j == 1:
                self.copy(a, "dp", 3).start()

    def from_bucket(self, j):
        for a in self.arrays:
            self.copy(a, "bucket", j).wait_recv()
            self.copy(a, "corner_far", j).start()
            self.copy(a, "twin_bucket", j).start()

    def from_far(self, j):
        for a in self.arrays:
            self.copy(a, "far", j).wait_recv()
            self.copy(a, "corner_bucket", j).start()
            self.copy(a, "twin_far", j).start()

    def corner(self, j):
        for a in self.arrays:
            self.copy(a, "corner_far", j).wait_recv()
            self.copy(a, "twin_corner0", j).start()
            self.copy(a, "corner_bucket", j).wait_recv()
            self.copy(a, "twin_corner1", j).start()

    def arrived(self, kind, j):
        for a in self.arrays:
            self.copy(a, kind, j).wait_recv()

    def sent(self):
        kinds = ("bucket", "far", "corner_far", "corner_bucket")
        last = ("twin", "twin_bucket", "twin_far", "twin_corner0", "twin_corner1")
        for a in self.arrays:
            for j in range(4):
                if j:
                    self.copy(a, "dp", j).wait_send()
                for kind in kinds + last:
                    self.copy(a, kind, j).wait_send()

    def kept(self):
        for a in self.arrays:
            self.keep(a).wait()

    def first_half(self):
        self.from_dp(1)
        self.from_bucket(0)
        self.from_far(0)
        self.from_dp(2)

    def finish(self):
        self.corner(0)
        self.from_bucket(1)
        self.from_far(1)
        self.from_dp(3)
        self.from_bucket(2)
        self.from_far(2)
        self.corner(1)
        self.from_bucket(3)
        self.from_far(3)
        self.corner(2)
        self.corner(3)
        self.kept()
        for kind in ("twin", "twin_bucket", "twin_far", "twin_corner0", "twin_corner1"):
            for j in range(4):
                self.arrived(kind, j)
        self.sent()


class Group:
    def __init__(self, x_ref, out_ref, parts, sems, own_sem):
        bucket, dp, seq, far, twin = own_place()
        to_far, to_twin = {"seq": far}, {"seq": twin}
        rows = x_ref.shape[0] // parts

        def cut(ref, p):
            return ref.at[pl.ds(p * rows, rows)]

        self.keep = pltpu.make_async_copy(x_ref, out_ref.at[seq], own_sem)
        self.fars = [
            hand_over(cut(x_ref, p), cut(out_ref.at[seq], p), sems, p, to_far)
            for p in range(parts)
        ]
        self.twins = hand_over(x_ref, out_ref.at[seq], sems, parts, to_twin)
        self.relays = [
            hand_over(cut(out_ref.at[far], p), cut(out_ref.at[far], p), sems, parts + 1 + p, to_twin)
            for p in range(parts)
        ]

    def start(self):
        for copy in self.fars:
            copy.start()
        self.twins.start()
        self.keep.start()

    def finish(self):
        for far, relay in zip(self.fars, self.relays):
            far.wait_recv()
            relay.start()
        self.keep.wait()
        self.twins.wait()
        for far, relay in zip(self.fars, self.relays):
            far.wait_send()
            relay.wait()


def opening_kernel(
    cond_ref,
    ada_ref,
    bias_ref,
    patches_ref,
    qkv_ref,
    small_ref,
    modul_ref,
    patches_out,
    qkv_out,
    small_out,
    cond_in,
    stacked,
    part,
    part_in,
    send_sem,
    recv_sem,
    own_sem,
    side_send,
    side_recv,
    side_own,
    mod_send,
    mod_recv,
):
    bucket, dp, seq, far, twin = own_place()
    spread = Spread(
        (qkv_ref, small_ref), (qkv_out, small_out), (True, True), (send_sem, recv_sem), own_sem
    )
    side = Group(patches_ref, patches_out, 2, (side_send, side_recv), side_own)
    greet(spread.partners)
    mods = (mod_send, mod_recv)
    ahead = [{"dp": lax.rem(dp + k, 4)} for k in range(4)]
    conds = [
        hand_over(cond_ref.at[lax.rem(dp + k, 4)], cond_in.at[k - 1], mods, (0, k - 1), ahead[k])
        for k in (1, 2, 3)
    ]
    for copy in conds:
        copy.start()
    side.start()
    spread.start()
    for copy in conds:
        copy.wait_recv()
    images = cond_ref.shape[1]
    width = ada_ref.shape[1]
    chunk = width // 4
    stacked[:images] = cond_ref[dp]
    for k in (1, 2, 3):
        stacked[k * images : (k + 1) * images] = cond_in[k - 1]
    rows = stacked[...].astype(jnp.bfloat16)
    for c in range(4):
        here = slice(c * chunk, (c + 1) * chunk)
        share = matmul_low(rows, ada_ref[:, here])
        share = share + jnp.where(dp == c, 1.0, 0.0) * bias_ref[...]
        for k in range(4):
            part[k, :, here] = share[k * images : (k + 1) * images]
    shares = [
        hand_over(part.at[k], part_in.at[k - 1], mods, (1, k - 1), ahead[4 - k])
        for k in (1, 2, 3)
    ]
    for copy in shares:
        copy.start()
    spread.first_half()
    for copy in shares:
        copy.wait_recv()
    modul_ref[...] = part[0] + part_in[0] + part_in[1] + part_in[2]
    side.finish()
    spread.finish()
    for copy in conds + shares:
        copy.wait_send()


def opening(cond_cols, ada_weight, bias, patches, qkv_weight, small, number):
    _, images, columns = cond_cols.shape
    width = ada_weight.shape[1]
    anywhere = pl.BlockSpec(memory_space=pl.ANY)
    inside = pl.BlockSpec(memory_space=pltpu.VMEM)
    dma = pltpu.SemaphoreType.DMA
    return pl.pallas_call(
        opening_kernel,
        out_shape=(
            jax.ShapeDtypeStruct((images, width), jnp.float32),
            jax.ShapeDtypeStruct((4,) + patches.shape, patches.dtype),
            jax.ShapeDtypeStruct((4 * qkv_weight.shape[0], qkv_weight.shape[1]), qkv_weight.dtype),
            jax.ShapeDtypeStruct((4 * small.shape[0], small.shape[1]), small.dtype),
        ),
        in_specs=[inside] * 3 + [anywhere] * 3,
        out_specs=(inside,) + (anywhere,) * 3,
        scratch_shapes=[
            pltpu.VMEM((3, images, columns), jnp.float32),
            pltpu.VMEM((4 * images, columns), jnp.float32),
            pltpu.VMEM((4, images, width), jnp.float32),
            pltpu.VMEM((3, images, width), jnp.float32),
            dma((2, 39)),
            dma((2, 39)),
            dma((2,)),
            dma((5,)),
            dma((5,)),
            dma,
            dma((2, 3)),
            dma((2, 3)),
        ],
        compiler_params=pltpu.CompilerParams(
            collective_id=number, has_side_effects=True, vmem_limit_bytes=16 * 2**20
        ),
    )(cond_cols, ada_weight, bias, patches, qkv_weight, small)


def bent_parts(inputs):
    square = inputs * inputs
    bent = jnp.tanh(gelu_coef * (inputs + cube_coef * square * inputs))
    half = 0.5 * (1.0 + bent)
    slope = half + 0.5 * inputs * (1.0 - bent * bent) * gelu_coef * (1.0 + 3.0 * cube_coef * square)
    return half * inputs, slope


def units_kernel(
    capacity,
    all_experts,
    extras_ref,
    row_ref,
    grads_ref,
    expert_in_ref,
    expert_out_ref,
    shared_in_ref,
    shared_out_ref,
    in_grad_ref,
    out_grad_ref,
    shared_in_grad_ref,
    shared_out_grad_ref,
    rows_ref,
    everyone,
    in_own,
    out_own,
    grads_in,
    grads_low,
    table,
    x_slots,
    g_slots,
    in_sum,
    shared_in_sum,
    load_sem,
    weight_sem,
    send_sem,
    recv_sem,
    own_sem,
):
    f32, bf16 = jnp.float32, jnp.bfloat16
    ranks, columns, tok_rows, width = grads_ref.shape
    block_rows = extras_ref.shape[0]
    local_experts, units, _ = out_own.shape
    bucket, dp, seq, far, twin = own_place()
    far_twin = lax.rem(twin + 2, 4)
    spread = Spread(
        (extras_ref, row_ref),
        (everyone, rows_ref),
        (False, False),
        (send_sem, recv_sem),
        own_sem,
    )
    greet(spread.partners)
    spread.start()
    at_units = pl.multiple_of((bucket * 4 + dp) * units, 128)
    weights = (
        pltpu.make_async_copy(
            expert_in_ref.at[:, :, pl.ds(at_units, units)], in_own, weight_sem.at[0]
        ),
        pltpu.make_async_copy(
            expert_out_ref.at[:, pl.ds(at_units, units), :], out_own, weight_sem.at[1]
        ),
    )
    for copy in weights:
        copy.start()
    blocks = 4
    count = ranks * columns

    groups = (("near", 0), ("rest", 0), ("near", 1), ("near", 2), ("rest", 1), ("near", 3), ("rest", 2), ("rest", 3))

    def one_of(index, values):
        out = values[-1]
        for k in range(len(values) - 1):
            out = jnp.where(index == k, values[k], out)
        return out

    def place(i):
        b, group = lax.rem(i, blocks), i // blocks
        at_dp = one_of(group, [spread.at_dp[j] for _, j in groups])
        late = one_of(group, [jnp.int32(kind == "rest") for kind, _ in groups]) == 1
        near_bucket = one_of(b, [bucket, bucket, 1 - bucket, bucket])
        near_seq = one_of(b, [seq, twin, seq, far])
        rest_bucket = one_of(b, [1 - bucket, bucket, 1 - bucket, 1 - bucket])
        rest_seq = one_of(b, [twin, far_twin, far, far_twin])
        return at_dp, jnp.where(late, rest_bucket * 4 + rest_seq, near_bucket * 4 + near_seq)

    def load(i):
        at_dp, column = place(i)
        slot = lax.rem(i, 4)
        return pltpu.make_async_copy(
            grads_ref.at[at_dp, column], grads_in.at[slot], load_sem.at[slot]
        )

    for i in range(3):
        load(i).start()
    in_sum[...] = jnp.zeros_like(in_sum)
    out_grad_ref[...] = jnp.zeros_like(out_grad_ref)
    shared_in_sum[...] = jnp.zeros_like(shared_in_sum)
    shared_out_grad_ref[...] = jnp.zeros_like(shared_out_grad_ref)
    first_expert = seq * local_experts
    slot_rows = lax.broadcasted_iota(jnp.int32, (local_experts * capacity, tok_rows), 0)
    slot_ids = (lax.rem(slot_rows, capacity) + 1).astype(f32)
    second = slot_rows >= capacity
    spread.kept()
    for copy in weights:
        copy.wait()

    events = {at: [] for at in range(count)}
    for g, (kind, j) in enumerate(groups):
        at = blocks * g
        if kind == "near":
            events[at + 1].append((spread.arrived, ("twin", j)))
            events[at + 2].append((spread.from_bucket, (j,)))
            events[at + 3].append((spread.from_far, (j,)))
        else:
            events[at].append((spread.arrived, ("twin_bucket", j)))
            events[at + 1].append((spread.arrived, ("twin_far", j)))
            events[at + 3].append((spread.arrived, ("twin_corner0", j)))
            events[at + 3].append((spread.arrived, ("twin_corner1", j)))
    for at, j in ((5, 1), (8, 2), (15, 3)):
        events[at].append((spread.from_dp, (j,)))
    for at, j in ((6, 0), (16, 1), (22, 2), (28, 3)):
        events[at].append((spread.corner, (j,)))

    @pl.loop(0, count)
    def _(i):
        @pl.when(i + 3 < count)
        def _():
            load(i + 3).start()

        for at, calls in events.items():
            if not calls:
                continue

            @pl.when(i == at)
            def _():
                for call, values in calls:
                    call(*values)

        load(i).wait()
        at_dp, at_column = place(i)
        b = lax.rem(i, blocks)
        start = pl.multiple_of((at_dp * columns + at_column) * block_rows, 16)
        features = everyone[pl.ds(start, tok_rows), :]
        table[...] = everyone[pl.ds(start + tok_rows, block_rows - tok_rows), :].astype(f32)
        gate_two = table[8:9, :] + table[9:10, :] + table[10:11, :]
        grads_low[...] = (grads_in[lax.rem(i, 4)].astype(f32) * gate_two).astype(bf16)
        entries = [table[pl.ds(first_expert + e, 1), :] for e in range(2)]
        places = [entry[:, :tok_rows] for entry in entries]
        gates = [entry[:, tok_rows : 2 * tok_rows] + entry[:, 2 * tok_rows :] for entry in entries]
        hit = slot_ids == jnp.where(second, places[1], places[0])
        pick = jnp.where(hit, 1.0, 0.0).astype(bf16)
        slot_gate = jnp.sum(
            jnp.where(hit, jnp.where(second, gates[1], gates[0]), 0.0), axis=1, keepdims=True
        )
        active, slope = bent_parts(matmul_low(features, shared_in_ref[...]))
        slope = matmul_right_t(grads_low[...], shared_out_ref[...]) * slope
        from_features = matmul_low(
            jnp.concatenate([pick, jnp.transpose(slope).astype(bf16)], axis=0), features
        )
        from_grads = matmul_low(
            jnp.concatenate([pick, jnp.transpose(active).astype(bf16)], axis=0), grads_low[...]
        )
        here = pl.ds(pl.multiple_of(b * capacity, 32), capacity)
        picked = local_experts * capacity
        x_picked = from_features[:picked].astype(bf16)
        g_picked = (slot_gate * from_grads[:picked]).astype(bf16)
        for e in range(local_experts):
            x_slots[e, here, :] = x_picked[e * capacity : (e + 1) * capacity]
            g_slots[e, here, :] = g_picked[e * capacity : (e + 1) * capacity]
        shared_in_sum[...] += from_features[picked:]
        shared_out_grad_ref[...] += from_grads[picked:]

        @pl.when(b == blocks - 1)
        def _():
            for e in range(local_experts):
                act, bent = bent_parts(matmul_low(x_slots[e], in_own[e]))
                bent = (matmul_right_t(g_slots[e], out_own[e]) * bent).astype(bf16)
                out_grad_ref[e] += matmul_left_t(act.astype(bf16), g_slots[e])
                in_sum[e] += matmul_left_t(bent, x_slots[e])

    shards, _, rows, _ = in_grad_ref.shape
    for e in range(local_experts):
        for s in range(shards):
            in_grad_ref[s, e] = jnp.transpose(in_sum[e, :, s * rows : (s + 1) * rows]).astype(bf16)
    turned = jnp.transpose(shared_in_sum[...])
    pieces, unit_rows, _ = shared_in_grad_ref.shape
    for r in range(pieces):
        shared_in_grad_ref[r] = turned[r * unit_rows : (r + 1) * unit_rows]
    spread.sent()


def unit_gradients(
    extras, row_block, grads, expert_in, expert_out, shared_in_own, shared_out_own, capacity, all_experts, shards, number
):
    ranks, columns, tok_rows, width = grads.shape
    local_experts, hidden, _ = expert_out.shape
    units = hidden // shards
    shared_units = shared_out_own.shape[0]
    devices = ranks * columns
    bf16, f32 = jnp.bfloat16, jnp.float32
    anywhere = pl.BlockSpec(memory_space=pl.ANY)
    inside = pl.BlockSpec(memory_space=pltpu.VMEM)
    dma = pltpu.SemaphoreType.DMA
    shape = jax.ShapeDtypeStruct
    return pl.pallas_call(
        functools.partial(units_kernel, capacity, all_experts),
        out_shape=(
            shape((shards, local_experts, width // shards, units), bf16),
            shape((local_experts, units, width), f32),
            shape((devices, width // devices, shared_units), f32),
            shape((shared_units, width), f32),
            shape((devices * row_block.shape[0], row_block.shape[1]), f32),
        ),
        in_specs=[anywhere] * 5 + [inside] * 2,
        out_specs=(inside,) * 4 + (anywhere,),
        scratch_shapes=[
            pltpu.VMEM((devices * extras.shape[0], width), bf16),
            pltpu.VMEM((local_experts, width, units), bf16),
            pltpu.VMEM((local_experts, units, width), bf16),
            pltpu.VMEM((4, tok_rows, width), bf16),
            pltpu.VMEM((tok_rows, width), bf16),
            pltpu.VMEM((16, width), f32),
            pltpu.VMEM((local_experts, 4 * capacity, width), bf16),
            pltpu.VMEM((local_experts, 4 * capacity, width), bf16),
            pltpu.VMEM((local_experts, units, width), f32),
            pltpu.VMEM((shared_units, width), f32),
            dma((4,)),
            dma((2,)),
            dma((2, 39)),
            dma((2, 39)),
            dma((2,)),
        ],
        compiler_params=pltpu.CompilerParams(
            collective_id=number, has_side_effects=True, vmem_limit_bytes=40 * 2**20
        ),
        cost_estimate=pl.CostEstimate(
            flops=70_000_000_000, bytes_accessed=40_000_000, transcendentals=4_000_000
        ),
    )(extras, row_block, grads, expert_in, expert_out, shared_in_own, shared_out_own)


def norm_rows(rows):
    centred = rows - jnp.mean(rows, axis=-1, keepdims=True)
    root = lax.rsqrt(jnp.mean(centred * centred, axis=-1, keepdims=True) + norm_eps)
    return centred * root, root


def half_masks(rows):
    lane = lax.broadcasted_iota(jnp.int32, (rows, 128), 1)
    return lane, (lane < 64, lane >= 64)


def forward_kernel(
    all_experts,
    bias_ref,
    patches_ref,
    rows_ref,
    qkv_ref,
    small_ref,
    routes_ref,
    out_grad_ref,
    hidden_ref,
    q_ref,
    kv_ref,
    mixed_ref,
    stats_ref,
    branch_ref,
    after_ref,
    gates_ref,
    extras_ref,
    grads_ref,
    stats,
    send_sem,
    recv_sem,
    own_sem,
):
    f32, bf16 = jnp.float32, jnp.bfloat16
    bucket, dp, seq, far, twin = own_place()
    group = Group(out_grad_ref, grads_ref, 2, (send_sem, recv_sem), own_sem)
    greet([{"seq": far}, {"seq": twin}])
    group.start()
    sources, tok_rows, width = patches_ref.shape

    def row(j, part):
        return rows_ref[pl.ds(j, 1), part * width : (part + 1) * width]

    def hidden_of(j):
        normed, _ = norm_rows(patches_ref[j].astype(f32))
        return (normed * (1.0 + row(j, 1)) + row(j, 0)).astype(bf16)

    @pl.loop(0, sources)
    def _(j):
        here = pl.ds(pl.multiple_of(j * tok_rows, tok_rows), tok_rows)
        kv_ref[here, :] = matmul_low(hidden_of(j), qkv_ref[:, width:]).astype(bf16)

    hidden_ref[...] = hidden_of(seq)
    q_ref[...] = matmul_low(hidden_ref[...], qkv_ref[:, :width]).astype(bf16)
    stats[...] = jnp.zeros_like(stats)
    lane, halves = half_masks(tok_rows)
    score_scale = 1.0 / math.sqrt(64)

    @pl.loop(0, HEADS // 2)
    def _(p):
        cols = pl.ds(pl.multiple_of(p * 128, 128), 128)
        value_cols = pl.ds(pl.multiple_of(width + p * 128, 128), 128)
        pair = (q_ref[:, cols].astype(f32) * score_scale).astype(bf16)
        outs = []
        for h in range(2):
            query = jnp.where(halves[h], pair, jnp.zeros_like(pair))
            scores = [
                matmul_right_t(query, kv_ref[j * tok_rows : (j + 1) * tok_rows, cols]) + bias_ref[j]
                for j in range(sources)
            ]
            top = jnp.max(scores[0], axis=-1, keepdims=True)
            for score in scores[1:]:
                top = jnp.maximum(top, jnp.max(score, axis=-1, keepdims=True))
            powers = [jnp.exp(score - top) for score in scores]
            total = jnp.sum(powers[0], axis=-1, keepdims=True)
            for power in powers[1:]:
                total = total + jnp.sum(power, axis=-1, keepdims=True)
            part = 1.0 / total
            out = jnp.zeros((tok_rows, 128), f32)
            for j in range(sources):
                out = out + matmul_low(
                    (powers[j] * part).astype(bf16),
                    kv_ref[j * tok_rows : (j + 1) * tok_rows, value_cols],
                )
            outs.append(out)
            head = 2 * p + h
            stats[...] = jnp.where(
                lane == head, top, jnp.where(lane == head + 64, part, stats[...])
            )
        mixed_ref[:, cols] = jnp.where(halves[0], outs[0], outs[1])

    stats_ref[...] = jnp.transpose(stats[...])
    branch = matmul_low(mixed_ref[...].astype(bf16), small_ref[:, :width])
    branch_ref[...] = branch
    after = patches_ref[seq].astype(f32) + row(seq, 2) * branch
    after_ref[...] = after
    normed, _ = norm_rows(after)
    hidden_two = (normed * (1.0 + row(seq, 4)) + row(seq, 3)).astype(bf16)
    extras_ref[:tok_rows, :] = hidden_two
    logits = matmul_low(hidden_two, small_ref[:, width:])
    picks = [lane == routes_ref[:, k : k + 1] for k in range(2)]
    pair = [jnp.sum(jnp.where(pick, logits, 0.0), axis=-1, keepdims=True) for pick in picks]
    pair_max = jnp.maximum(pair[0], pair[1])
    exps = [jnp.exp(value - pair_max) for value in pair]
    gates = [value / (exps[0] + exps[1]) for value in exps]
    hits = jnp.where(jnp.logical_or(picks[0], picks[1]), 1.0, 0.0)
    rows_at = lax.broadcasted_iota(jnp.int32, (tok_rows, tok_rows), 0)
    cols_at = lax.broadcasted_iota(jnp.int32, (tok_rows, tok_rows), 1)
    upto = jnp.where(cols_at <= rows_at, 1.0, 0.0).astype(bf16)
    place = matmul_low(upto, hits.astype(bf16)) * hits
    gate_table = jnp.where(picks[0], gates[0], jnp.where(picks[1], gates[1], 0.0))
    gates_ref[...] = gate_table
    high = gate_table.astype(bf16).astype(f32)
    rest = gate_table - high
    gate_two = row(seq, 5)
    first = gate_two.astype(bf16).astype(f32)
    second = (gate_two - first).astype(bf16).astype(f32)
    third = gate_two - first - second
    turned = [jnp.transpose(term)[:all_experts] for term in (place, high, rest)]
    at = lax.broadcasted_iota(jnp.int32, (8, width), 0)
    gate_rows = jnp.where(at == 0, first, jnp.where(at == 1, second, jnp.where(at == 2, third, 0.0)))
    extras_ref[tok_rows:, :] = jnp.concatenate(
        [jnp.concatenate(turned, axis=1), gate_rows], axis=0
    ).astype(bf16)
    group.finish()


def forward_block(bias, patches_group, rows_group, qkv_full, small_full, routes, out_grad, all_experts, number):
    sources, tok_rows, width = patches_group.shape
    f32, bf16 = jnp.float32, jnp.bfloat16
    inside = pl.BlockSpec(memory_space=pltpu.VMEM)
    anywhere = pl.BlockSpec(memory_space=pl.ANY)
    shape = jax.ShapeDtypeStruct
    return pl.pallas_call(
        functools.partial(forward_kernel, all_experts),
        out_shape=(
            shape((tok_rows, width), bf16),
            shape((tok_rows, width), bf16),
            shape((sources * tok_rows, 2 * width), bf16),
            shape((tok_rows, width), f32),
            shape((128, tok_rows), f32),
            shape((tok_rows, width), f32),
            shape((tok_rows, width), f32),
            shape((tok_rows, 128), f32),
            shape((tok_rows + 16, width), bf16),
            shape((sources, tok_rows, width), bf16),
        ),
        in_specs=[pl.BlockSpec(memory_space=pltpu.SMEM)] + [inside] * 5 + [anywhere],
        out_specs=(inside,) * 9 + (anywhere,),
        scratch_shapes=[
            pltpu.VMEM((tok_rows, 128), f32),
            pltpu.SemaphoreType.DMA((5,)),
            pltpu.SemaphoreType.DMA((5,)),
            pltpu.SemaphoreType.DMA,
        ],
        compiler_params=pltpu.CompilerParams(
            collective_id=number, has_side_effects=True, vmem_limit_bytes=26 * 2**20
        ),
        cost_estimate=pl.CostEstimate(
            flops=12_000_000_000, bytes_accessed=12_000_000, transcendentals=4_000_000
        ),
    )(bias, patches_group, rows_group, qkv_full, small_full, routes, out_grad)


def middle_kernel(
    capacity,
    all_experts,
    extras_ref,
    own_ref,
    grads_ref,
    gates_ref,
    expert_in_ref,
    expert_out_ref,
    shared_ref,
    back_ref,
    shared_val_ref,
    grad_hidden_ref,
    expert_in,
    expert_out,
    shared_in,
    shared_out,
    extras,
    features,
    grads_low,
    table,
    x_slots,
    g_slots,
    value_sum,
    row_sum,
    outgo,
    weight_sem,
    group_send,
    group_recv,
    own_sem,
    back_send,
    back_recv,
    keep_sem,
):
    f32, bf16 = jnp.float32, jnp.bfloat16
    bucket, dp, seq, far, twin = own_place()
    far_twin = lax.rem(twin + 2, 4)
    sources, tok_rows, width = grads_ref.shape
    local_experts = expert_in.shape[0]
    hidden = expert_in.shape[2]
    group = Group(extras_ref, extras, 2, (group_send, group_recv), own_sem)
    greet([{"seq": far}, {"seq": twin}, {"seq": far_twin}])
    group.start()
    loads = []
    for e in range(local_experts):
        loads.append(
            (
                pltpu.make_async_copy(expert_in_ref.at[e], expert_in.at[e], weight_sem.at[0, e]),
                pltpu.make_async_copy(expert_out_ref.at[e], expert_out.at[e], weight_sem.at[1, e]),
            )
        )
    columns = shared_in.shape[0]
    ranks, side = shared_ref.shape[0], shared_ref.shape[3]
    row_step = shared_in.shape[2]
    unit_step = shared_out.shape[2]
    shared_loads = [
        pltpu.make_async_copy(
            shared_ref.at[:, k, pl.ds(0, row_step), :], shared_in.at[k], weight_sem.at[2, k]
        )
        for k in range(columns)
    ] + [
        pltpu.make_async_copy(
            shared_ref.at[r, :, pl.ds(row_step + h * unit_step, unit_step), :],
            shared_out.at[h, pl.ds(r * columns, columns)],
            weight_sem.at[3, h * ranks + r],
        )
        for h in range(2)
        for r in range(ranks)
    ]
    for copy in shared_loads:
        copy.start()
    for pair in loads:
        for copy in pair:
            copy.start()
    for j in range(sources):
        grads_low[j] = (grads_ref[j].astype(f32) * gates_ref[j : j + 1, :]).astype(bf16)
    for copy in shared_loads:
        copy.wait()
    shared_val_ref[...] = jnp.zeros_like(shared_val_ref)
    grad_hidden_ref[...] = jnp.zeros_like(grad_hidden_ref)
    features[...] = own_ref[:tok_rows, :]

    def shared_part(k):
        grads = grads_low[seq]
        weight = shared_in[k].reshape(width, side)
        at = pl.ds(pl.multiple_of(k * (side // unit_step), 4), side // unit_step)
        lower = shared_out[0, at].reshape(side, side)
        upper = shared_out[1, at].reshape(side, side)
        active, slope = bent_parts(matmul_low(features[...], weight))
        active = active.astype(bf16)
        back = matmul_right_t(grads[:, :side], lower) + matmul_right_t(grads[:, side:], upper)
        slope = (back * slope).astype(bf16)
        shared_val_ref[:, :side] += matmul_low(active, lower)
        shared_val_ref[:, side:] += matmul_low(active, upper)
        grad_hidden_ref[...] += matmul_right_t(slope, weight)

    early = columns * 5 // 8
    pl.loop(0, early)(shared_part)
    group.finish()
    first_expert = seq * local_experts
    slot_ids = (lax.broadcasted_iota(jnp.int32, (capacity, tok_rows), 0) + 1).astype(f32)

    @pl.loop(0, sources)
    def _(j):
        table[...] = extras[j, tok_rows:, :].astype(f32)
        here = pl.ds(pl.multiple_of(j * capacity, 32), capacity)
        for e in range(local_experts):
            entry = table[pl.ds(first_expert + e, 1), :]
            gate = entry[:, tok_rows : 2 * tok_rows] + entry[:, 2 * tok_rows :]
            hit = slot_ids == entry[:, :tok_rows]
            pick = jnp.where(hit, 1.0, 0.0).astype(bf16)
            slot_gate = jnp.sum(jnp.where(hit, gate, 0.0), axis=1, keepdims=True)
            x_slots[e, here, :] = matmul_low(pick, extras[j, :tok_rows, :]).astype(bf16)
            g_slots[e, here, :] = (slot_gate * matmul_low(pick, grads_low[j])).astype(bf16)

    sends = []
    for e in range(local_experts):
        for copy in loads[e]:
            copy.wait()
        value_sum[...] = jnp.zeros_like(value_sum)
        row_sum[...] = jnp.zeros_like(row_sum)

        @pl.loop(0, hidden // width)
        def _(c):
            cols = pl.ds(pl.multiple_of(c * width, 256), width)
            active, slope = bent_parts(matmul_low(x_slots[e], expert_in[e, :, cols]))
            slope = (matmul_right_t(g_slots[e], expert_out[e, cols, :]) * slope).astype(bf16)
            value_sum[...] += matmul_low(active.astype(bf16), expert_out[e, cols, :])
            row_sum[...] += matmul_right_t(slope, expert_in[e, :, cols])

        for j in range(sources):
            here = slice(j * capacity, (j + 1) * capacity)
            outgo[e, j, :, :width] = value_sum[here].astype(bf16)
            outgo[e, j, :, width:] = row_sum[here].astype(bf16)
        for k, to in enumerate((far_twin, far, twin)):
            copy = hand_over(
                outgo.at[e, to], back_ref.at[seq, e], (back_send, back_recv), (e, k), {"seq": to}
            )
            copy.start()
            sends.append(copy)
        keep = pltpu.make_async_copy(outgo.at[e, seq], back_ref.at[seq, e], keep_sem.at[e])
        keep.start()
        sends.append(keep)

    pl.loop(early, columns)(shared_part)
    for copy in sends:
        copy.wait()


def middle(extras, grads_group, gates_group, expert_in, expert_out, shared_all, capacity, all_experts, number):
    sources, tok_rows, width = grads_group.shape
    local_experts, _, hidden = expert_in.shape
    f32, bf16 = jnp.float32, jnp.bfloat16
    ranks, columns, rows, side = shared_all.shape
    row_step = width // ranks
    unit_step = (rows - row_step) // 2
    anywhere = pl.BlockSpec(memory_space=pl.ANY)
    inside = pl.BlockSpec(memory_space=pltpu.VMEM)
    dma = pltpu.SemaphoreType.DMA
    slots = sources * capacity
    return pl.pallas_call(
        functools.partial(middle_kernel, capacity, all_experts),
        out_shape=(
            jax.ShapeDtypeStruct((sources, local_experts, capacity, 2 * width), bf16),
            jax.ShapeDtypeStruct((tok_rows, width), f32),
            jax.ShapeDtypeStruct((tok_rows, width), f32),
        ),
        in_specs=[anywhere, inside, inside, inside, anywhere, anywhere, anywhere],
        out_specs=(anywhere, inside, inside),
        scratch_shapes=[
            pltpu.VMEM(expert_in.shape, bf16),
            pltpu.VMEM(expert_out.shape, bf16),
            pltpu.VMEM((columns, ranks, row_step, side), bf16),
            pltpu.VMEM((2, ranks * columns, unit_step, side), bf16),
            pltpu.VMEM((sources,) + extras.shape, bf16),
            pltpu.VMEM((tok_rows, width), bf16),
            pltpu.VMEM((sources, tok_rows, width), bf16),
            pltpu.VMEM((16, width), f32),
            pltpu.VMEM((local_experts, slots, width), bf16),
            pltpu.VMEM((local_experts, slots, width), bf16),
            pltpu.VMEM((slots, width), f32),
            pltpu.VMEM((slots, width), f32),
            pltpu.VMEM((local_experts, sources, capacity, 2 * width), bf16),
            dma((4, 8)),
            dma((5,)),
            dma((5,)),
            dma,
            dma((local_experts, 3)),
            dma((local_experts, 3)),
            dma((local_experts,)),
        ],
        compiler_params=pltpu.CompilerParams(
            collective_id=number, has_side_effects=True, vmem_limit_bytes=48 * 2**20
        ),
        cost_estimate=pl.CostEstimate(
            flops=50_000_000_000, bytes_accessed=40_000_000, transcendentals=4_000_000
        ),
    )(extras, extras, grads_group, gates_group, expert_in, expert_out, shared_all)


def home_kernel(
    capacity,
    all_experts,
    extras_ref,
    gates_ref,
    back_ref,
    shared_val_ref,
    grad_hidden_ref,
    out_grad_ref,
    after_ref,
    branch_ref,
    row_ref,
    small_ref,
    block_ref,
    grad_after_ref,
    grad_branch_ref,
    grad_mixed_ref,
    sums_ref,
    router_ref,
    table,
    grad_mix,
    mixture,
    grad_hidden,
    dots,
):
    f32, bf16 = jnp.float32, jnp.bfloat16
    tok_rows, width = out_grad_ref.shape
    local_experts = back_ref.shape[1]

    def row(part):
        return row_ref[:, part * width : (part + 1) * width]

    table[...] = extras_ref[tok_rows:, :].astype(f32)
    lane = lax.broadcasted_iota(jnp.int32, (tok_rows, 128), 1)
    gates = gates_ref[...]
    slot_ids = (lax.broadcasted_iota(jnp.int32, (capacity, tok_rows), 0) + 1).astype(f32)
    grad_block = out_grad_ref[...].astype(f32)
    grad_mix[...] = grad_block * row(5)
    mixture[...] = shared_val_ref[...]
    grad_hidden[...] = grad_hidden_ref[...]
    dots[...] = jnp.zeros_like(dots)

    @pl.loop(0, all_experts)
    def _(e):
        pick = jnp.where(slot_ids == table[pl.ds(e, 1), :tok_rows], 1.0, 0.0).astype(bf16)
        got = back_ref[e // local_experts, lax.rem(e, local_experts)]
        value = matmul_left_t(pick, got[:, :width])
        gate = jnp.sum(jnp.where(lane == e, gates, 0.0), axis=-1, keepdims=True)
        mixture[...] += gate * value
        dot = jnp.sum(grad_mix[...] * value, axis=-1, keepdims=True)
        dots[...] = jnp.where(lane == e, dot, dots[...])
        grad_hidden[...] += matmul_left_t(pick, got[:, width:])

    both = jnp.sum(gates * dots[...], axis=-1, keepdims=True)
    grad_logits = (gates * (dots[...] - both)).astype(bf16)
    hidden_two = extras_ref[:tok_rows, :]
    router_ref[...] = matmul_left_t(hidden_two, grad_logits).astype(bf16)
    grads = grad_hidden[...] + matmul_right_t(grad_logits, small_ref[:, width:])
    after = after_ref[...]
    block_ref[...] = (after + row(5) * mixture[...]).astype(bf16)
    normed, root = norm_rows(after)
    grad_after = grad_block + norm_back(grads * (1.0 + row(4)), normed, root)
    grad_after_ref[...] = grad_after
    grad_branch = (grad_after * row(2)).astype(bf16)
    grad_branch_ref[...] = grad_branch
    grad_mixed_ref[...] = matmul_right_t(grad_branch, small_ref[:, :width]).astype(bf16)
    sums_ref[...] = jnp.zeros_like(sums_ref)
    for at, term in enumerate(
        (
            grad_after * branch_ref[...],
            grads,
            grads * normed,
            grad_block * mixture[...],
        )
    ):
        sums_ref[at : at + 1, :] = jnp.sum(term, axis=0, keepdims=True)


def home(extras, gates, back, shared_val, grad_hidden, out_grad, after, branch, row, small_full, all_experts):
    tok_rows, width = out_grad.shape
    f32, bf16 = jnp.float32, jnp.bfloat16
    inside = pl.BlockSpec(memory_space=pltpu.VMEM)
    shape = jax.ShapeDtypeStruct
    return pl.pallas_call(
        functools.partial(home_kernel, back.shape[2], all_experts),
        out_shape=(
            shape((tok_rows, width), bf16),
            shape((tok_rows, width), f32),
            shape((tok_rows, width), bf16),
            shape((tok_rows, width), bf16),
            shape((8, width), f32),
            shape((width, 128), bf16),
        ),
        in_specs=[inside] * 10,
        out_specs=(inside,) * 6,
        scratch_shapes=[
            pltpu.VMEM((16, width), f32),
            pltpu.VMEM((tok_rows, width), f32),
            pltpu.VMEM((tok_rows, width), f32),
            pltpu.VMEM((tok_rows, width), f32),
            pltpu.VMEM((tok_rows, 128), f32),
        ],
        compiler_params=pltpu.CompilerParams(vmem_limit_bytes=20 * 2**20),
        cost_estimate=pl.CostEstimate(
            flops=10_000_000_000, bytes_accessed=12_000_000, transcendentals=10_000
        ),
    )(extras, gates, back, shared_val, grad_hidden, out_grad, after, branch, row, small_full)


def last_kernel(
    parts,
    bias_ref,
    q_ref,
    kv_ref,
    grad_ref,
    mixed_ref,
    stats_ref,
    hidden_ref,
    grad_branch_ref,
    grad_after_ref,
    patches_ref,
    row_ref,
    qkv_ref,
    router_ref,
    dense_ref,
    patch_grad_ref,
    sums_ref,
    dots,
    dq_sum,
    dkv,
    from_twin,
    outgo,
    from_far,
    grad_project,
    send_sem,
    recv_sem,
):
    f32, bf16 = jnp.float32, jnp.bfloat16
    bucket, dp, seq, far, twin = own_place()
    far_twin = lax.rem(twin + 2, 4)
    to_far, to_twin = {"seq": far}, {"seq": twin}
    greet([to_far, to_twin])
    sems = (send_sem, recv_sem)
    tok_rows, width = q_ref.shape
    sources = kv_ref.shape[0] // tok_rows
    rows = tok_rows // parts

    def cut(ref, p):
        return ref.at[pl.ds(p * rows, rows)]

    first = [
        hand_over(cut(dkv.at[far_twin], p), cut(from_twin.at[0], p), sems, p, to_twin)
        for p in range(parts)
    ]
    second = hand_over(dkv.at[twin], from_twin.at[1], sems, parts, to_twin)
    third = [
        hand_over(cut(outgo, p), cut(from_far, p), sems, parts + 1 + p, to_far)
        for p in range(parts)
    ]
    score_scale = 1.0 / math.sqrt(64)
    lane, halves = half_masks(tok_rows)
    head_of = lax.broadcasted_iota(jnp.int32, (128, width), 1) // 64
    chosen = (head_of == lax.broadcasted_iota(jnp.int32, (128, width), 0)).astype(f32)
    dots[...] = lax.dot_general(
        chosen,
        mixed_ref[...] * grad_ref[...].astype(f32),
        (((1,), (1,)), ((), ())),
        precision=highest,
        preferred_element_type=f32,
    )
    dq_sum[...] = jnp.zeros_like(dq_sum)

    @pl.loop(0, sources)
    def _(step):
        j = jnp.where(
            step == 0, far_twin, jnp.where(step == 1, far, jnp.where(step == 2, twin, seq))
        )
        here = pl.ds(pl.multiple_of(j * tok_rows, tok_rows), tok_rows)

        @pl.loop(0, HEADS // 2)
        def _(p):
            cols = pl.ds(pl.multiple_of(p * 128, 128), 128)
            value_cols = pl.ds(pl.multiple_of(width + p * 128, 128), 128)
            queries = (q_ref[:, cols].astype(f32) * score_scale).astype(bf16)
            grads = grad_ref[:, cols]
            keys, values = kv_ref[here, cols], kv_ref[here, value_cols]
            grad_keys = jnp.zeros((tok_rows, 128), f32)
            grad_values = jnp.zeros((tok_rows, 128), f32)
            grad_queries = jnp.zeros((tok_rows, 128), f32)
            for h in range(2):
                head = 2 * p + h
                query = jnp.where(halves[h], queries, jnp.zeros_like(queries))
                grad = jnp.where(halves[h], grads, jnp.zeros_like(grads))
                scores = matmul_right_t(keys, query) + bias_ref[j]
                probs = jnp.exp(scores - stats_ref[pl.ds(head, 1), :]) * stats_ref[pl.ds(head + 64, 1), :]
                back = probs * (matmul_right_t(values, grad) - dots[pl.ds(head, 1), :])
                back = back.astype(bf16)
                grad_keys = grad_keys + matmul_low(back, query)
                grad_values = grad_values + matmul_low(probs.astype(bf16), grad)
                grad_queries = grad_queries + jnp.where(halves[h], matmul_left_t(back, keys), 0.0)
            dkv[j, :, cols] = grad_keys.astype(bf16)
            dkv[j, :, value_cols] = grad_values.astype(bf16)
            dq_sum[:, cols] += grad_queries

        @pl.when(step == 0)
        def _():
            for copy in first:
                copy.start()

        @pl.when(step == 1)
        def _():
            for p in range(parts):
                first[p].wait_recv()
                cuts = pl.ds(p * rows, rows)
                outgo[cuts] = (
                    dkv[far, cuts].astype(f32) + from_twin[0, cuts].astype(f32)
                ).astype(bf16)
                third[p].start()

        @pl.when(step == 2)
        def _():
            second.start()

    grad_project[:, :width] = (dq_sum[...] * score_scale).astype(bf16)
    dense_ref[:, 4 * width :] = router_ref[...]
    dense_ref[:, 3 * width : 4 * width] = matmul_left_t(
        mixed_ref[...].astype(bf16), grad_branch_ref[...]
    ).astype(bf16)
    dense_ref[:, :width] = matmul_left_t(hidden_ref[...], grad_project[:, :width]).astype(bf16)
    second.wait_recv()
    for p in range(parts):
        cuts = pl.ds(p * rows, rows)
        third[p].wait_recv()
        grad_project[cuts, width:] = (
            dkv[seq, cuts].astype(f32)
            + from_twin[1, cuts].astype(f32)
            + from_far[cuts].astype(f32)
        ).astype(bf16)
    dense_ref[:, width : 3 * width] = matmul_left_t(
        hidden_ref[...], grad_project[:, width:]
    ).astype(bf16)
    grads = matmul_right_t(grad_project[...], qkv_ref[...])
    normed, root = norm_rows(patches_ref[...].astype(f32))
    patch_grad_ref[...] = grad_after_ref[...] + norm_back(
        grads * (1.0 + row_ref[:, width : 2 * width]), normed, root
    )
    sums_ref[...] = jnp.zeros_like(sums_ref)
    sums_ref[0:1, :] = jnp.sum(grads, axis=0, keepdims=True)
    sums_ref[1:2, :] = jnp.sum(grads * normed, axis=0, keepdims=True)
    second.wait_send()
    for p in range(parts):
        first[p].wait_send()
        third[p].wait_send()


def last_block(bias, q, kv, grad_mixed, mixed, stats, hidden, grad_branch, grad_after, patches, row, qkv_full, router_part, number, parts=4):
    tok_rows, width = q.shape
    sources = kv.shape[0] // tok_rows
    f32, bf16 = jnp.float32, jnp.bfloat16
    inside = pl.BlockSpec(memory_space=pltpu.VMEM)
    dma = pltpu.SemaphoreType.DMA
    return pl.pallas_call(
        functools.partial(last_kernel, parts),
        out_shape=(
            jax.ShapeDtypeStruct((width, 4 * width + 128), bf16),
            jax.ShapeDtypeStruct((tok_rows, width), f32),
            jax.ShapeDtypeStruct((8, width), f32),
        ),
        in_specs=[pl.BlockSpec(memory_space=pltpu.SMEM)] + [inside] * 12,
        out_specs=(inside,) * 3,
        scratch_shapes=[
            pltpu.VMEM((128, tok_rows), f32),
            pltpu.VMEM((tok_rows, width), f32),
            pltpu.VMEM((sources, tok_rows, 2 * width), bf16),
            pltpu.VMEM((2, tok_rows, 2 * width), bf16),
            pltpu.VMEM((tok_rows, 2 * width), bf16),
            pltpu.VMEM((tok_rows, 2 * width), bf16),
            pltpu.VMEM((tok_rows, 3 * width), bf16),
            dma((2 * parts + 1,)),
            dma((2 * parts + 1,)),
        ],
        compiler_params=pltpu.CompilerParams(
            collective_id=number, has_side_effects=True, vmem_limit_bytes=34 * 2**20
        ),
        cost_estimate=pl.CostEstimate(
            flops=30_000_000_000, bytes_accessed=20_000_000, transcendentals=4_000_000
        ),
    )(bias, q, kv, grad_mixed, mixed, stats, hidden, grad_branch, grad_after, patches, row, qkv_full, router_part)


def finish_kernel(
    rows_ref,
    shares_ref,
    ada_ref,
    expert_in_grad_ref,
    ada_grad_ref,
    bias_ref,
    cond_ref,
    shares_in,
    modul,
    cond,
    cond_part,
    share_send,
    share_recv,
    cond_send,
    cond_recv,
    own_sem,
):
    f32, bf16 = jnp.float32, jnp.bfloat16
    bucket, dp, seq, far, twin = own_place()
    devices, _, width = rows_ref.shape
    shards, local_experts, _, units = shares_ref.shape
    images = cond_part.shape[1]
    others = [
        (q, lax.rem(bucket + q // 4, 2), lax.rem(dp + q % 4, 4)) for q in range(1, shards)
    ]
    greet([{"bucket": b, "dp": d} for _, b, d in others])
    own = bucket * 4 + dp
    sends = [
        hand_over(
            shares_ref.at[b * 4 + d],
            shares_in.at[own],
            (share_send, share_recv),
            q - 1,
            {"bucket": b, "dp": d},
        )
        for q, b, d in others
    ]
    for copy in sends:
        copy.start()
    keep = pltpu.make_async_copy(shares_ref.at[own], shares_in.at[own], own_sem)
    keep.start()

    device = lax.broadcasted_iota(jnp.int32, (devices, 128), 0)
    image = lax.broadcasted_iota(jnp.int32, (devices, 128), 1)
    group = ((device // 4) % 2) * 4 + device // 8
    slot = rows_ref[:, 7, :][:, :128].astype(jnp.int32)
    member = (image == group * images + slot).astype(f32)
    total = shards * images
    for p in range(6):
        modul[:, p * width : (p + 1) * width] = lax.dot_general(
            member,
            rows_ref[:, p, :],
            (((0,), (0,)), ((), ())),
            precision=highest,
            preferred_element_type=f32,
        )[:total]
    bias_ref[...] = jnp.sum(modul[...], axis=0, keepdims=True)
    for d in range(4):
        for b in range(2):
            at = (b * 4 + d) * images
            cond[at : at + images, :] = rows_ref[d * 8 + b * 4 : d * 8 + b * 4 + images, 6, :]
    bucket_rows = modul[pl.ds(pl.multiple_of(bucket * (4 * images), 8), 4 * images), :]
    high = bucket_rows.astype(bf16)
    rest = bucket_rows - high.astype(f32)
    middle_part = rest.astype(bf16)
    low_part = (rest - middle_part.astype(f32)).astype(bf16)
    cond_rows = (
        matmul_right_t(high, ada_ref[...])
        + matmul_right_t(middle_part, ada_ref[...])
        + matmul_right_t(low_part, ada_ref[...])
    )
    for k in range(4):
        cond_part[k] = cond_rows[k * images : (k + 1) * images]
    conds = [
        hand_over(
            cond_part.at[lax.rem(dp + k, 4)],
            cond_ref.at[dp],
            (cond_send, cond_recv),
            k - 1,
            {"dp": lax.rem(dp + k, 4)},
        )
        for k in (1, 2, 3)
    ]
    for copy in conds:
        copy.start()
    cond_ref[dp] = cond_part[dp]
    rows = ada_grad_ref.shape[0]
    first = (own * 4 + seq) * rows
    chosen = (
        lax.broadcasted_iota(jnp.int32, (rows, width), 1)
        == lax.broadcasted_iota(jnp.int32, (rows, width), 0) + first
    ).astype(f32)
    cond_cols = matmul_right_t(chosen.astype(bf16), cond[...].astype(bf16))
    ada_grad_ref[...] = jnp.dot(
        cond_cols, modul[...], precision=highest, preferred_element_type=f32
    )
    keep.wait()
    for copy in sends:
        copy.wait_recv()
    for s in range(shards):
        for e in range(local_experts):
            expert_in_grad_ref[e, :, s * units : (s + 1) * units] = shares_in[s, e].astype(f32)
    for copy in conds:
        copy.wait()
    for copy in sends:
        copy.wait_send()


def finish(rows, shares, ada_weight, images, number):
    devices, _, width = rows.shape
    shards, local_experts, share_rows, units = shares.shape
    f32 = jnp.float32
    inside = pl.BlockSpec(memory_space=pltpu.VMEM)
    dma = pltpu.SemaphoreType.DMA
    shape = jax.ShapeDtypeStruct
    columns = ada_weight.shape[0]
    return pl.pallas_call(
        finish_kernel,
        out_shape=(
            shape((local_experts, share_rows, shards * units), f32),
            shape((width // devices, 6 * width), f32),
            shape((1, 6 * width), f32),
            shape((4, images, columns), f32),
        ),
        in_specs=[inside] * 3,
        out_specs=(inside,) * 4,
        scratch_shapes=[
            pltpu.VMEM(shares.shape, shares.dtype),
            pltpu.VMEM((shards * images, 6 * width), f32),
            pltpu.VMEM((shards * images, width), f32),
            pltpu.VMEM((4, images, columns), f32),
            dma((shards - 1,)),
            dma((shards - 1,)),
            dma((3,)),
            dma((3,)),
            dma,
        ],
        compiler_params=pltpu.CompilerParams(
            collective_id=number, has_side_effects=True, vmem_limit_bytes=24 * 2**20
        ),
        cost_estimate=pl.CostEstimate(
            flops=20_000_000_000, bytes_accessed=20_000_000, transcendentals=0
        ),
    )(rows, shares, ada_weight)


def body_general(
    patches,
    conditioning,
    image_slot,
    routes,
    ada_weight,
    ada_bias,
    qkv_weight,
    out_weight,
    router_weight,
    shared_in,
    shared_out,
    expert_in,
    expert_out,
    out_grad,
):
    seq_count = lax.axis_size("seq")
    seq_place = lax.axis_index("seq")
    outer_count = lax.axis_size(("bucket", "dp"))
    tok_rows = patches.shape[0]
    width = patches.shape[1]
    images = conditioning.shape[0]
    local_experts = expert_in.shape[0]
    all_experts = local_experts * seq_count
    capacity = 3 * tok_rows // all_experts
    head_dim = width // HEADS
    score_scale = 1.0 / math.sqrt(head_dim)
    dense = (
        lax.all_gather(ada_weight, "dp", axis=0, tiled=True),
        lax.all_gather(ada_bias, "dp", axis=0, tiled=True),
        lax.all_gather(qkv_weight, "dp", axis=0, tiled=True),
        lax.all_gather(out_weight, "dp", axis=0, tiled=True),
        lax.all_gather(router_weight, "dp", axis=0, tiled=True),
        lax.all_gather(shared_in, "dp", axis=0, tiled=True),
        lax.all_gather(shared_out, "dp", axis=0, tiled=True),
    )
    ada_full, bias_full, qkv_full, proj_full, router_full, inner_full, outer_full = dense
    cond_float = conditioning.astype(jnp.float32)
    cond_act = silu_curve(cond_float).astype(jnp.bfloat16)
    modul = matmul_low(cond_act, ada_full) + bias_full.astype(jnp.float32)
    own_slots = lax.dynamic_slice_in_dim(image_slot, seq_place * tok_rows, tok_rows)
    image_ids = jnp.arange(images, dtype=jnp.int32)
    onehot = (own_slots[:, None] == image_ids[None, :]).astype(jnp.float32)
    per_row = jnp.dot(onehot, modul, precision=highest)
    shift_one, scale_one, gate_one, shift_two, scale_two, gate_two = jnp.split(per_row, 6, axis=1)
    rows_float = patches.astype(jnp.float32)
    hidden_one_f, norm_one_pull = jax.vjp(modulate, rows_float, scale_one, shift_one)
    hidden_one = hidden_one_f.astype(jnp.bfloat16)
    project = matmul_low(hidden_one, qkv_full).astype(jnp.bfloat16)
    queries_heads = project[:, :width].reshape(tok_rows, HEADS, head_dim)
    key_value = project[:, width:]
    kv_all = lax.all_gather(key_value, "seq", axis=0, tiled=True)
    group_rows = kv_all.shape[0]
    keys_all = kv_all[:, :width].reshape(group_rows, HEADS, head_dim)
    values_all = kv_all[:, width:].reshape(group_rows, HEADS, head_dim)
    scores = (
        jnp.einsum("qhd,khd->hqk", queries_heads, keys_all, preferred_element_type=jnp.float32)
        * score_scale
    )
    same_image = own_slots[:, None] == image_slot[None, :]
    scores = jnp.where(same_image[None, :, :], scores, -1e30)
    row_max = jnp.max(scores, axis=-1, keepdims=True)
    exp_scores = jnp.exp(scores - row_max)
    probs = exp_scores / jnp.sum(exp_scores, axis=-1, keepdims=True)
    probs_low = probs.astype(jnp.bfloat16)
    mixed = (
        jnp.einsum("hqk,khd->qhd", probs_low, values_all, preferred_element_type=jnp.float32)
        .reshape(tok_rows, width)
        .astype(jnp.bfloat16)
    )
    branch = matmul_low(mixed, proj_full)
    after = rows_float + gate_one * branch
    hidden_two_f, norm_two_pull = jax.vjp(modulate, after, scale_two, shift_two)
    hidden_two = hidden_two_f.astype(jnp.bfloat16)
    shared_inner = matmul_low(hidden_two, inner_full)
    shared_act = gelu_curve(shared_inner).astype(jnp.bfloat16)
    shared_val = matmul_low(shared_act, outer_full)
    logits = matmul_low(hidden_two, router_full)
    expert_ids = jnp.arange(all_experts, dtype=jnp.int32)
    pick_zero = (routes[:, 0:1] == expert_ids[None, :]).astype(jnp.float32)
    pick_one = (routes[:, 1:2] == expert_ids[None, :]).astype(jnp.float32)
    pair = jnp.stack(
        [jnp.sum(logits * pick_zero, axis=1), jnp.sum(logits * pick_one, axis=1)], axis=1
    )
    pair_max = jnp.max(pair, axis=1, keepdims=True)
    pair_exp = jnp.exp(pair - pair_max)
    gates = pair_exp / jnp.sum(pair_exp, axis=1, keepdims=True)
    flat_routes = routes.reshape(-1)
    pair_hits = (flat_routes[:, None] == expert_ids[None, :]).astype(jnp.int32)
    running = jnp.cumsum(pair_hits, axis=0)
    place = jnp.sum(running * pair_hits, axis=1) - 1
    slot_of = flat_routes * capacity + place
    slot_ids = jnp.arange(all_experts * capacity, dtype=jnp.int32)
    spread = (slot_ids[:, None] == slot_of[None, :]).astype(jnp.bfloat16)
    spread_pairs = spread.reshape(all_experts * capacity, tok_rows, 2)
    dispatch_mat = spread_pairs[:, :, 0] + spread_pairs[:, :, 1]
    send = (
        matmul_low(dispatch_mat, hidden_two)
        .astype(jnp.bfloat16)
        .reshape(seq_count, local_experts, capacity, width)
    )
    inner = jnp.einsum(
        "secd,edf->secf",
        lax.all_to_all(send, "seq", split_axis=0, concat_axis=0, tiled=True),
        expert_in,
        preferred_element_type=jnp.float32,
    )
    active = gelu_curve(inner).astype(jnp.bfloat16)
    result = jnp.einsum(
        "secf,efd->secd", active, expert_out, preferred_element_type=jnp.float32
    ).astype(jnp.bfloat16)
    returned = lax.all_to_all(result, "seq", split_axis=0, concat_axis=0, tiled=True)
    slot_values = returned.reshape(all_experts * capacity, width)
    picked_zero = matmul_left_t(spread_pairs[:, :, 0], slot_values)
    picked_one = matmul_left_t(spread_pairs[:, :, 1], slot_values)
    mixture = shared_val + gates[:, 0:1] * picked_zero + gates[:, 1:2] * picked_one
    block_out = (after + gate_two * mixture).astype(jnp.bfloat16)
    grad_block = out_grad.astype(jnp.float32)
    grad_gate_two = grad_block * mixture
    grad_mix = grad_block * gate_two
    back_dense = (
        lax.all_gather(ada_weight, "dp", axis=0, tiled=True),
        lax.all_gather(qkv_weight, "dp", axis=0, tiled=True),
        lax.all_gather(out_weight, "dp", axis=0, tiled=True),
        lax.all_gather(router_weight, "dp", axis=0, tiled=True),
        lax.all_gather(shared_in, "dp", axis=0, tiled=True),
        lax.all_gather(shared_out, "dp", axis=0, tiled=True),
    )
    ada_back, qkv_back, proj_back, router_back, inner_back, outer_back = back_dense
    grad_shared = grad_mix.astype(jnp.bfloat16)
    grad_shared_act = matmul_right_t(grad_shared, outer_back)
    grad_shared_inner = (grad_shared_act * gelu_slope(shared_inner)).astype(jnp.bfloat16)
    grad_outer_w = matmul_left_t(shared_act, grad_shared)
    grad_inner_w = matmul_left_t(hidden_two, grad_shared_inner)
    grad_hidden = matmul_right_t(grad_shared_inner, inner_back)
    grad_gates = jnp.stack(
        [jnp.sum(grad_mix * picked_zero, axis=1), jnp.sum(grad_mix * picked_one, axis=1)], axis=1
    )
    grad_pair = gates * (grad_gates - jnp.sum(gates * grad_gates, axis=1, keepdims=True))
    grad_logits = (grad_pair[:, 0:1] * pick_zero + grad_pair[:, 1:2] * pick_one).astype(
        jnp.bfloat16
    )
    grad_router_w = matmul_left_t(hidden_two, grad_logits)
    grad_hidden = grad_hidden + matmul_right_t(grad_logits, router_back)
    grad_pairs = (
        jnp.stack([gates[:, 0:1] * grad_mix, gates[:, 1:2] * grad_mix], axis=1)
        .reshape(2 * tok_rows, width)
        .astype(jnp.bfloat16)
    )
    grad_send = (
        matmul_low(spread, grad_pairs)
        .astype(jnp.bfloat16)
        .reshape(seq_count, local_experts, capacity, width)
    )
    inputs_in = lax.all_to_all(send, "seq", split_axis=0, concat_axis=0, tiled=True)
    grads_in = lax.all_to_all(grad_send, "seq", split_axis=0, concat_axis=0, tiled=True)
    inner = jnp.einsum("secd,edf->secf", inputs_in, expert_in, preferred_element_type=jnp.float32)
    active = gelu_curve(inner).astype(jnp.bfloat16)
    grad_act = jnp.einsum(
        "secd,efd->secf", grads_in, expert_out, preferred_element_type=jnp.float32
    )
    grad_inner = (grad_act * gelu_slope(inner)).astype(jnp.bfloat16)
    grad_rows = jnp.einsum(
        "secf,edf->secd", grad_inner, expert_in, preferred_element_type=jnp.float32
    ).astype(jnp.bfloat16)
    sent_back = lax.all_to_all(grad_rows, "seq", split_axis=0, concat_axis=0, tiled=True)
    grad_expert_in = jnp.einsum(
        "secd,secf->edf", inputs_in, grad_inner, preferred_element_type=jnp.float32
    )
    grad_expert_out = jnp.einsum(
        "secf,secd->efd", active, grads_in, preferred_element_type=jnp.float32
    )
    grad_hidden = grad_hidden + matmul_left_t(
        dispatch_mat, sent_back.reshape(all_experts * capacity, width)
    )
    grad_after_norm, grad_scale_two, grad_shift_two = norm_two_pull(grad_hidden)
    grad_after = grad_block + grad_after_norm
    grad_gate_one = grad_after * branch
    grad_branch = (grad_after * gate_one).astype(jnp.bfloat16)
    grad_proj_w = matmul_left_t(mixed, grad_branch)
    grad_mixed = matmul_right_t(grad_branch, proj_back).astype(jnp.bfloat16)
    grad_mixed_heads = grad_mixed.reshape(tok_rows, HEADS, head_dim)
    grad_probs = jnp.einsum(
        "qhd,khd->hqk", grad_mixed_heads, values_all, preferred_element_type=jnp.float32
    )
    row_dot = jnp.sum(probs * grad_probs, axis=-1, keepdims=True)
    grad_scores = (probs * (grad_probs - row_dot)).astype(jnp.bfloat16)
    grad_queries = (
        jnp.einsum("hqk,khd->qhd", grad_scores, keys_all, preferred_element_type=jnp.float32)
        * score_scale
    )
    grad_keys = (
        jnp.einsum("hqk,qhd->khd", grad_scores, queries_heads, preferred_element_type=jnp.float32)
        * score_scale
    )
    grad_values = jnp.einsum(
        "hqk,qhd->khd", probs_low, grad_mixed_heads, preferred_element_type=jnp.float32
    )
    grad_kv = lax.psum_scatter(
        jnp.concatenate(
            [
                grad_keys.reshape(lax.axis_size("seq") * tok_rows, width),
                grad_values.reshape(lax.axis_size("seq") * tok_rows, width),
            ],
            axis=1,
        ).astype(jnp.bfloat16),
        "seq",
        scatter_dimension=0,
        tiled=True,
    ).astype(jnp.float32)
    grad_project = jnp.concatenate([grad_queries.reshape(tok_rows, width), grad_kv], axis=1).astype(
        jnp.bfloat16
    )
    grad_qkv_w = matmul_left_t(hidden_one, grad_project)
    grad_hidden_one = matmul_right_t(grad_project, qkv_back)
    grad_rows, grad_scale_one, grad_shift_one = norm_one_pull(grad_hidden_one)
    patch_grad = grad_after + grad_rows
    grad_per_row = jnp.concatenate(
        [
            grad_shift_one,
            grad_scale_one,
            grad_gate_one,
            grad_shift_two,
            grad_scale_two,
            grad_gate_two,
        ],
        axis=1,
    )
    grad_modul = lax.dot_general(onehot, grad_per_row, (((0,), (0,)), ((), ())), precision=highest)
    grad_ada_w = lax.dot_general(
        cond_act.astype(jnp.float32), grad_modul, (((0,), (0,)), ((), ())), precision=highest
    )
    grad_ada_b = jnp.sum(grad_modul, axis=0)
    grad_cond_part = lax.dot_general(
        grad_modul,
        ada_back,
        (((1,), (1,)), ((), ())),
        precision=highest,
        preferred_element_type=jnp.float32,
    ) * silu_slope(cond_float)
    dense_terms = (
        grad_ada_w,
        grad_ada_b,
        grad_qkv_w,
        grad_proj_w,
        grad_router_w,
        grad_inner_w,
        grad_outer_w,
    )
    ordered = tuple((order_rows(term, outer_count, seq_count) for term in dense_terms))
    first_sums = (
        lax.psum_scatter(
            grad_cond_part.astype(jnp.bfloat16), "seq", scatter_dimension=1, tiled=True
        ).astype(jnp.float32),
        lax.psum_scatter(
            ordered[0].astype(jnp.bfloat16), "seq", scatter_dimension=0, tiled=True
        ).astype(jnp.float32),
        lax.psum_scatter(
            ordered[1].astype(jnp.bfloat16), "seq", scatter_dimension=0, tiled=True
        ).astype(jnp.float32),
        lax.psum_scatter(
            ordered[2].astype(jnp.bfloat16), "seq", scatter_dimension=0, tiled=True
        ).astype(jnp.float32),
        lax.psum_scatter(
            ordered[3].astype(jnp.bfloat16), "seq", scatter_dimension=0, tiled=True
        ).astype(jnp.float32),
        lax.psum_scatter(
            ordered[4].astype(jnp.bfloat16), "seq", scatter_dimension=0, tiled=True
        ).astype(jnp.float32),
        lax.psum_scatter(
            ordered[5].astype(jnp.bfloat16), "seq", scatter_dimension=0, tiled=True
        ).astype(jnp.float32),
        lax.psum_scatter(
            ordered[6].astype(jnp.bfloat16), "seq", scatter_dimension=0, tiled=True
        ).astype(jnp.float32),
    )
    cond_grad = first_sums[0]
    second_sums = (
        lax.psum_scatter(first_sums[1], ("bucket", "dp"), scatter_dimension=0, tiled=True),
        lax.psum_scatter(first_sums[2], ("bucket", "dp"), scatter_dimension=0, tiled=True),
        lax.psum_scatter(first_sums[3], ("bucket", "dp"), scatter_dimension=0, tiled=True),
        lax.psum_scatter(first_sums[4], ("bucket", "dp"), scatter_dimension=0, tiled=True),
        lax.psum_scatter(first_sums[5], ("bucket", "dp"), scatter_dimension=0, tiled=True),
        lax.psum_scatter(first_sums[6], ("bucket", "dp"), scatter_dimension=0, tiled=True),
        lax.psum_scatter(first_sums[7], ("bucket", "dp"), scatter_dimension=0, tiled=True),
        lax.psum_scatter(grad_expert_in, ("bucket", "dp"), scatter_dimension=1, tiled=True),
        lax.psum_scatter(grad_expert_out, ("bucket", "dp"), scatter_dimension=1, tiled=True),
    )
    dense_out = second_sums[:7]
    expert_sums = second_sums[7:]
    return (
        block_out,
        patch_grad,
        cond_grad,
        dense_out[0],
        dense_out[1],
        dense_out[2],
        dense_out[3],
        dense_out[4],
        dense_out[5],
        dense_out[6],
        expert_sums[0],
        expert_sums[1],
    )


def norm_parts(rows_in):
    centred = rows_in - jnp.mean(rows_in, axis=-1, keepdims=True)
    scale = lax.rsqrt(jnp.mean(centred * centred, axis=-1, keepdims=True) + norm_eps)
    return centred * scale, scale


def norm_back(grad_normed, normed, scale):
    mean_grad = jnp.mean(grad_normed, axis=-1, keepdims=True)
    mean_prod = jnp.mean(grad_normed * normed, axis=-1, keepdims=True)
    return scale * (grad_normed - mean_grad - normed * mean_prod)


def two_parts(value):
    high = value.astype(jnp.bfloat16)
    return high, (value - high.astype(jnp.float32)).astype(jnp.bfloat16)


def body_tokens(
    patches,
    conditioning,
    image_slot,
    routes,
    ada_weight,
    ada_bias,
    qkv_weight,
    out_weight,
    router_weight,
    shared_in,
    shared_out,
    expert_in,
    expert_out,
    out_grad,
):
    bf16, f32 = jnp.bfloat16, jnp.float32
    every = ("bucket", "dp", "seq")
    outer = ("bucket", "dp")
    spare = ("bucket", "seq")
    seq_count = lax.axis_size("seq")
    dp_count = lax.axis_size("dp")
    outer_count = lax.axis_size(outer)
    spare_count = lax.axis_size(spare)
    devices = outer_count * seq_count
    seq_place = lax.axis_index("seq")
    dp_place = lax.axis_index("dp")
    outer_place = lax.axis_index(outer)
    place_all = lax.axis_index(every)
    spare_place = lax.axis_index(spare)
    tok_rows, width = patches.shape
    images = conditioning.shape[0]
    hidden = shared_in.shape[1]
    local_experts = expert_in.shape[0]
    all_experts = local_experts * seq_count
    capacity = 3 * tok_rows // all_experts
    head_dim = width // HEADS
    score_scale = 1.0 / math.sqrt(head_dim)

    def piece(weight):
        rows = weight.shape[0] // spare_count
        return lax.dynamic_slice_in_dim(weight, spare_place * rows, rows)

    turned = ("dp", "bucket", "seq")
    side = hidden // spare_count
    unit_rows = shared_out.shape[0] // spare_count
    out_piece = piece(shared_out)
    load = jnp.concatenate(
        [
            lax.dynamic_slice_in_dim(shared_in, spare_place * side, side, axis=1),
            out_piece[:, :side],
            out_piece[:, side:],
        ],
        axis=0,
    )
    shared_all = lax.all_gather(load, turned, axis=0, tiled=True).reshape(
        dp_count, spare_count, -1, side
    )
    grads_all = lax.all_gather(out_grad, turned, axis=0, tiled=True).reshape(
        dp_count, spare_count, tok_rows, width
    )

    cond_float = conditioning.astype(f32)
    cond_act = silu_curve(cond_float).astype(bf16)
    cond_cols = jnp.swapaxes(cond_act.astype(f32).reshape(images, dp_count, -1), 0, 1)
    small = jnp.concatenate(
        [out_weight, jnp.pad(router_weight, ((0, 0), (0, 128 - all_experts)))], axis=1
    )
    modul, patches_group, qkv_full, small_full = opening(
        cond_cols,
        ada_weight,
        ada_bias.astype(f32)[None, :],
        patches,
        qkv_weight,
        small,
        1,
    )
    proj_full = small_full[:, :width]
    router_full = small_full[:, width : width + all_experts]
    slots_group = image_slot.reshape(seq_count, tok_rows)[:, 0]
    slot = lax.dynamic_slice_in_dim(slots_group, seq_place, 1)[0]
    row = lax.dynamic_slice_in_dim(modul, slot, 1)
    image_ids_own = jnp.arange(images, dtype=jnp.int32)
    rows_group = jnp.sum(
        jnp.where(
            (slots_group[:, None] == image_ids_own[None, :])[:, :, None], modul[None], 0.0
        ),
        axis=1,
    )
    shift_one, scale_one, gate_one, shift_two, scale_two, gate_two = jnp.split(row, 6, axis=1)

    hidden_seen = jnp.where(slots_group == slot, 0.0, -1e30)
    hidden_one, queries, kv_all, mixed, stats, branch, after, gates, extras, grads_group = forward_block(
        hidden_seen, patches_group, rows_group, qkv_full, small_full, routes, out_grad, all_experts, 6
    )
    back, shared_val, grad_hidden = middle(
        extras,
        grads_group,
        rows_group[:, 5 * width :],
        expert_in,
        expert_out,
        shared_all,
        capacity,
        all_experts,
        2,
    )
    block_out, grad_after, grad_branch, grad_mixed, sums_two, router_part = home(
        extras,
        gates,
        back,
        shared_val,
        grad_hidden,
        out_grad,
        after,
        branch,
        row,
        small_full,
        all_experts,
    )
    dense_part, patch_grad, sums_one = last_block(
        hidden_seen,
        queries,
        kv_all,
        grad_mixed,
        mixed,
        stats,
        hidden_one,
        grad_branch,
        grad_after,
        patches,
        row,
        qkv_full,
        router_part,
        3,
    )

    own_cols = width // devices
    dense_sum = lax.psum_scatter(dense_part, every, scatter_dimension=0, tiled=True).astype(f32)
    qkv_out = dense_sum[:, : 3 * width]
    proj_out = dense_sum[:, 3 * width : 4 * width]
    router_out = dense_sum[:, 4 * width : 4 * width + all_experts]

    row_block = jnp.concatenate(
        [
            sums_one[:2],
            sums_two[:4],
            lax.dynamic_slice_in_dim(cond_act, seq_place, 1).astype(f32),
            jnp.full((1, width), 1.0, f32) * slot.astype(f32),
        ],
        axis=0,
    )
    own_shared = hidden // devices
    first_unit = place_all * own_shared
    in_rank = shared_in.shape[0]
    shared_in_own = lax.dynamic_slice(
        shared_all, (0, first_unit // side, 0, first_unit % side), (dp_count, 1, in_rank, own_shared)
    ).reshape(width, own_shared)
    shared_out_own = lax.dynamic_slice(
        shared_all.reshape(devices, -1, side),
        (first_unit // unit_rows, in_rank, 0),
        (1, 2 * unit_rows, side),
    )
    shared_out_own = jnp.concatenate(
        [shared_out_own[0, :unit_rows], shared_out_own[0, unit_rows:]], axis=1
    )
    in_shares, expert_out_grad, shared_in_turned, shared_out_grad, row_all = unit_gradients(
        extras,
        row_block,
        grads_all,
        expert_in,
        expert_out,
        jnp.pad(shared_in_own, ((0, 0), (0, 128 - own_shared))),
        jnp.pad(shared_out_own, ((0, 128 - own_shared), (0, 0))),
        capacity,
        all_experts,
        outer_count,
        4,
    )
    expert_in_grad, ada_out, bias_sum, cond_back = finish(
        row_all.reshape(devices, -1, width), in_shares, ada_weight, images, 5
    )
    bias_cols = 6 * width // devices
    bias_out = lax.dynamic_slice_in_dim(bias_sum[0], place_all * bias_cols, bias_cols)
    cond_cols_own = width // seq_count
    cond_out = lax.dynamic_slice_in_dim(cond_back, seq_place, 1)[0] * silu_slope(
        lax.dynamic_slice_in_dim(cond_float, seq_place * cond_cols_own, cond_cols_own, axis=1)
    )

    shared_out_grad = shared_out_grad[:own_shared]
    shared_shares = lax.all_to_all(
        shared_in_turned, every, split_axis=0, concat_axis=0, tiled=True
    )[:, :, :own_shared]
    shared_in_grad = jnp.transpose(shared_shares, (1, 0, 2)).reshape(own_cols, hidden)
    return (
        block_out,
        patch_grad,
        cond_out,
        ada_out,
        bias_out,
        qkv_out,
        proj_out,
        router_out,
        shared_in_grad,
        shared_out_grad,
        expert_in_grad,
        expert_out_grad,
    )


def solution(mesh):
    in_specs = (
        P(("bucket", "dp", "seq"), None),
        P(("bucket", "dp"), None),
        P(("bucket", "dp")),
        P(("bucket", "dp", "seq"), None),
        P("dp", None),
        P("dp"),
        P("dp", None),
        P("dp", None),
        P("dp", None),
        P("dp", None),
        P("dp", None),
        P("seq", None, None),
        P("seq", None, None),
        P(("bucket", "dp", "seq"), None),
    )
    out_specs = (
        P(("bucket", "dp", "seq"), None),
        P(("bucket", "dp", "seq"), None),
        P(("bucket", "dp"), "seq"),
        P(("bucket", "dp", "seq"), None),
        P(("bucket", "dp", "seq")),
        P(("bucket", "dp", "seq"), None),
        P(("bucket", "dp", "seq"), None),
        P(("bucket", "dp", "seq"), None),
        P(("bucket", "dp", "seq"), None),
        P(("bucket", "dp", "seq"), None),
        P("seq", ("bucket", "dp"), None),
        P("seq", ("bucket", "dp"), None),
    )
    shape = tuple(mesh.shape[name] for name in ("bucket", "dp", "seq"))
    body = body_tokens if shape == (2, 4, 4) else body_general
    return jax.shard_map(body, mesh=mesh, in_specs=in_specs, out_specs=out_specs, check_vma=False)
```
